256 devices in a mesh: seq: 16 (over z_lo, y), head: 16 (over x, z_hi, core).
Axes of the slice: x: 4, y: 4, z: 8 (z_hi: 2, z_lo: 4; z = z_hi * 4 + z_lo), core: 2. Of those that a mesh axis runs over, the one named last changes fastest.
Arguments:
- query: bfloat16 [16384, 2048], P(('seq', 'head')), may hold values from -6 to 6
- key: bfloat16 [16384, 2048], P(('seq', 'head')), may hold values from -6 to 6
- value: bfloat16 [16384, 2048], P(('seq', 'head')), may hold values from -6 to 6
- output: bfloat16 [16384, 2048], P(('seq', 'head')), may hold values from -6 to 6
- grad_out: bfloat16 [16384, 2048], P(('seq', 'head')), may hold values from -6 to 6
- logsumexp: float32 [16, 16384], P('head', 'seq'), may hold values from 3.5 to 8.5, as said below
- rand_blocks: int32 [256, 3], replicated, may hold values from 0 to 255, as said below
Outputs:
- grad_query: bfloat16 [16384, 2048], P(('seq', 'head'))
- grad_key: bfloat16 [16384, 2048], P(('seq', 'head'))
- grad_value: bfloat16 [16384, 2048], P(('seq', 'head'))
The draws below stay inside these ranges and needn't reach their ends.
Inputs may be any that keep to these rules, and one draw needn't show every extreme that they name: `rand_blocks`: each row names 3 different blocks, none below 2 and none within one block of the row's own block. In aligned runs of 16 rows, exactly 3 of the run's entries fall in each aligned run of 16 key blocks. `logsumexp`: rows of the first 2 blocks lie between 7 and 8.5, all others between 3.5 and 5.
All inputs are finite; a program needn't handle non-finite values.
Results may differ from the reference program's by a relative error of at most 0.02.
Values may be sent and summed in bfloat16 or wider, within the bound.
No kernel may reach another device: no remote copies, remote signals or barrier semaphores. Data moves between devices by JAX's collectives and lax.ppermute only.
A program may use at most 64 MiB of HBM per device.

```python
import math
import jax
import jax.numpy as jnp
from jax import lax

HEADS = 16
HD = 128
BLK = 64
GLOB = 2
RAND = 3
QB_DEV = 16
NQB = 256
LENGTH = 16384
FEAT = 2048


def draw_logsumexp(key, part):
    positions = jnp.arange(LENGTH)
    glob_mask = positions < GLOB * BLK
    baseline = jnp.where(glob_mask, 7.0, 3.5).astype(jnp.float32)
    jitter = jax.random.uniform(key, (HEADS, LENGTH), jnp.float32)
    return (baseline[None, :] + 1.5 * jitter).astype(jnp.float32)


def draw_rand_blocks(key, part):
    groups_count = NQB // QB_DEV
    per_group = RAND * QB_DEV // groups_count
    labels = jnp.repeat(jnp.arange(groups_count, dtype=jnp.int32), per_group)
    group_keys = jax.random.split(jax.random.fold_in(key, 1), groups_count)
    shuffled = jax.vmap(lambda subkey: jax.random.permutation(subkey, labels))(group_keys)
    targets = shuffled.reshape(NQB, RAND).astype(jnp.int32)
    scores = jax.random.randint(jax.random.fold_in(key, 2), (NQB, RAND, QB_DEV), 0, 1 << 20, dtype=jnp.int32)
    scores = scores * QB_DEV + jnp.arange(QB_DEV, dtype=jnp.int32)[None, None, :]
    own_block = jnp.arange(NQB, dtype=jnp.int32)[:, None]
    chosen = []
    for slot_index in range(RAND):
        candidate = targets[:, slot_index][:, None] * QB_DEV + jnp.arange(QB_DEV, dtype=jnp.int32)[None, :]
        banned = (candidate < GLOB) | (jnp.abs(candidate - own_block) <= 1)
        for earlier in chosen:
            banned = banned | (candidate == earlier[:, None])
        masked = jnp.where(banned, -1, scores[:, slot_index])
        best_pick = lax.top_k(masked, 1)[1][:, 0].astype(jnp.int32)
        chosen.append(targets[:, slot_index] * QB_DEV + best_pick)
    return jnp.stack(chosen, axis=1).astype(jnp.int32)


def shard_levels(stream_key, shape, shards, least, top_value):
    gain, own = 1.0, jax.random.fold_in(stream_key, 6)
    for dim, blocks in shards:
        steps = jnp.exp(jax.random.uniform(jax.random.fold_in(own, dim), (blocks,), jnp.float32, least / len(shards), top_value / len(shards)))
        gain = gain * jnp.repeat(steps, shape[dim] // blocks).reshape([-1 if axis == dim else 1 for axis in range(len(shape))])
    return gain


def normal_values(rng, dims, spread, limit, cuts=(), kind=jnp.bfloat16):
    entries = spread * jax.random.normal(rng, dims, jnp.float32)
    if cuts:
        entries = entries * shard_levels(rng, dims, cuts, -0.22, 0.18)
    return jnp.clip(entries, -limit, limit).astype(kind)


def setup_inputs(seed: int = 0) -> dict:
    streams_of = jax.random.split(jax.random.key(seed), 8)
    query = normal_values(streams_of[0], (LENGTH, FEAT), 1.0, 6.0, ((0, 256),))
    key = normal_values(streams_of[1], (LENGTH, FEAT), 1.0, 6.0, ((0, 256),))
    value = normal_values(streams_of[2], (LENGTH, FEAT), 1.0, 6.0, ((0, 256),))
    output = normal_values(streams_of[3], (LENGTH, FEAT), 1.0, 6.0, ((0, 256),))
    grad_out = normal_values(streams_of[4], (LENGTH, FEAT), 1.0, 6.0, ((0, 256),))
    logsumexp = draw_logsumexp(jax.random.fold_in(streams_of[7], 71), 0)
    rand_blocks = draw_rand_blocks(jax.random.fold_in(streams_of[7], 71), 0)
    return {"query": query, "key": key, "value": value, "output": output, "grad_out": grad_out, "logsumexp": logsumexp, "rand_blocks": rand_blocks}


def block_grads(queries, grad_rows, log_norm, deltas, keys, values, usable, factor):
    query_wide = queries.astype(jnp.float32)
    grad_wide = grad_rows.astype(jnp.float32)
    key_wide = keys.astype(jnp.float32)
    value_wide = values.astype(jnp.float32)
    scores = jnp.einsum('...md,...nd->...mn', query_wide, key_wide) * factor
    weights = jnp.where(usable, jnp.exp(scores - log_norm[..., None]), 0.0)
    weights_low = weights.astype(jnp.bfloat16).astype(jnp.float32)
    grad_values = jnp.einsum('...mn,...md->...nd', weights_low, grad_wide)
    grad_probs = jnp.einsum('...md,...nd->...mn', grad_wide, value_wide)
    grad_scores = (weights * (grad_probs - deltas[..., None])).astype(jnp.bfloat16).astype(jnp.float32)
    grad_queries = jnp.einsum('...mn,...nd->...md', grad_scores, key_wide) * factor
    grad_keys = jnp.einsum('...mn,...md->...nd', grad_scores, query_wide) * factor
    return (grad_queries, grad_keys, grad_values)

def reference(query, key, value, output, grad_out, logsumexp, rand_blocks):
    factor = 1.0 / math.sqrt(HD)
    block_ids = jnp.arange(NQB, dtype=jnp.int32)
    offsets = jnp.array([-1, 0, 1], dtype=jnp.int32)
    window = block_ids[:, None] + offsets[None, :]
    window_ok = (window >= GLOB) & (window < NQB)
    global_ids = jnp.broadcast_to(jnp.arange(GLOB, dtype=jnp.int32)[None, :], (NQB, GLOB))
    key_ids = jnp.concatenate([global_ids, jnp.clip(window, 0, NQB - 1), rand_blocks.astype(jnp.int32)], axis=1)
    key_ok = jnp.concatenate([jnp.ones((NQB, GLOB), bool), window_ok, jnp.ones((NQB, RAND), bool)], axis=1)
    key_ok = key_ok & (block_ids >= GLOB)[:, None]
    key_count = GLOB + 3 + RAND
    column_ok = jnp.repeat(key_ok, BLK, axis=1)
    glob_rows = GLOB * BLK

    def one_head(head_index):

        def columns(matrix):
            return lax.dynamic_slice_in_dim(matrix, head_index * HD, HD, 1)
        query_head = columns(query)
        key_head = columns(key)
        value_head = columns(value)
        grad_head = columns(grad_out)
        out_head = columns(output)
        norm_head = lax.dynamic_slice_in_dim(logsumexp, head_index, 1, 0)[0]
        delta_head = lax.optimization_barrier(jnp.sum(grad_head.astype(jnp.float32) * out_head.astype(jnp.float32), axis=-1))
        query_blk = query_head.reshape(NQB, BLK, HD)
        grad_blk = grad_head.reshape(NQB, BLK, HD)
        key_blk = key_head.reshape(NQB, BLK, HD)
        value_blk = value_head.reshape(NQB, BLK, HD)
        key_sel = key_blk[key_ids].reshape(NQB, key_count * BLK, HD)
        value_sel = value_blk[key_ids].reshape(NQB, key_count * BLK, HD)
        part_q, part_k, part_v = block_grads(query_blk, grad_blk, norm_head.reshape(NQB, BLK), delta_head.reshape(NQB, BLK), key_sel, value_sel, column_ok[:, None, :], factor)
        grad_k = jnp.zeros((NQB, BLK, HD), jnp.float32).at[key_ids].add(part_k.reshape(NQB, key_count, BLK, HD))
        grad_v = jnp.zeros((NQB, BLK, HD), jnp.float32).at[key_ids].add(part_v.reshape(NQB, key_count, BLK, HD))
        glob_q, glob_k, glob_v = block_grads(query_head[:glob_rows], grad_head[:glob_rows], norm_head[:glob_rows], delta_head[:glob_rows], key_head, value_head, True, factor)
        grad_q = part_q.reshape(LENGTH, HD).at[:glob_rows].add(glob_q)
        grad_k = grad_k.reshape(LENGTH, HD) + glob_k
        grad_v = grad_v.reshape(LENGTH, HD) + glob_v
        return (grad_q, grad_k, grad_v)
    grad_q, grad_k, grad_v = lax.map(one_head, jnp.arange(HEADS, dtype=jnp.int32))

    def to_tokens(stack):
        return stack.transpose(1, 0, 2).reshape(LENGTH, HEADS * HD).astype(jnp.bfloat16)
    return (to_tokens(grad_q), to_tokens(grad_k), to_tokens(grad_v))
```

```python
import jax
import jax.numpy as jnp
from jax import lax
from jax.experimental import pallas as pl
from jax.experimental.pallas import tpu as pltpu
from jax.sharding import PartitionSpec as P

HEADS = 16
HD = 128
BLK = 64
GLOB = 2
RAND = 3
NB = 16
FACTOR = HD ** (-0.5)
OFF = 1e30
SLAB = 4 * BLK + 16
PAIR = RAND * 2 * BLK + 16
F32 = jnp.float32
BF16 = jnp.bfloat16

VM = pl.BlockSpec(memory_space=pltpu.VMEM)
SM = pl.BlockSpec(memory_space=pltpu.SMEM)


def call(body, outs, in_specs, flops=0, nbytes=0, scratch=(), aliases={}):
    return pl.pallas_call(
        body,
        out_shape=outs,
        in_specs=in_specs,
        out_specs=jax.tree.map(lambda _: VM, outs),
        scratch_shapes=list(scratch),
        input_output_aliases=aliases,
        compiler_params=pltpu.CompilerParams(vmem_limit_bytes=32 << 20),
        cost_estimate=pl.CostEstimate(flops=flops, bytes_accessed=nbytes, transcendentals=0),
    )


def nt(a, b):
    return lax.dot_general(a, b, (((1,), (1,)), ((), ())), preferred_element_type=F32)


def nn(a, b):
    return lax.dot_general(a, b, (((1,), (0,)), ((), ())), preferred_element_type=F32)


def tn(a, b):
    return lax.dot_general(a, b, (((0,), (0,)), ((), ())), preferred_element_type=F32)


def pieces(x):
    high = x.astype(BF16).astype(F32)
    return high, (x - high).astype(BF16).astype(F32)


def pack_body(q, k, v, o, g, out):
    lane = lax.broadcasted_iota(jnp.int32, (BLK, HD), 1)
    row = lax.broadcasted_iota(jnp.int32, (16, HD), 0)
    deltas = jnp.zeros((BLK, HD), F32)
    for h in range(HEADS):
        cols = pl.ds(h * HD, HD)
        gh = g[:, cols]
        out[h, 0:64] = q[:, cols]
        out[h, 64:128] = k[:, cols]
        out[h, 128:192] = v[:, cols]
        out[h, 192:256] = gh
        part = jnp.sum(gh.astype(F32) * o[:, cols].astype(F32), axis=1, keepdims=True)
        deltas = jnp.where(lane == h, part, deltas)
    turned = jnp.transpose(jnp.concatenate([deltas, jnp.zeros((BLK, HD), F32)], axis=0))
    high, low = pieces(turned)
    for h in range(HEADS):
        tile = jnp.where(row == 0, high[h : h + 1], jnp.where(row == 1, low[h : h + 1], 0.0))
        out[h, 256:272] = tile.astype(BF16)


def table_body(pos, entries, out):
    here = pos[0]
    e = entries[...]
    width = e.shape[1]
    lane = lax.broadcasted_iota(jnp.int32, (NB, width), 1)
    row = lax.broadcasted_iota(jnp.int32, (NB, width), 0)
    mine = jnp.sum(jnp.where(row == here, e, 0), axis=0, keepdims=True)
    to_group = jnp.broadcast_to(mine, (NB, width)) >> 4
    hit = jnp.concatenate(
        [jnp.where(to_group == row, 1.0, 0.0), jnp.where((e >> 4) == here, 1.0, 0.0)], axis=0
    )
    value = jnp.concatenate([(lane * 171) >> 9, e & 15], axis=0)
    ii = lax.broadcasted_iota(jnp.int32, (width, width), 0)
    jj = lax.broadcasted_iota(jnp.int32, (width, width), 1)
    before = jnp.where(ii < jj, 1.0, 0.0).astype(BF16)
    rank = nn(hit.astype(BF16), before)
    out_lane = lax.broadcasted_iota(jnp.int32, (2 * NB, HD), 1)
    result = jnp.zeros((2 * NB, HD), jnp.int32)
    for r in range(RAND):
        chosen = jnp.where((hit > 0.5) & (jnp.abs(rank - r) < 0.5), value, 0)
        total = jnp.sum(chosen, axis=1, keepdims=True)
        result = jnp.where(out_lane == r, total, result)
    out[...] = result


def norm_rows(lse, b):
    pair = lse[:, (b // 2) * HD : (b // 2 + 1) * HD]
    return pair[:, 64:128] if b % 2 else pair[:, 0:64]


def select_body(pos, table, x, lse, out, halo, glob, ext):
    row = lax.broadcasted_iota(jnp.int32, (16, BLK), 0)
    lse_all = lse[...]

    def ext_of(b, norm):
        high, low = pieces(norm)
        tile = jnp.where(row == 2, high, jnp.where(row == 3, low, 0.0))
        return x[b, 256:272, 0:64].astype(F32) + tile

    for b in range(NB):
        norm = norm_rows(lse_all, b)
        if b < GLOB:
            plain = ext_of(b, norm)
            glob[b, 0:256] = x[b, 0:256]
            glob[b, 256:272] = jnp.concatenate([plain, plain], axis=1).astype(BF16)
            norm = jnp.where(pos[0] == 0, OFF, norm)
        ext[b] = ext_of(b, norm)
        if b == NB - 1:
            halo[0:256] = x[b, 0:256]
            halo[256:272] = jnp.concatenate([ext[b], ext[b]], axis=1).astype(BF16)

    rows16 = lax.broadcasted_iota(jnp.int32, (16, BLK), 0)

    def step(t, carry):
        tile = jnp.zeros((16, BLK), F32)
        for r in range(RAND):
            b = table[t, r]
            out[t, r * 128 : r * 128 + 64] = x[b, 0:64]
            out[t, r * 128 + 64 : r * 128 + 128] = x[b, 192:256]
            part = ext[b]
            if r:
                part = pltpu.roll(part, 4 * r, 0)
            tile = tile + part
        out[t, 384:400] = jnp.concatenate([tile, tile], axis=1).astype(BF16)
        return carry

    lax.fori_loop(0, NB, step, 0)


def grads(q, g, norm, delta, k, v, keep=None):
    st = nt(k, q) * FACTOR
    pt = jnp.exp(st - norm)
    if keep is not None:
        pt = jnp.where(keep, pt, 0.0)
    dst = (pt * (nt(v, g) - delta)).astype(BF16)
    return tn(dst, k), nn(dst, q), nn(pt.astype(BF16), g)


def home_body(pos, x, lse, glob, halo, dq, dk, dv, gpart, hback):
    here = pos[0]
    lse_all = lse[...]
    lanes = lax.broadcasted_iota(jnp.int32, lse_all.shape, 1)
    lse_all = jnp.where((here == 0) & (lanes < GLOB * BLK), OFF, lse_all)

    def two(ext, a):
        return ext[a : a + 1].astype(F32) + ext[a + 1 : a + 2].astype(F32)

    def part(b, a):
        return x[b, a * 64 : (a + 1) * 64]

    def rows(b, a):
        return jnp.concatenate([part(b, a), part(b + 1, a)], axis=0)

    gq = jnp.concatenate([glob[0, 0:64], glob[1, 0:64]], axis=0)
    gk = jnp.concatenate([glob[0, 64:128], glob[1, 64:128]], axis=0)
    gv = jnp.concatenate([glob[0, 128:192], glob[1, 128:192]], axis=0)
    gg = jnp.concatenate([glob[0, 192:256], glob[1, 192:256]], axis=0)
    ext0 = glob[0, 256:272].astype(F32)
    ext1 = glob[1, 256:272].astype(F32)
    gdelta = jnp.concatenate([two(ext0, 0)[:, 0:64], two(ext1, 0)[:, 0:64]], axis=1)
    gnorm = jnp.concatenate([two(ext0, 2)[:, 0:64], two(ext1, 2)[:, 0:64]], axis=1)

    gq_sum = jnp.zeros((HD, HD), F32)
    gk_sum = jnp.zeros((HD, HD), F32)
    gv_sum = jnp.zeros((HD, HD), F32)
    for i in range(NB // 2):
        b = 2 * i
        fq, fk, fv = grads(gq, gg, gnorm, gdelta, rows(b, 1), rows(b, 2))
        gq_sum = gq_sum + fq
        dk[b * 64 : b * 64 + 128] = fk
        dv[b * 64 : b * 64 + 128] = fv
    for i in range(NB // 2):
        b = 2 * i
        q2, g2 = rows(b, 0), rows(b, 3)
        norm = lse_all[:, i * HD : (i + 1) * HD]
        e0 = x[b, 256:272].astype(F32)
        e1 = x[b + 1, 256:272].astype(F32)
        delta = jnp.concatenate([two(e0, 0)[:, 0:64], two(e1, 0)[:, 0:64]], axis=1)
        low, high = max(b - 1, 0), min(b + 3, NB)
        count = high - low
        keys = jnp.concatenate([gk] + [part(n, 1) for n in range(low, high)], axis=0)
        vals = jnp.concatenate([gv] + [part(n, 2) for n in range(low, high)], axis=0)
        shape = (HD + count * BLK, HD)
        sub = lax.broadcasted_iota(jnp.int32, shape, 0)
        lane = lax.broadcasted_iota(jnp.int32, shape, 1)
        kb = (sub >> 6) - 2 + low
        qb = (lane >> 6) + b
        keep = (sub < HD) | (jnp.abs(kb - qb) <= 1)
        if i <= 1:
            keep = keep & ((sub < HD) | (here > 0) | (kb >= GLOB))
        wq, wk, wv = grads(q2, g2, norm, delta, keys, vals, keep)
        dq[b * 64 : b * 64 + 128] = wq
        gk_sum = gk_sum + wk[0:HD]
        gv_sum = gv_sum + wv[0:HD]
        span = slice(low * 64, high * 64)
        dk[span] = dk[span] + wk[HD:]
        dv[span] = dv[span] + wv[HD:]
    hext = halo[256:272].astype(F32)
    hdelta = two(hext, 0)[:, 0:64]
    hnorm = jnp.where(here == 0, OFF, two(hext, 2)[:, 0:64])
    hq, hk, hv, hg = halo[0:64], halo[64:128], halo[128:192], halo[192:256]
    e0 = x[0, 256:272].astype(F32)
    aq, ak, av = grads(
        part(0, 0), part(0, 3), lse_all[:, 0:64], two(e0, 0)[:, 0:64], hk, hv
    )
    bq, bk, bv = grads(hq, hg, hnorm, hdelta, part(0, 1), part(0, 2))
    dq[0:64] = dq[0:64] + aq
    dk[0:64] = dk[0:64] + bk
    dv[0:64] = dv[0:64] + bv
    hback[0:64] = (bq * FACTOR).astype(BF16)
    hback[64:128] = (ak * FACTOR).astype(BF16)
    hback[128:192] = av.astype(BF16)
    gpart[0] = gq_sum * FACTOR
    gpart[1] = gk_sum * FACTOR
    gpart[2] = gv_sum


def rand_body(table, x, y, dk_in, dv_in, dk, dv, z):
    dk[...] = dk_in[...]
    dv[...] = dv_in[...]

    def step(t, carry):
        ext = y[t, 384:400].astype(F32)
        for r in range(RAND):
            j = table[NB + t, r]
            k = x[j, 64:128]
            v = x[j, 128:192]
            q = y[t, r * 128 : r * 128 + 64]
            g = y[t, r * 128 + 64 : r * 128 + 128]
            delta = (ext[4 * r : 4 * r + 1] + ext[4 * r + 1 : 4 * r + 2])[:, 0:64]
            norm = (ext[4 * r + 2 : 4 * r + 3] + ext[4 * r + 3 : 4 * r + 4])[:, 0:64]
            pq, pk, pv = grads(q, g, norm, delta, k, v)
            z[t, r * 64 : r * 64 + 64] = (pq * FACTOR).astype(BF16)
            span = pl.ds(pl.multiple_of(j * 64, 64), 64)
            dk[span] = dk[span] + pk
            dv[span] = dv[span] + pv
        return carry

    lax.fori_loop(0, NB, step, 0)


def merge_body(pos, table, dq, dk, dv, z, hback, gtot, out, acc):
    acc[...] = dq[...] * FACTOR

    def step(t, carry):
        for r in range(RAND):
            b = table[t, r]
            span = pl.ds(pl.multiple_of(b * 64, 64), 64)
            acc[span] = acc[span] + z[t, r * 64 : r * 64 + 64].astype(F32)
        return carry

    lax.fori_loop(0, NB, step, 0)
    home = jnp.where(pos[0] == 0, 1.0, 0.0)
    for b in range(NB):
        span = slice(b * 64, b * 64 + 64)
        rq, rk, rv = acc[span], dk[span] * FACTOR, dv[span]
        if b < GLOB:
            rq = rq + home * gtot[0, span]
            rk = rk + home * gtot[1, span]
            rv = rv + home * gtot[2, span]
        if b == NB - 1:
            rq = rq + hback[0:64].astype(F32)
            rk = rk + hback[64:128].astype(F32)
            rv = rv + hback[128:192].astype(F32)
        out[b, 0:64] = rq.astype(BF16)
        out[b, 64:128] = rk.astype(BF16)
        out[b, 128:192] = rv.astype(BF16)


def unpack_body(w, q, k, v):
    for h in range(HEADS):
        cols = pl.ds(h * HD, HD)
        q[:, cols] = w[h, 0:64]
        k[:, cols] = w[h, 64:128]
        v[:, cols] = w[h, 128:192]


def struct(shape, dtype=BF16):
    return jax.ShapeDtypeStruct(shape, dtype)


def exchange(x, axis):
    return lax.all_to_all(x, axis, split_axis=0, concat_axis=0, tiled=True)


def per_device(query, key, value, output, grad_out, logsumexp, rand_blocks):
    position = lax.axis_index("seq")
    pos = position.astype(jnp.int32).reshape(1)
    rows = NB * BLK
    packed = call(
        pack_body, struct((HEADS, SLAB, HD)), [VM] * 5, nbytes=5 << 18
    )(query, key, value, output, grad_out)
    x = exchange(packed, "head")
    table = call(table_body, struct((2 * NB, HD), jnp.int32), [SM, VM], nbytes=1 << 14)(
        pos, rand_blocks.reshape(NB, NB * RAND)
    )
    y, halo, glob = call(
        select_body,
        (struct((NB, PAIR, HD)), struct((SLAB, HD)), struct((GLOB, SLAB, HD))),
        [SM, SM, VM, VM],
        nbytes=3 << 20,
        scratch=[pltpu.VMEM((NB, 16, BLK), F32)],
    )(pos, table, x, logsumexp)
    groups = NB
    halo = lax.ppermute(halo, "seq", [(s, s + 1) for s in range(groups - 1)])
    glob = jnp.where(position == 0, glob, 0).astype(BF16)
    for reach in (8, 4, 2, 1):
        moved = lax.ppermute(
            glob, "seq", [(s, s + reach) for s in range(0, groups, 2 * reach)]
        )
        glob = jnp.where(position % (2 * reach) == reach, moved, glob)
    y = exchange(y, "seq")
    dq, dk, dv, gpart, hback = call(
        home_body,
        (
            struct((rows, HD), F32),
            struct((rows, HD), F32),
            struct((rows, HD), F32),
            struct((3, HD, HD), F32),
            struct((3 * BLK, HD)),
        ),
        [SM, VM, VM, VM, VM],
        flops=1 << 30,
        nbytes=4 << 20,
    )(pos, x, logsumexp, glob, halo)
    hback = lax.ppermute(hback, "seq", [(s, s - 1) for s in range(1, groups)])
    dk, dv, z = call(
        rand_body,
        (struct((rows, HD), F32), struct((rows, HD), F32), struct((NB, RAND * BLK, HD))),
        [SM, VM, VM, VM, VM],
        flops=1 << 28,
        nbytes=6 << 20,
        aliases={3: 0, 4: 1},
    )(table, x, y, dk, dv)
    z = exchange(z, "seq")
    for reach in (1, 2, 4, 8):
        moved = lax.ppermute(
            gpart.astype(BF16),
            "seq",
            [(s + reach, s) for s in range(0, groups, 2 * reach)],
        )
        gpart = gpart + moved.astype(F32)
    w = call(
        merge_body,
        struct((NB, 3 * BLK, HD)),
        [SM, SM, VM, VM, VM, VM, VM, VM],
        nbytes=4 << 20,
        scratch=[pltpu.VMEM((rows, HD), F32)],
    )(pos, table, dq, dk, dv, z, hback, gpart)
    w = exchange(w, "head")
    shape = struct((BLK, HEADS * HD))
    return call(unpack_body, (shape, shape, shape), [VM], nbytes=3 << 19)(w)


def solution(mesh):
    in_specs = (
        P(("seq", "head"), None),
        P(("seq", "head"), None),
        P(("seq", "head"), None),
        P(("seq", "head"), None),
        P(("seq", "head"), None),
        P("head", "seq"),
        P(),
    )
    out_specs = (P(("seq", "head"), None), P(("seq", "head"), None), P(("seq", "head"), None))
    return jax.shard_map(
        per_device, mesh=mesh, in_specs=in_specs, out_specs=out_specs, check_vma=False
    )
```

```python
import functools

import jax
import jax.numpy as jnp
from jax import lax
from jax.experimental import pallas as pl
from jax.experimental.pallas import tpu as pltpu
from jax.sharding import PartitionSpec as P

HEADS = 16
HD = 128
BLK = 64
GLOB = 2
RAND = 3
NB = 16
FACTOR = HD ** (-0.5)
OFF = 1e30
EDGES = (0, 1, NB - 1)
SLAB = 4 * BLK + 16
PAIR = RAND * 2 * BLK + 16
F32 = jnp.float32
BF16 = jnp.bfloat16

HB = pl.BlockSpec(memory_space=pltpu.HBM)
VM = pl.BlockSpec(memory_space=pltpu.VMEM)
SM = pl.BlockSpec(memory_space=pltpu.SMEM)


def call(body, outs, in_specs, out_specs, flops=0, nbytes=0, scratch=(), aliases={}, limit=8):
    return pl.pallas_call(
        body,
        out_shape=outs,
        in_specs=in_specs,
        out_specs=out_specs,
        scratch_shapes=list(scratch),
        input_output_aliases=aliases,
        compiler_params=pltpu.CompilerParams(vmem_limit_bytes=limit << 20),
        cost_estimate=pl.CostEstimate(flops=flops, bytes_accessed=nbytes, transcendentals=0),
    )


def nt(a, b):
    return lax.dot_general(a, b, (((1,), (1,)), ((), ())), preferred_element_type=F32)


def nn(a, b):
    return lax.dot_general(a, b, (((1,), (0,)), ((), ())), preferred_element_type=F32)


def tn(a, b):
    return lax.dot_general(a, b, (((0,), (0,)), ((), ())), preferred_element_type=F32)


def pieces(x):
    high = x.astype(BF16).astype(F32)
    return high, (x - high).astype(BF16).astype(F32)


def pack_body(q, k, v, o, g, out, qs, ks, vs, os, gs, ps, in_sem, out_sem):
    pulls = [
        pltpu.make_async_copy(src, dst, in_sem.at[i])
        for i, (src, dst) in enumerate(zip((o, g, q, k, v), (os, gs, qs, ks, vs)))
    ]
    for pull in pulls:
        pull.start()
    lane = lax.broadcasted_iota(jnp.int32, (BLK, HD), 1)
    row = lax.broadcasted_iota(jnp.int32, (16, HD), 0)
    deltas = jnp.zeros((BLK, HD), F32)
    pulls[0].wait()
    pulls[1].wait()
    for h in range(HEADS):
        cols = pl.ds(h * HD, HD)
        gh = gs[:, cols]
        ps[h, 192:256] = gh
        part = jnp.sum(gh.astype(F32) * os[:, cols].astype(F32), axis=1, keepdims=True)
        deltas = jnp.where(lane == h, part, deltas)
    turned = jnp.transpose(jnp.concatenate([deltas, jnp.zeros((BLK, HD), F32)], axis=0))
    high, low = pieces(turned)
    for pull in pulls[2:]:
        pull.wait()
    pushes = []
    for h in range(HEADS):
        cols = pl.ds(h * HD, HD)
        ps[h, 0:64] = qs[:, cols]
        ps[h, 64:128] = ks[:, cols]
        ps[h, 128:192] = vs[:, cols]
        tile = jnp.where(row == 0, high[h : h + 1], jnp.where(row == 1, low[h : h + 1], 0.0))
        ps[h, 256:272] = tile.astype(BF16)
        push = pltpu.make_async_copy(ps.at[h], out.at[h], out_sem.at[h])
        push.start()
        pushes.append(push)
    for push in pushes:
        push.wait()


def table_body(pos, entries, out):
    here = pos[0]
    e = entries[...]
    width = e.shape[1]
    lane = lax.broadcasted_iota(jnp.int32, (NB, width), 1)
    row = lax.broadcasted_iota(jnp.int32, (NB, width), 0)
    mine = jnp.sum(jnp.where(row == here, e, 0), axis=0, keepdims=True)
    to_group = jnp.broadcast_to(mine, (NB, width)) >> 4
    hit = jnp.concatenate(
        [jnp.where(to_group == row, 1.0, 0.0), jnp.where((e >> 4) == here, 1.0, 0.0)], axis=0
    )
    value = jnp.concatenate([(lane * 171) >> 9, e & 15], axis=0)
    ii = lax.broadcasted_iota(jnp.int32, (width, width), 0)
    jj = lax.broadcasted_iota(jnp.int32, (width, width), 1)
    before = jnp.where(ii < jj, 1.0, 0.0).astype(BF16)
    rank = nn(hit.astype(BF16), before)
    out_lane = lax.broadcasted_iota(jnp.int32, (2 * NB, HD), 1)
    result = jnp.zeros((2 * NB, HD), jnp.int32)
    for r in range(RAND):
        chosen = jnp.where((hit > 0.5) & (jnp.abs(rank - r) < 0.5), value, 0)
        total = jnp.sum(chosen, axis=1, keepdims=True)
        result = jnp.where(out_lane == r, total, result)
    out[...] = result


def norm_rows(lse, b):
    pair = lse[:, (b // 2) * HD : (b // 2 + 1) * HD]
    return pair[:, 64:128] if b % 2 else pair[:, 0:64]


def select_body(pos, table, x, lse, dest, halo, glob, ext, out, sem):
    row = lax.broadcasted_iota(jnp.int32, (16, BLK), 0)
    lse_all = lse[...]

    def ext_of(b, norm):
        high, low = pieces(norm)
        tile = jnp.where(row == 2, high, jnp.where(row == 3, low, 0.0))
        return x[b, 256:272, 0:64].astype(F32) + tile

    for b in range(NB):
        norm = norm_rows(lse_all, b)
        if b < GLOB:
            plain = ext_of(b, norm)
            full = jnp.concatenate([plain, plain], axis=1).astype(BF16)
            keep = pos[0] == 0
            glob[b, 0:256] = jnp.where(keep, x[b, 0:256], jnp.zeros((256, HD), BF16))
            glob[b, 256:272] = jnp.where(keep, full, jnp.zeros((16, HD), BF16))
            norm = jnp.where(pos[0] == 0, OFF, norm)
        ext[b] = ext_of(b, norm)
        if b == NB - 1:
            halo[0:256] = x[b, 0:256]
            halo[256:272] = jnp.concatenate([ext[b], ext[b]], axis=1).astype(BF16)

    rows16 = lax.broadcasted_iota(jnp.int32, (16, BLK), 0)

    def step(t, carry):
        tile = jnp.zeros((16, BLK), F32)
        for r in range(RAND):
            b = table[t, r]
            out[t, r * 128 : r * 128 + 64] = x[b, 0:64]
            out[t, r * 128 + 64 : r * 128 + 128] = x[b, 192:256]
            part = ext[b]
            if r:
                part = pltpu.roll(part, 4 * r, 0)
            tile = tile + part
        out[t, 384:400] = jnp.concatenate([tile, tile], axis=1).astype(BF16)
        pltpu.make_async_copy(out.at[t], dest.at[t], sem.at[t]).start()
        return carry

    lax.fori_loop(0, NB, step, 0)

    def finish(t, carry):
        pltpu.make_async_copy(out.at[t], dest.at[t], sem.at[t]).wait()
        return carry

    lax.fori_loop(0, NB, finish, 0)


def grads(q, g, norm, delta, k, v, keep=None):
    st = nt(k, q) * FACTOR
    pt = jnp.exp(st - norm)
    if keep is not None:
        pt = jnp.where(keep, pt, 0.0)
    dst = (pt * (nt(v, g) - delta)).astype(BF16)
    return tn(dst, k), nn(dst, q), nn(pt.astype(BF16), g)


def home_body(
    pos, x, lse, glob, halo, dk_far, dv_far, w, dq, edge, gpart, glow, hback,
    dk, dv, dk_in, dv_in, buf, in_sem, out_sem,
):
    here = pos[0]
    pulls = [
        pltpu.make_async_copy(dk_far, dk_in, in_sem.at[0]),
        pltpu.make_async_copy(dv_far, dv_in, in_sem.at[1]),
    ]
    for pull in pulls:
        pull.start()
    lse_all = lse[...]
    lanes = lax.broadcasted_iota(jnp.int32, lse_all.shape, 1)
    lse_all = jnp.where((here == 0) & (lanes < GLOB * BLK), OFF, lse_all)

    def two(ext, a):
        return ext[a : a + 1].astype(F32) + ext[a + 1 : a + 2].astype(F32)

    def part(b, a):
        return x[b, a * 64 : (a + 1) * 64]

    def rows(b, a):
        return jnp.concatenate([part(b, a), part(b + 1, a)], axis=0)

    gq = jnp.concatenate([glob[0, 0:64], glob[1, 0:64]], axis=0)
    gk = jnp.concatenate([glob[0, 64:128], glob[1, 64:128]], axis=0)
    gv = jnp.concatenate([glob[0, 128:192], glob[1, 128:192]], axis=0)
    gg = jnp.concatenate([glob[0, 192:256], glob[1, 192:256]], axis=0)
    ext0 = glob[0, 256:272].astype(F32)
    ext1 = glob[1, 256:272].astype(F32)
    gdelta = jnp.concatenate([two(ext0, 0)[:, 0:64], two(ext1, 0)[:, 0:64]], axis=1)
    gnorm = jnp.concatenate([two(ext0, 2)[:, 0:64], two(ext1, 2)[:, 0:64]], axis=1)

    gq_sum = jnp.zeros((HD, HD), F32)
    gk_sum = jnp.zeros((HD, HD), F32)
    gv_sum = jnp.zeros((HD, HD), F32)
    for i in range(NB // 2):
        b = 2 * i
        fq, fk, fv = grads(gq, gg, gnorm, gdelta, rows(b, 1), rows(b, 2))
        gq_sum = gq_sum + fq
        span = slice(b * 64, b * 64 + 128)
        dk[span] = fk
        dv[span] = fv
    for i in range(NB // 2):
        b = 2 * i
        q2, g2 = rows(b, 0), rows(b, 3)
        norm = lse_all[:, i * HD : (i + 1) * HD]
        e0 = x[b, 256:272].astype(F32)
        e1 = x[b + 1, 256:272].astype(F32)
        delta = jnp.concatenate([two(e0, 0)[:, 0:64], two(e1, 0)[:, 0:64]], axis=1)
        low, high = max(b - 1, 0), min(b + 3, NB)
        count = high - low
        keys = jnp.concatenate([gk] + [part(n, 1) for n in range(low, high)], axis=0)
        vals = jnp.concatenate([gv] + [part(n, 2) for n in range(low, high)], axis=0)
        shape = (HD + count * BLK, HD)
        sub = lax.broadcasted_iota(jnp.int32, shape, 0)
        lane = lax.broadcasted_iota(jnp.int32, shape, 1)
        kb = (sub >> 6) - 2 + low
        qb = (lane >> 6) + b
        keep = (sub < HD) | (jnp.abs(kb - qb) <= 1)
        if i <= 1:
            keep = keep & ((sub < HD) | (here > 0) | (kb >= GLOB))
        wq, wk, wv = grads(q2, g2, norm, delta, keys, vals, keep)
        dq[b * 64 : b * 64 + 128] = wq
        gk_sum = gk_sum + wk[0:HD]
        gv_sum = gv_sum + wv[0:HD]
        span = slice(low * 64, high * 64)
        dk[span] = dk[span] + wk[HD:]
        dv[span] = dv[span] + wv[HD:]
    hext = halo[256:272].astype(F32)
    hdelta = two(hext, 0)[:, 0:64]
    hnorm = jnp.where(here == 0, OFF, two(hext, 2)[:, 0:64])
    hq, hk, hv, hg = halo[0:64], halo[64:128], halo[128:192], halo[192:256]
    e0 = x[0, 256:272].astype(F32)
    aq, ak, av = grads(
        part(0, 0), part(0, 3), lse_all[:, 0:64], two(e0, 0)[:, 0:64], hk, hv
    )
    bq, bk, bv = grads(hq, hg, hnorm, hdelta, part(0, 1), part(0, 2))
    dq[0:64] = dq[0:64] + aq
    dk[0:64] = dk[0:64] + bk
    dv[0:64] = dv[0:64] + bv
    hback[0:64] = (bq * FACTOR).astype(BF16)
    hback[64:128] = (ak * FACTOR).astype(BF16)
    hback[128:192] = av.astype(BF16)
    for n, total in enumerate((gq_sum * FACTOR, gk_sum * FACTOR, gv_sum)):
        gpart[n] = total
        glow[n] = total.astype(BF16)
    for pull in pulls:
        pull.wait()
    pushes = []
    for b in range(NB):
        span = slice(b * 64, b * 64 + 64)
        rk = (dk[span] + dk_in[span]) * FACTOR
        rv = dv[span] + dv_in[span]
        if b in EDGES:
            at = EDGES.index(b) * 128
            edge[at : at + 64] = rk
            edge[at + 64 : at + 128] = rv
            continue
        buf[b, 0:64] = rk.astype(BF16)
        buf[b, 64:128] = rv.astype(BF16)
        push = pltpu.make_async_copy(buf.at[b], w.at[b, pl.ds(64, 128)], out_sem.at[b])
        push.start()
        pushes.append(push)
    for push in pushes:
        push.wait()


def rand_body(first, last, per_step, table, x, y, *refs):
    ended = last == NB
    if first:
        dk_in, dv_in, z_in = refs[:3]
        refs = refs[3:]
    if ended:
        dk_out, dv_out, z, dk, dv, buf, sem, acc_sem = refs
        head = pltpu.make_async_copy(z_in, z.at[pl.ds(0, first)], sem.at[NB])
        head.start()
        target, base = buf, first
    else:
        dk, dv, z = refs
        target, base = z, 0
        if first:
            z[0:first] = z_in[...]
    if first:
        dk[...] = dk_in[...]
        dv[...] = dv_in[...]
    else:
        dk[...] = jnp.zeros_like(dk)
        dv[...] = jnp.zeros_like(dv)

    def step(i, carry):
        done = []
        for c in range(per_step):
            t = first + i * per_step + c
            ext = y[t, 384:400].astype(F32)
            for r in range(RAND):
                j = table[NB + t, r]
                k = x[j, 64:128]
                v = x[j, 128:192]
                q = y[t, r * 128 : r * 128 + 64]
                g = y[t, r * 128 + 64 : r * 128 + 128]
                delta = (ext[4 * r : 4 * r + 1] + ext[4 * r + 1 : 4 * r + 2])[:, 0:64]
                norm = (ext[4 * r + 2 : 4 * r + 3] + ext[4 * r + 3 : 4 * r + 4])[:, 0:64]
                pq, pk, pv = grads(q, g, norm, delta, k, v)
                target[t - base, r * 64 : r * 64 + 64] = (pq * FACTOR).astype(BF16)
                done.append((j, pk, pv))
            if ended:
                pltpu.make_async_copy(buf.at[t - base], z.at[t], sem.at[t]).start()
        for j, pk, pv in done:
            span = pl.ds(pl.multiple_of(j * 64, 64), 64)
            dk[span] = dk[span] + pk
            dv[span] = dv[span] + pv
        return carry

    lax.fori_loop(0, (last - first) // per_step, step, 0)
    if ended:
        drains = []
        for n in range(4):
            span = pl.ds(n * 256, 256)
            for m, (src, dst) in enumerate(((dk, dk_out), (dv, dv_out))):
                drain = pltpu.make_async_copy(src.at[span], dst.at[span], acc_sem.at[2 * n + m])
                drain.start()
                drains.append(drain)
        for drain in drains:
            drain.wait()
        head.wait()

        def finish(t, carry):
            pltpu.make_async_copy(buf.at[t - base], z.at[t], sem.at[t]).wait()
            return carry

        lax.fori_loop(first, last, finish, 0)


def merge_body(pos, table, dq, edge, z, hback, gtot, w_in, w, acc, out, out_edge, sem):
    acc[...] = dq[...] * FACTOR

    def step(t, carry):
        for r in range(RAND):
            b = table[t, r]
            span = pl.ds(pl.multiple_of(b * 64, 64), 64)
            acc[span] = acc[span] + z[t, r * 64 : r * 64 + 64].astype(F32)
        return carry

    lax.fori_loop(0, NB, step, 0)
    home = jnp.where(pos[0] == 0, 1.0, 0.0)
    pushes = []

    def send(src, dst, n):
        push = pltpu.make_async_copy(src, dst, sem.at[n])
        push.start()
        pushes.append(push)

    for n, b in enumerate(EDGES):
        rk, rv = edge[n * 128 : n * 128 + 64], edge[n * 128 + 64 : n * 128 + 128]
        if b < GLOB:
            rk = rk + home * gtot[1, b * 64 : b * 64 + 64]
            rv = rv + home * gtot[2, b * 64 : b * 64 + 64]
        else:
            rk = rk + hback[64:128].astype(F32)
            rv = rv + hback[128:192].astype(F32)
        out_edge[n, 0:64] = rk.astype(BF16)
        out_edge[n, 64:128] = rv.astype(BF16)
        send(out_edge.at[n], w.at[b, pl.ds(64, 128)], NB + n)
    for b in range(NB):
        span = slice(b * 64, b * 64 + 64)
        rq = acc[span]
        if b < GLOB:
            rq = rq + home * gtot[0, span]
        if b == NB - 1:
            rq = rq + hback[0:64].astype(F32)
        out[b] = rq.astype(BF16)
        send(out.at[b], w.at[b, pl.ds(0, 64)], b)
    for push in pushes:
        push.wait()


def unpack_body(w, q, k, v):
    for h in range(HEADS):
        cols = pl.ds(h * HD, HD)
        q[:, cols] = w[h, 0:64]
        k[:, cols] = w[h, 64:128]
        v[:, cols] = w[h, 128:192]


def struct(shape, dtype=BF16):
    return jax.ShapeDtypeStruct(shape, dtype)


def far(shape, dtype=BF16):
    return pltpu.HBM(shape, dtype)


def near(shape, dtype=BF16):
    return pltpu.VMEM(shape, dtype)


def hold(x):
    return pltpu.with_memory_space_constraint(x, pltpu.VMEM)


def keep_far(x):
    return pltpu.with_memory_space_constraint(x, pltpu.HBM)


def exchange(x, axis):
    return lax.all_to_all(x, axis, split_axis=0, concat_axis=0, tiled=True)


def per_device(query, key, value, output, grad_out, logsumexp, rand_blocks):
    position = lax.axis_index("seq")
    pos = position.astype(jnp.int32).reshape(1)
    rows = NB * BLK
    groups = NB
    dma = pltpu.SemaphoreType.DMA
    whole = pltpu.VMEM((BLK, HEADS * HD), BF16)
    packed = call(
        pack_body,
        far((HEADS, SLAB, HD)),
        [HB] * 5,
        HB,
        nbytes=5 << 18,
        scratch=[whole] * 5 + [pltpu.VMEM((HEADS, SLAB, HD), BF16), dma((5,)), dma((HEADS,))],
    )(*map(keep_far, (query, key, value, output, grad_out)))
    x = exchange(packed, "head")
    table = call(table_body, struct((2 * NB, HD), jnp.int32), [SM, VM], VM, nbytes=1 << 14)(
        pos, rand_blocks.reshape(NB, NB * RAND)
    )
    y, halo, glob = call(
        select_body,
        (far((NB, PAIR, HD)), struct((SLAB, HD)), struct((GLOB, SLAB, HD))),
        [SM, SM, VM, VM],
        (HB, VM, VM),
        nbytes=3 << 20,
        scratch=[
            pltpu.VMEM((NB, 16, BLK), F32),
            pltpu.VMEM((NB, PAIR, HD), BF16),
            dma((NB,)),
        ],
    )(pos, table, x, logsumexp)
    y = exchange(y, "seq")
    halo = lax.ppermute(halo, "seq", [(s, s + 1) for s in range(groups - 1)])

    def spread(glob, reach):
        return glob + lax.ppermute(
            glob, "seq", [(s, s + reach) for s in range(0, groups, 2 * reach)]
        )

    glob = spread(glob, 8)
    glob, halo, y = lax.optimization_barrier((glob, halo, y))
    grid = pltpu.VMEM((rows, HD), F32)
    carried = ()
    cuts = (0, 5, 10, 16)
    for n in range(3):
        first, last = cuts[n], cuts[n + 1]
        final = last == NB
        place = far if final else near
        scratch = []
        if final:
            scratch = [
                grid,
                grid,
                pltpu.VMEM((last - first, RAND * BLK, HD), BF16),
                dma((NB + 1,)),
                dma((8,)),
            ]
        moving = spread(glob, 4 >> n)
        carried = call(
            functools.partial(rand_body, first, last, 2 if final else 5),
            (
                place((rows, HD), F32),
                place((rows, HD), F32),
                place((last, RAND * BLK, HD)),
            ),
            [SM] + [VM] * (2 + len(carried)),
            (HB if final else VM,) * 3,
            flops=1 << 28,
            nbytes=3 << 20,
            scratch=scratch,
        )(table, x, y, *map(hold, carried))
        glob, carried = lax.optimization_barrier((moving, carried))
    dk, dv, z = carried
    z = exchange(z, "seq")
    w, dq, edge, gpart, glow, hback = call(
        home_body,
        (
            far((NB, 3 * BLK, HD)),
            near((rows, HD), F32),
            struct((len(EDGES) * 2 * BLK, HD), F32),
            struct((3, HD, HD), F32),
            struct((3, HD, HD)),
            struct((3 * BLK, HD)),
        ),
        [SM] + [VM] * 4 + [HB] * 2,
        (HB,) + (VM,) * 5,
        flops=1 << 30,
        nbytes=4 << 20,
        scratch=[grid] * 4 + [pltpu.VMEM((NB, 2 * BLK, HD), BF16), dma((2,)), dma((NB,))],
    )(pos, x, logsumexp, glob, halo, keep_far(dk), keep_far(dv))
    hback = lax.ppermute(hback, "seq", [(s, s - 1) for s in range(1, groups)])
    for reach in (1, 4):
        span = range(0, groups, 4) if reach == 1 else (0,)
        for n in (1, 2, 3):
            moved = lax.ppermute(glow, "seq", [(s + n * reach, s) for s in span])
            gpart = gpart + moved.astype(F32)
        glow = gpart.astype(BF16)
    w = call(
        merge_body,
        far((NB, 3 * BLK, HD)),
        [SM, SM] + [VM] * 5 + [HB],
        HB,
        nbytes=4 << 20,
        scratch=[
            grid,
            pltpu.VMEM((NB, BLK, HD), BF16),
            pltpu.VMEM((len(EDGES), 2 * BLK, HD), BF16),
            dma((NB + len(EDGES),)),
        ],
        aliases={7: 0},
    )(pos, table, hold(dq), edge, z, hback, gpart, w)
    w = exchange(w, "head")
    shape = struct((BLK, HEADS * HD))
    return call(unpack_body, (shape, shape, shape), [VM], (VM,) * 3, nbytes=3 << 19)(w)


def solution(mesh):
    in_specs = (
        P(("seq", "head"), None),
        P(("seq", "head"), None),
        P(("seq", "head"), None),
        P(("seq", "head"), None),
        P(("seq", "head"), None),
        P("head", "seq"),
        P(),
    )
    out_specs = (P(("seq", "head"), None), P(("seq", "head"), None), P(("seq", "head"), None))
    return jax.shard_map(
        per_device, mesh=mesh, in_specs=in_specs, out_specs=out_specs, check_vma=False
    )
```

```python
import jax
import jax.numpy as jnp
from jax import lax
from jax.experimental import pallas as pl
from jax.experimental.pallas import tpu as pltpu
from jax.sharding import PartitionSpec as P

HEADS = 16
HD = 128
BLK = 64
GLOB = 2
RAND = 3
NB = 16
FACTOR = HD ** (-0.5)
OFF = 1e30
EDGES = (0, 1, NB - 1)
SLAB = 4 * BLK + 16
PAIR = RAND * 2 * BLK + 16
F32 = jnp.float32
BF16 = jnp.bfloat16

HB = pl.BlockSpec(memory_space=pltpu.HBM)
VM = pl.BlockSpec(memory_space=pltpu.VMEM)
SM = pl.BlockSpec(memory_space=pltpu.SMEM)


def call(body, outs, in_specs, out_specs, flops=0, nbytes=0, scratch=(), aliases={}, limit=8):
    return pl.pallas_call(
        body,
        out_shape=outs,
        in_specs=in_specs,
        out_specs=out_specs,
        scratch_shapes=list(scratch),
        input_output_aliases=aliases,
        compiler_params=pltpu.CompilerParams(vmem_limit_bytes=limit << 20),
        cost_estimate=pl.CostEstimate(flops=flops, bytes_accessed=nbytes, transcendentals=0),
    )


def nt(a, b):
    return lax.dot_general(a, b, (((1,), (1,)), ((), ())), preferred_element_type=F32)


def nn(a, b):
    return lax.dot_general(a, b, (((1,), (0,)), ((), ())), preferred_element_type=F32)


def tn(a, b):
    return lax.dot_general(a, b, (((0,), (0,)), ((), ())), preferred_element_type=F32)


def pieces(x):
    high = x.astype(BF16).astype(F32)
    return high, (x - high).astype(BF16).astype(F32)


def pack_body(q, k, v, o, g, out, qs, ks, vs, os, gs, ps, in_sem, out_sem):
    pulls = [
        pltpu.make_async_copy(src, dst, in_sem.at[i])
        for i, (src, dst) in enumerate(zip((o, g, q, k, v), (os, gs, qs, ks, vs)))
    ]
    for pull in pulls:
        pull.start()
    lane = lax.broadcasted_iota(jnp.int32, (BLK, HD), 1)
    row = lax.broadcasted_iota(jnp.int32, (16, HD), 0)
    deltas = jnp.zeros((BLK, HD), F32)
    pulls[0].wait()
    pulls[1].wait()
    for h in range(HEADS):
        cols = pl.ds(h * HD, HD)
        gh = gs[:, cols]
        ps[h, 192:256] = gh
        part = jnp.sum(gh.astype(F32) * os[:, cols].astype(F32), axis=1, keepdims=True)
        deltas = jnp.where(lane == h, part, deltas)
    turned = jnp.transpose(jnp.concatenate([deltas, jnp.zeros((BLK, HD), F32)], axis=0))
    high, low = pieces(turned)
    for pull in pulls[2:]:
        pull.wait()
    pushes = []
    for h in range(HEADS):
        cols = pl.ds(h * HD, HD)
        ps[h, 0:64] = qs[:, cols]
        ps[h, 64:128] = ks[:, cols]
        ps[h, 128:192] = vs[:, cols]
        tile = jnp.where(row == 0, high[h : h + 1], jnp.where(row == 1, low[h : h + 1], 0.0))
        ps[h, 256:272] = tile.astype(BF16)
        push = pltpu.make_async_copy(ps.at[h], out.at[h], out_sem.at[h])
        push.start()
        pushes.append(push)
    for push in pushes:
        push.wait()


def table_body(pos, entries, out):
    here = pos[0]
    e = entries[...]
    width = e.shape[1]
    lane = lax.broadcasted_iota(jnp.int32, (NB, width), 1)
    row = lax.broadcasted_iota(jnp.int32, (NB, width), 0)
    mine = jnp.sum(jnp.where(row == here, e, 0), axis=0, keepdims=True)
    to_group = jnp.broadcast_to(mine, (NB, width)) >> 4
    hit = jnp.concatenate(
        [jnp.where(to_group == row, 1.0, 0.0), jnp.where((e >> 4) == here, 1.0, 0.0)], axis=0
    )
    value = jnp.concatenate([(lane * 171) >> 9, e & 15], axis=0)
    ii = lax.broadcasted_iota(jnp.int32, (width, width), 0)
    jj = lax.broadcasted_iota(jnp.int32, (width, width), 1)
    before = jnp.where(ii < jj, 1.0, 0.0).astype(BF16)
    rank = nn(hit.astype(BF16), before)
    out_lane = lax.broadcasted_iota(jnp.int32, (2 * NB, HD), 1)
    result = jnp.zeros((2 * NB, HD), jnp.int32)
    for r in range(RAND):
        chosen = jnp.where((hit > 0.5) & (jnp.abs(rank - r) < 0.5), value, 0)
        total = jnp.sum(chosen, axis=1, keepdims=True)
        result = jnp.where(out_lane == r, total, result)
    out[...] = result


def norm_rows(lse, b):
    pair = lse[:, (b // 2) * HD : (b // 2 + 1) * HD]
    return pair[:, 64:128] if b % 2 else pair[:, 0:64]


def select_body(pos, table, x, lse, dest, halo, glob, ext, out, sem):
    row = lax.broadcasted_iota(jnp.int32, (16, BLK), 0)
    lse_all = lse[...]

    def ext_of(b, norm):
        high, low = pieces(norm)
        tile = jnp.where(row == 2, high, jnp.where(row == 3, low, 0.0))
        return x[b, 256:272, 0:64].astype(F32) + tile

    for b in range(NB):
        norm = norm_rows(lse_all, b)
        if b < GLOB:
            plain = ext_of(b, norm)
            full = jnp.concatenate([plain, plain], axis=1).astype(BF16)
            keep = pos[0] == 0
            glob[b, 0:256] = jnp.where(keep, x[b, 0:256], jnp.zeros((256, HD), BF16))
            glob[b, 256:272] = jnp.where(keep, full, jnp.zeros((16, HD), BF16))
            norm = jnp.where(pos[0] == 0, OFF, norm)
        ext[b] = ext_of(b, norm)
        if b == NB - 1:
            halo[0:256] = x[b, 0:256]
            halo[256:272] = jnp.concatenate([ext[b], ext[b]], axis=1).astype(BF16)

    rows16 = lax.broadcasted_iota(jnp.int32, (16, BLK), 0)

    def step(i, carry):
        for c in range(2):
            t = i * 2 + c
            tile = jnp.zeros((16, BLK), F32)
            for r in range(RAND):
                b = table[t, r]
                out[t, r * 64 : r * 64 + 64] = x[b, 0:64]
                out[t, 192 + r * 64 : 256 + r * 64] = x[b, 192:256]
                part = ext[b]
                if r:
                    part = pltpu.roll(part, 4 * r, 0)
                tile = tile + part
            out[t, 384:400] = jnp.concatenate([tile, tile], axis=1).astype(BF16)
            pltpu.make_async_copy(out.at[t], dest.at[t], sem.at[t]).start()
        return carry

    lax.fori_loop(0, NB // 2, step, 0)

    def finish(t, carry):
        pltpu.make_async_copy(out.at[t], dest.at[t], sem.at[t]).wait()
        return carry

    lax.fori_loop(0, NB, finish, 0)


def grads(q, g, norm, delta, k, v, keep=None):
    st = nt(k, q) * FACTOR
    pt = jnp.exp(st - norm)
    if keep is not None:
        pt = jnp.where(keep, pt, 0.0)
    dst = (pt * (nt(v, g) - delta)).astype(BF16)
    return tn(dst, k), nn(dst, q), nn(pt.astype(BF16), g)


def two(ext, a):
    return ext[a : a + 1].astype(F32) + ext[a + 1 : a + 2].astype(F32)


def joined(ref, a, first, last):
    return jnp.concatenate([ref[n, a * 64 : (a + 1) * 64] for n in range(first, last)], axis=0)


def pair_delta(x, b):
    e0 = x[b, 256:272].astype(F32)
    e1 = x[b + 1, 256:272].astype(F32)
    return jnp.concatenate([two(e0, 0)[:, 0:64], two(e1, 0)[:, 0:64]], axis=1)


def masked_norms(pos, lse):
    lse_all = lse[...]
    lanes = lax.broadcasted_iota(jnp.int32, lse_all.shape, 1)
    return jnp.where((pos[0] == 0) & (lanes < GLOB * BLK), OFF, lse_all)


def window_body(pos, x, lse, dq_out, dk_out, dv_out, dq, dk, dv, sem):
    lse_all = masked_norms(pos, lse)
    for i in range(NB // 2):
        b = 2 * i
        norm = lse_all[:, i * HD : (i + 1) * HD]
        low, high = max(b - 1, 0), min(b + 3, NB)
        shape = ((high - low) * BLK, HD)
        kb = (lax.broadcasted_iota(jnp.int32, shape, 0) >> 6) + low
        qb = (lax.broadcasted_iota(jnp.int32, shape, 1) >> 6) + b
        keep = jnp.abs(kb - qb) <= 1
        if low < GLOB:
            keep = keep & ((pos[0] > 0) | (kb >= GLOB))
        wq, wk, wv = grads(
            joined(x, 0, b, b + 2),
            joined(x, 3, b, b + 2),
            norm,
            pair_delta(x, b),
            joined(x, 1, low, high),
            joined(x, 2, low, high),
            keep,
        )
        dq[b * 64 : b * 64 + 128] = wq
        for acc, part in ((dk, wk), (dv, wv)):
            old = min(b + 1, NB) * 64 if b else 0
            seen = slice(low * 64, old)
            if b:
                acc[seen] = acc[seen] + part[0 : old - low * 64]
            acc[old : high * 64] = part[old - low * 64 :]
    pushes = [
        pltpu.make_async_copy(src, dst, sem.at[n])
        for n, (src, dst) in enumerate(((dq, dq_out), (dk, dk_out), (dv, dv_out)))
    ]
    for push in pushes:
        push.start()
    for push in pushes:
        push.wait()


def rand_body(table, x, y, dk_out, dv_out, z, dk, dv, buf, sem, acc_sem):
    dk[...] = jnp.zeros_like(dk)
    dv[...] = jnp.zeros_like(dv)
    sub = lax.broadcasted_iota(jnp.int32, (HD, HD), 0)
    lane = lax.broadcasted_iota(jnp.int32, (HD, HD), 1)
    keep = (sub >> 6) == (lane >> 6)
    left = lax.broadcasted_iota(jnp.int32, (1, HD), 1) < 64
    per_step = 4

    def step(i, carry):
        t0 = i * per_step
        exts = [y[t0 + c, 384:400].astype(F32) for c in range(per_step)]
        entries = [(c, r) for c in range(per_step) for r in range(RAND)]
        done = []
        for n in range(0, len(entries), 2):
            pair = entries[n : n + 2]

            def both(base):
                return jnp.concatenate(
                    [y[t0 + c, base + r * 64 : base + r * 64 + 64] for c, r in pair], axis=0
                )

            def row(a):
                one, other = (two(exts[c], 4 * r + a) for c, r in pair)
                return jnp.where(left, one, other)

            js = [table[NB + t0 + c, r] for c, r in pair]
            k = jnp.concatenate([x[j, 64:128] for j in js], axis=0)
            v = jnp.concatenate([x[j, 128:192] for j in js], axis=0)
            pq, pk, pv = grads(both(0), both(192), row(2), row(0), k, v, keep)
            low = (pq * FACTOR).astype(BF16)
            for m, (c, r) in enumerate(pair):
                buf[t0 + c, r * 64 : r * 64 + 64] = low[m * 64 : m * 64 + 64]
            done.append((js, pk, pv))
        for c in range(per_step):
            t = t0 + c
            pltpu.make_async_copy(buf.at[t], z.at[t], sem.at[t]).start()
        for js, pk, pv in done:
            for m, j in enumerate(js):
                span = pl.ds(pl.multiple_of(j * 64, 64), 64)
                dk[span] = dk[span] + pk[m * 64 : m * 64 + 64]
                dv[span] = dv[span] + pv[m * 64 : m * 64 + 64]
        return carry

    lax.fori_loop(0, NB // per_step, step, 0)
    drains = []
    for n in range(4):
        span = pl.ds(n * 256, 256)
        for m, (src, dst) in enumerate(((dk, dk_out), (dv, dv_out))):
            drain = pltpu.make_async_copy(src.at[span], dst.at[span], acc_sem.at[2 * n + m])
            drain.start()
            drains.append(drain)
    for drain in drains:
        drain.wait()

    def finish(t, carry):
        pltpu.make_async_copy(buf.at[t], z.at[t], sem.at[t]).wait()
        return carry

    lax.fori_loop(0, NB, finish, 0)


def global_body(pos, x, lse, glob, halo, dq, dk, dv, gpart, glow, hback):
    here = pos[0]
    lse_all = masked_norms(pos, lse)
    gq, gk, gv, gg = (joined(glob, a, 0, GLOB) for a in range(4))
    ext0 = glob[0, 256:272].astype(F32)
    ext1 = glob[1, 256:272].astype(F32)
    gdelta = jnp.concatenate([two(ext0, 0)[:, 0:64], two(ext1, 0)[:, 0:64]], axis=1)
    gnorm = jnp.concatenate([two(ext0, 2)[:, 0:64], two(ext1, 2)[:, 0:64]], axis=1)
    gq_sum = jnp.zeros((HD, HD), F32)
    gk_sum = jnp.zeros((HD, HD), F32)
    gv_sum = jnp.zeros((HD, HD), F32)
    for i in range(NB // 2):
        b = 2 * i
        span = slice(b * 64, b * 64 + 128)
        q2, k2, v2, g2 = (joined(x, a, b, b + 2) for a in range(4))
        fq, fk, fv = grads(gq, gg, gnorm, gdelta, k2, v2)
        gq_sum = gq_sum + fq
        dk[span] = fk
        dv[span] = fv
        norm = lse_all[:, i * HD : (i + 1) * HD]
        wq, wk, wv = grads(q2, g2, norm, pair_delta(x, b), gk, gv)
        dq[span] = wq
        gk_sum = gk_sum + wk
        gv_sum = gv_sum + wv
    hext = halo[256:272].astype(F32)
    hdelta = two(hext, 0)[:, 0:64]
    hnorm = jnp.where(here == 0, OFF, two(hext, 2)[:, 0:64])
    hq, hk, hv, hg = halo[0:64], halo[64:128], halo[128:192], halo[192:256]
    e0 = x[0, 256:272].astype(F32)
    aq, ak, av = grads(
        x[0, 0:64], x[0, 192:256], lse_all[:, 0:64], two(e0, 0)[:, 0:64], hk, hv
    )
    bq, bk, bv = grads(hq, hg, hnorm, hdelta, x[0, 64:128], x[0, 128:192])
    dq[0:64] = dq[0:64] + aq
    dk[0:64] = dk[0:64] + bk
    dv[0:64] = dv[0:64] + bv
    hback[0:64] = (bq * FACTOR).astype(BF16)
    hback[64:128] = (ak * FACTOR).astype(BF16)
    hback[128:192] = av.astype(BF16)
    for n, total in enumerate((gq_sum * FACTOR, gk_sum * FACTOR, gv_sum)):
        gpart[n] = total
        glow[n] = total.astype(BF16)


def gather_body(
    dq_g, dk_g, dv_g, dq_w, dk_w, dv_w, dk_r, dv_r, w, dq, edge,
    s0, s1, s2, s3, s4, buf, in_sem, out_sem,
):
    held = (s0, s1, s2, s3, s4)
    pulls = [
        pltpu.make_async_copy(src, dst, in_sem.at[n])
        for n, (src, dst) in enumerate(zip((dq_w, dk_w, dv_w, dk_r, dv_r), held))
    ]
    for pull in pulls:
        pull.start()
    for pull in pulls:
        pull.wait()
    dq[...] = dq_g[...] + s0[...]
    pushes = []
    for b in range(NB):
        span = slice(b * 64, b * 64 + 64)
        rk = (dk_g[span] + s1[span] + s3[span]) * FACTOR
        rv = dv_g[span] + s2[span] + s4[span]
        if b in EDGES:
            at = EDGES.index(b) * 128
            edge[at : at + 64] = rk
            edge[at + 64 : at + 128] = rv
            continue
        buf[b, 0:64] = rk.astype(BF16)
        buf[b, 64:128] = rv.astype(BF16)
        push = pltpu.make_async_copy(buf.at[b], w.at[b, pl.ds(64, 128)], out_sem.at[b])
        push.start()
        pushes.append(push)
    for push in pushes:
        push.wait()


def merge_body(pos, table, dq, edge, z, hback, gtot, w_in, w, acc, out, out_edge, sem):
    acc[...] = dq[...] * FACTOR

    def step(t, carry):
        for r in range(RAND):
            b = table[t, r]
            span = pl.ds(pl.multiple_of(b * 64, 64), 64)
            acc[span] = acc[span] + z[t, r * 64 : r * 64 + 64].astype(F32)
        return carry

    lax.fori_loop(0, NB, step, 0)
    home = jnp.where(pos[0] == 0, 1.0, 0.0)
    pushes = []

    def send(src, dst, n):
        push = pltpu.make_async_copy(src, dst, sem.at[n])
        push.start()
        pushes.append(push)

    for n, b in enumerate(EDGES):
        rk, rv = edge[n * 128 : n * 128 + 64], edge[n * 128 + 64 : n * 128 + 128]
        if b < GLOB:
            rk = rk + home * gtot[1, b * 64 : b * 64 + 64]
            rv = rv + home * gtot[2, b * 64 : b * 64 + 64]
        else:
            rk = rk + hback[64:128].astype(F32)
            rv = rv + hback[128:192].astype(F32)
        out_edge[n, 0:64] = rk.astype(BF16)
        out_edge[n, 64:128] = rv.astype(BF16)
        send(out_edge.at[n], w.at[b, pl.ds(64, 128)], NB + n)
    for b in range(NB):
        span = slice(b * 64, b * 64 + 64)
        rq = acc[span]
        if b < GLOB:
            rq = rq + home * gtot[0, span]
        if b == NB - 1:
            rq = rq + hback[0:64].astype(F32)
        out[b] = rq.astype(BF16)
        send(out.at[b], w.at[b, pl.ds(0, 64)], b)
    for push in pushes:
        push.wait()


def unpack_body(w, q, k, v):
    for h in range(HEADS):
        cols = pl.ds(h * HD, HD)
        q[:, cols] = w[h, 0:64]
        k[:, cols] = w[h, 64:128]
        v[:, cols] = w[h, 128:192]


def struct(shape, dtype=BF16):
    return jax.ShapeDtypeStruct(shape, dtype)


def far(shape, dtype=BF16):
    return pltpu.HBM(shape, dtype)


def near(shape, dtype=BF16):
    return pltpu.VMEM(shape, dtype)


def hold(x):
    return pltpu.with_memory_space_constraint(x, pltpu.VMEM)


def keep_far(x):
    return pltpu.with_memory_space_constraint(x, pltpu.HBM)


def exchange(x, axis):
    return lax.all_to_all(x, axis, split_axis=0, concat_axis=0, tiled=True)


def per_device(query, key, value, output, grad_out, logsumexp, rand_blocks):
    position = lax.axis_index("seq")
    pos = position.astype(jnp.int32).reshape(1)
    rows = NB * BLK
    groups = NB
    dma = pltpu.SemaphoreType.DMA
    whole = pltpu.VMEM((BLK, HEADS * HD), BF16)
    packed = call(
        pack_body,
        far((HEADS, SLAB, HD)),
        [HB] * 5,
        HB,
        nbytes=5 << 18,
        scratch=[whole] * 5 + [pltpu.VMEM((HEADS, SLAB, HD), BF16), dma((5,)), dma((HEADS,))],
    )(*map(keep_far, (query, key, value, output, grad_out)))
    x = exchange(packed, "head")
    table = call(table_body, struct((2 * NB, HD), jnp.int32), [SM, VM], VM, nbytes=1 << 14)(
        pos, rand_blocks.reshape(NB, NB * RAND)
    )
    y, halo, glob = call(
        select_body,
        (far((NB, PAIR, HD)), struct((SLAB, HD)), struct((GLOB, SLAB, HD))),
        [SM, SM, VM, VM],
        (HB, VM, VM),
        nbytes=3 << 20,
        scratch=[
            pltpu.VMEM((NB, 16, BLK), F32),
            pltpu.VMEM((NB, PAIR, HD), BF16),
            dma((NB,)),
        ],
    )(pos, table, x, logsumexp)
    y = exchange(y, "seq")
    halo = lax.ppermute(halo, "seq", [(s, s + 1) for s in range(groups - 1)])

    def spread(glob, reach):
        starts = range(0, groups, 4 * reach)
        source = glob
        for n in (1, 2, 3):
            glob = glob + lax.ppermute(source, "seq", [(s, s + n * reach) for s in starts])
        return glob

    glob = spread(glob, 4)
    grid = pltpu.VMEM((rows, HD), F32)
    far_acc = far((rows, HD), F32)
    acc = near((rows, HD), F32)
    dq_w, dk_w, dv_w = call(
        window_body,
        (far_acc,) * 3,
        [SM, VM, VM],
        (HB,) * 3,
        flops=1 << 29,
        nbytes=2 << 20,
        scratch=[grid] * 3 + [dma((3,))],
    )(pos, x, logsumexp)
    glob, halo, y, dq_w = lax.optimization_barrier((glob, halo, y, dq_w))
    glob = spread(glob, 1)
    dk_r, dv_r, z = call(
        rand_body,
        (far_acc, far_acc, far((NB, RAND * BLK, HD))),
        [SM, VM, VM],
        (HB,) * 3,
        flops=1 << 29,
        nbytes=4 << 20,
        scratch=[grid, grid, pltpu.VMEM((NB, RAND * BLK, HD), BF16), dma((NB,)), dma((8,))],
    )(table, x, y)
    glob, z = lax.optimization_barrier((glob, z))
    z = exchange(z, "seq")
    dq_g, dk_g, dv_g, gpart, glow, hback = call(
        global_body,
        (acc,) * 3 + (struct((3, HD, HD), F32), struct((3, HD, HD)), struct((3 * BLK, HD))),
        [SM] + [VM] * 4,
        (VM,) * 6,
        flops=1 << 29,
        nbytes=4 << 20,
    )(pos, x, logsumexp, glob, halo)
    hback = lax.ppermute(hback, "seq", [(s, s - 1) for s in range(1, groups)])
    for reach in (1, 4):
        span = range(0, groups, 4) if reach == 1 else (0,)
        for n in (1, 2, 3):
            moved = lax.ppermute(glow, "seq", [(s + n * reach, s) for s in span])
            gpart = gpart + moved.astype(F32)
        glow = gpart.astype(BF16)
    w, dq, edge = call(
        gather_body,
        (far((NB, 3 * BLK, HD)), acc, struct((len(EDGES) * 2 * BLK, HD), F32)),
        [VM] * 3 + [HB] * 5,
        (HB, VM, VM),
        flops=1 << 24,
        nbytes=4 << 20,
        scratch=[grid] * 5 + [pltpu.VMEM((NB, 2 * BLK, HD), BF16), dma((5,)), dma((NB,))],
    )(*map(hold, (dq_g, dk_g, dv_g)), *map(keep_far, (dq_w, dk_w, dv_w, dk_r, dv_r)))
    w = call(
        merge_body,
        far((NB, 3 * BLK, HD)),
        [SM, SM] + [VM] * 5 + [HB],
        HB,
        nbytes=4 << 20,
        scratch=[
            grid,
            pltpu.VMEM((NB, BLK, HD), BF16),
            pltpu.VMEM((len(EDGES), 2 * BLK, HD), BF16),
            dma((NB + len(EDGES),)),
        ],
        aliases={7: 0},
    )(pos, table, hold(dq), edge, z, hback, gpart, w)
    w = exchange(w, "head")
    shape = struct((BLK, HEADS * HD))
    return call(unpack_body, (shape, shape, shape), [VM], (VM,) * 3, nbytes=3 << 19)(w)


def solution(mesh):
    in_specs = (
        P(("seq", "head"), None),
        P(("seq", "head"), None),
        P(("seq", "head"), None),
        P(("seq", "head"), None),
        P(("seq", "head"), None),
        P("head", "seq"),
        P(),
    )
    out_specs = (P(("seq", "head"), None), P(("seq", "head"), None), P(("seq", "head"), None))
    return jax.shard_map(
        per_device, mesh=mesh, in_specs=in_specs, out_specs=out_specs, check_vma=False
    )
```

```python
import jax
import jax.numpy as jnp
from jax import lax
from jax.experimental import pallas as pl
from jax.experimental.pallas import tpu as pltpu
from jax.sharding import PartitionSpec as P

HEADS = 16
HD = 128
BLK = 64
GLOB = 2
RAND = 3
NB = 16
FACTOR = HD ** (-0.5)
OFF = 1e30
EDGES = (0, 1, NB - 1)
SLAB = 4 * BLK + 16
PAIR = RAND * 2 * BLK + 16
F32 = jnp.float32
BF16 = jnp.bfloat16

HB = pl.BlockSpec(memory_space=pltpu.HBM)
VM = pl.BlockSpec(memory_space=pltpu.VMEM)
SM = pl.BlockSpec(memory_space=pltpu.SMEM)


def call(body, outs, in_specs, out_specs, flops=0, nbytes=0, scratch=(), aliases={}, limit=8):
    return pl.pallas_call(
        body,
        out_shape=outs,
        in_specs=in_specs,
        out_specs=out_specs,
        scratch_shapes=list(scratch),
        input_output_aliases=aliases,
        compiler_params=pltpu.CompilerParams(vmem_limit_bytes=limit << 20),
        cost_estimate=pl.CostEstimate(flops=flops, bytes_accessed=nbytes, transcendentals=0),
    )


def nt(a, b):
    return lax.dot_general(a, b, (((1,), (1,)), ((), ())), preferred_element_type=F32)


def nn(a, b):
    return lax.dot_general(a, b, (((1,), (0,)), ((), ())), preferred_element_type=F32)


def tn(a, b):
    return lax.dot_general(a, b, (((0,), (0,)), ((), ())), preferred_element_type=F32)


def pieces(x):
    high = x.astype(BF16).astype(F32)
    return high, (x - high).astype(BF16).astype(F32)


def pack_body(q, k, v, o, g, out, qs, ks, vs, os, gs, ps, in_sem, out_sem):
    pulls = [
        pltpu.make_async_copy(src, dst, in_sem.at[i])
        for i, (src, dst) in enumerate(zip((o, g, q, k, v), (os, gs, qs, ks, vs)))
    ]
    for pull in pulls:
        pull.start()
    lane = lax.broadcasted_iota(jnp.int32, (BLK, HD), 1)
    row = lax.broadcasted_iota(jnp.int32, (16, HD), 0)
    deltas = jnp.zeros((BLK, HD), F32)
    pulls[0].wait()
    pulls[1].wait()
    for h in range(HEADS):
        cols = pl.ds(h * HD, HD)
        gh = gs[:, cols]
        ps[h, 192:256] = gh
        part = jnp.sum(gh.astype(F32) * os[:, cols].astype(F32), axis=1, keepdims=True)
        deltas = jnp.where(lane == h, part, deltas)
    turned = jnp.transpose(jnp.concatenate([deltas, jnp.zeros((BLK, HD), F32)], axis=0))
    high, low = pieces(turned)
    for pull in pulls[2:]:
        pull.wait()
    pushes = []
    for h in range(HEADS):
        cols = pl.ds(h * HD, HD)
        ps[h, 0:64] = qs[:, cols]
        ps[h, 64:128] = ks[:, cols]
        ps[h, 128:192] = vs[:, cols]
        tile = jnp.where(row == 0, high[h : h + 1], jnp.where(row == 1, low[h : h + 1], 0.0))
        ps[h, 256:272] = tile.astype(BF16)
        push = pltpu.make_async_copy(ps.at[h], out.at[h], out_sem.at[h])
        push.start()
        pushes.append(push)
    for push in pushes:
        push.wait()


def table_body(pos, entries, out):
    here = pos[0]
    e = entries[...]
    width = e.shape[1]
    lane = lax.broadcasted_iota(jnp.int32, (NB, width), 1)
    row = lax.broadcasted_iota(jnp.int32, (NB, width), 0)
    mine = jnp.sum(jnp.where(row == here, e, 0), axis=0, keepdims=True)
    to_group = jnp.broadcast_to(mine, (NB, width)) >> 4
    hit = jnp.concatenate(
        [jnp.where(to_group == row, 1.0, 0.0), jnp.where((e >> 4) == here, 1.0, 0.0)], axis=0
    )
    value = jnp.concatenate([(lane * 171) >> 9, e & 15], axis=0)
    ii = lax.broadcasted_iota(jnp.int32, (width, width), 0)
    jj = lax.broadcasted_iota(jnp.int32, (width, width), 1)
    before = jnp.where(ii < jj, 1.0, 0.0).astype(BF16)
    rank = nn(hit.astype(BF16), before)
    out_lane = lax.broadcasted_iota(jnp.int32, (2 * NB, HD), 1)
    result = jnp.zeros((2 * NB, HD), jnp.int32)
    for r in range(RAND):
        chosen = jnp.where((hit > 0.5) & (jnp.abs(rank - r) < 0.5), value, 0)
        total = jnp.sum(chosen, axis=1, keepdims=True)
        result = jnp.where(out_lane == r, total, result)
    out[...] = result


def norm_rows(lse, b):
    pair = lse[:, (b // 2) * HD : (b // 2 + 1) * HD]
    return pair[:, 64:128] if b % 2 else pair[:, 0:64]


def select_body(pos, table, x, lse, dest, halo, glob, ext, out, sem):
    row = lax.broadcasted_iota(jnp.int32, (16, BLK), 0)
    lse_all = lse[...]

    def ext_of(b, norm):
        high, low = pieces(norm)
        tile = jnp.where(row == 2, high, jnp.where(row == 3, low, 0.0))
        return x[b, 256:272, 0:64].astype(F32) + tile

    for b in range(NB):
        norm = norm_rows(lse_all, b)
        if b < GLOB:
            plain = ext_of(b, norm)
            full = jnp.concatenate([plain, plain], axis=1).astype(BF16)
            keep = pos[0] == 0
            glob[b, 0:256] = jnp.where(keep, x[b, 0:256], jnp.zeros((256, HD), BF16))
            glob[b, 256:272] = jnp.where(keep, full, jnp.zeros((16, HD), BF16))
            norm = jnp.where(pos[0] == 0, OFF, norm)
        ext[b] = ext_of(b, norm)
        if b == NB - 1:
            halo[0:256] = x[b, 0:256]
            halo[256:272] = jnp.concatenate([ext[b], ext[b]], axis=1).astype(BF16)

    rows16 = lax.broadcasted_iota(jnp.int32, (16, BLK), 0)

    def step(i, carry):
        for c in range(2):
            t = i * 2 + c
            tile = jnp.zeros((16, BLK), F32)
            for r in range(RAND):
                b = table[t, r]
                out[t, r * 64 : r * 64 + 64] = x[b, 0:64]
                out[t, 192 + r * 64 : 256 + r * 64] = x[b, 192:256]
                part = ext[b]
                if r:
                    part = pltpu.roll(part, 4 * r, 0)
                tile = tile + part
            out[t, 384:400] = jnp.concatenate([tile, tile], axis=1).astype(BF16)
            pltpu.make_async_copy(out.at[t], dest.at[t], sem.at[t]).start()
        return carry

    lax.fori_loop(0, NB // 2, step, 0)

    def finish(t, carry):
        pltpu.make_async_copy(out.at[t], dest.at[t], sem.at[t]).wait()
        return carry

    lax.fori_loop(0, NB, finish, 0)


def grads(q, g, norm, delta, k, v, keep=None):
    st = nt(k, q) * FACTOR
    pt = jnp.exp(st - norm)
    if keep is not None:
        pt = jnp.where(keep, pt, 0.0)
    dst = (pt * (nt(v, g) - delta)).astype(BF16)
    return tn(dst, k), nn(dst, q), nn(pt.astype(BF16), g)


def staged(tiles, scores, probs, lows):
    depth = 3
    held = {}
    for step in range(len(tiles) + 2):
        if step < len(tiles):
            tile = tiles[step]()
            held[step] = tile
            shape = (tile["k"].shape[0], tile["q"].shape[0])
            slot = step % depth
            view = (slot, slice(0, shape[0]), slice(0, shape[1]))
            scores[view] = nt(tile["k"], tile["q"])
            probs[view] = nt(tile["v"], tile["g"])
        n = step - 1
        if 0 <= n < len(tiles):
            tile = held[n]
            shape = (tile["k"].shape[0], tile["q"].shape[0])
            view = (n % depth, slice(0, shape[0]), slice(0, shape[1]))
            pt = jnp.exp(scores[view] * FACTOR - tile["norm"])
            if tile.get("keep") is not None:
                pt = jnp.where(tile["keep"], pt, 0.0)
            low_view = (n % depth, 0) + view[1:]
            lows[low_view] = pt.astype(BF16)
            low_view = (n % depth, 1) + view[1:]
            lows[low_view] = (pt * (probs[view] - tile["delta"])).astype(BF16)
        n = step - 2
        if 0 <= n < len(tiles):
            tile = held.pop(n)
            shape = (tile["k"].shape[0], tile["q"].shape[0])
            cut = (slice(0, shape[0]), slice(0, shape[1]))
            pt = lows[(n % depth, 0) + cut]
            dst = lows[(n % depth, 1) + cut]
            tile["use"](tn(dst, tile["k"]), nn(dst, tile["q"]), nn(pt, tile["g"]))


def two(ext, a):
    return ext[a : a + 1].astype(F32) + ext[a + 1 : a + 2].astype(F32)


def joined(ref, a, first, last):
    return jnp.concatenate([ref[n, a * 64 : (a + 1) * 64] for n in range(first, last)], axis=0)


def pair_delta(x, b):
    e0 = x[b, 256:272].astype(F32)
    e1 = x[b + 1, 256:272].astype(F32)
    return jnp.concatenate([two(e0, 0)[:, 0:64], two(e1, 0)[:, 0:64]], axis=1)


def masked_norms(pos, lse):
    lse_all = lse[...]
    lanes = lax.broadcasted_iota(jnp.int32, lse_all.shape, 1)
    return jnp.where((pos[0] == 0) & (lanes < GLOB * BLK), OFF, lse_all)


def window_body(pos, x, lse, dq_out, dk_out, dv_out, dq, dk, dv, sem):
    lse_all = masked_norms(pos, lse)
    for i in range(NB // 2):
        b = 2 * i
        norm = lse_all[:, i * HD : (i + 1) * HD]
        low, high = max(b - 1, 0), min(b + 3, NB)
        shape = ((high - low) * BLK, HD)
        kb = (lax.broadcasted_iota(jnp.int32, shape, 0) >> 6) + low
        qb = (lax.broadcasted_iota(jnp.int32, shape, 1) >> 6) + b
        keep = jnp.abs(kb - qb) <= 1
        if low < GLOB:
            keep = keep & ((pos[0] > 0) | (kb >= GLOB))
        wq, wk, wv = grads(
            joined(x, 0, b, b + 2),
            joined(x, 3, b, b + 2),
            norm,
            pair_delta(x, b),
            joined(x, 1, low, high),
            joined(x, 2, low, high),
            keep,
        )
        dq[b * 64 : b * 64 + 128] = wq
        for acc, part in ((dk, wk), (dv, wv)):
            old = min(b + 1, NB) * 64 if b else 0
            seen = slice(low * 64, old)
            if b:
                acc[seen] = acc[seen] + part[0 : old - low * 64]
            acc[old : high * 64] = part[old - low * 64 :]
    pushes = [
        pltpu.make_async_copy(src, dst, sem.at[n])
        for n, (src, dst) in enumerate(((dq, dq_out), (dk, dk_out), (dv, dv_out)))
    ]
    for push in pushes:
        push.start()
    for push in pushes:
        push.wait()


def rand_body(table, x, y, dk_out, dv_out, z, dk, dv, buf, sem, acc_sem, scores, probs, lows):
    dk[...] = jnp.zeros_like(dk)
    dv[...] = jnp.zeros_like(dv)
    sub = lax.broadcasted_iota(jnp.int32, (HD, HD), 0)
    lane = lax.broadcasted_iota(jnp.int32, (HD, HD), 1)
    keep = (sub >> 6) == (lane >> 6)
    left = lax.broadcasted_iota(jnp.int32, (1, HD), 1) < 64
    entries = [(t, r) for t in range(NB) for r in range(RAND)]

    def tile_of(n):
        pair = entries[2 * n : 2 * n + 2]

        def make():
            def both(base):
                return jnp.concatenate(
                    [y[t, base + r * 64 : base + r * 64 + 64] for t, r in pair], axis=0
                )

            def row(a):
                one, other = (two(y[t, 384:400].astype(F32), 4 * r + a) for t, r in pair)
                return jnp.where(left, one, other)

            js = [table[NB + t, r] for t, r in pair]

            def use(pq, pk, pv):
                low = (pq * FACTOR).astype(BF16)
                for m, (t, r) in enumerate(pair):
                    rows = slice(m * 64, m * 64 + 64)
                    buf[t, r * 64 : r * 64 + 64] = low[rows]
                    span = pl.ds(pl.multiple_of(js[m] * 64, 64), 64)
                    dk[span] = dk[span] + pk[rows]
                    dv[span] = dv[span] + pv[rows]
                    if r == RAND - 1:
                        pltpu.make_async_copy(buf.at[t], z.at[t], sem.at[t]).start()

            return dict(
                q=both(0),
                g=both(192),
                k=jnp.concatenate([x[j, 64:128] for j in js], axis=0),
                v=jnp.concatenate([x[j, 128:192] for j in js], axis=0),
                norm=row(2),
                delta=row(0),
                keep=keep,
                use=use,
            )

        return make

    staged([tile_of(n) for n in range(len(entries) // 2)], scores, probs, lows)
    drains = []
    for n in range(4):
        span = pl.ds(n * 256, 256)
        for m, (src, dst) in enumerate(((dk, dk_out), (dv, dv_out))):
            drain = pltpu.make_async_copy(src.at[span], dst.at[span], acc_sem.at[2 * n + m])
            drain.start()
            drains.append(drain)
    for drain in drains:
        drain.wait()

    def finish(t, carry):
        pltpu.make_async_copy(buf.at[t], z.at[t], sem.at[t]).wait()
        return carry

    lax.fori_loop(0, NB, finish, 0)


def global_body(
    pos, x, lse, glob, halo, dq, dk, dv, gpart, glow, hback, sums, scores, probs, lows
):
    here = pos[0]
    lse_all = masked_norms(pos, lse)
    gq, gk, gv, gg = (joined(glob, a, 0, GLOB) for a in range(4))
    ext0 = glob[0, 256:272].astype(F32)
    ext1 = glob[1, 256:272].astype(F32)
    gdelta = jnp.concatenate([two(ext0, 0)[:, 0:64], two(ext1, 0)[:, 0:64]], axis=1)
    gnorm = jnp.concatenate([two(ext0, 2)[:, 0:64], two(ext1, 2)[:, 0:64]], axis=1)
    sums[...] = jnp.zeros_like(sums)
    tiles = []
    for i in range(4):
        b = 4 * i
        span = slice(b * 64, b * 64 + 256)

        def down(b=b, span=span):
            def use(fq, fk, fv):
                sums[0] = sums[0] + fq
                dk[span] = fk
                dv[span] = fv

            return dict(
                q=gq,
                g=gg,
                k=joined(x, 1, b, b + 4),
                v=joined(x, 2, b, b + 4),
                norm=gnorm,
                delta=gdelta,
                use=use,
            )

        def across(b=b, span=span):
            def use(wq, wk, wv):
                dq[span] = wq
                sums[1] = sums[1] + wk
                sums[2] = sums[2] + wv

            return dict(
                q=joined(x, 0, b, b + 4),
                g=joined(x, 3, b, b + 4),
                k=gk,
                v=gv,
                norm=lse_all[:, span],
                delta=jnp.concatenate([pair_delta(x, b), pair_delta(x, b + 2)], axis=1),
                use=use,
            )

        tiles += [down, across]
    staged(tiles, scores, probs, lows)
    gq_sum, gk_sum, gv_sum = sums[0], sums[1], sums[2]
    hext = halo[256:272].astype(F32)
    hdelta = two(hext, 0)[:, 0:64]
    hnorm = jnp.where(here == 0, OFF, two(hext, 2)[:, 0:64])
    hq, hk, hv, hg = halo[0:64], halo[64:128], halo[128:192], halo[192:256]
    e0 = x[0, 256:272].astype(F32)
    aq, ak, av = grads(
        x[0, 0:64], x[0, 192:256], lse_all[:, 0:64], two(e0, 0)[:, 0:64], hk, hv
    )
    bq, bk, bv = grads(hq, hg, hnorm, hdelta, x[0, 64:128], x[0, 128:192])
    dq[0:64] = dq[0:64] + aq
    dk[0:64] = dk[0:64] + bk
    dv[0:64] = dv[0:64] + bv
    hback[0:64] = (bq * FACTOR).astype(BF16)
    hback[64:128] = (ak * FACTOR).astype(BF16)
    hback[128:192] = av.astype(BF16)
    for n, total in enumerate((gq_sum * FACTOR, gk_sum * FACTOR, gv_sum)):
        gpart[n] = total
        glow[n] = total.astype(BF16)


def gather_body(
    dq_g, dk_g, dv_g, dq_w, dk_w, dv_w, dk_r, dv_r, w, dq, edge,
    s0, s1, s2, s3, s4, buf, in_sem, out_sem,
):
    held = (s0, s1, s2, s3, s4)
    pulls = [
        pltpu.make_async_copy(src, dst, in_sem.at[n])
        for n, (src, dst) in enumerate(zip((dq_w, dk_w, dv_w, dk_r, dv_r), held))
    ]
    for pull in pulls:
        pull.start()
    for pull in pulls:
        pull.wait()
    dq[...] = dq_g[...] + s0[...]
    pushes = []
    for b in range(NB):
        span = slice(b * 64, b * 64 + 64)
        rk = (dk_g[span] + s1[span] + s3[span]) * FACTOR
        rv = dv_g[span] + s2[span] + s4[span]
        if b in EDGES:
            at = EDGES.index(b) * 128
            edge[at : at + 64] = rk
            edge[at + 64 : at + 128] = rv
            continue
        buf[b, 0:64] = rk.astype(BF16)
        buf[b, 64:128] = rv.astype(BF16)
        push = pltpu.make_async_copy(buf.at[b], w.at[b, pl.ds(64, 128)], out_sem.at[b])
        push.start()
        pushes.append(push)
    for push in pushes:
        push.wait()


def merge_body(pos, table, dq, edge, z, hback, gtot, w_in, w, acc, out, out_edge, sem):
    acc[...] = dq[...] * FACTOR

    def step(t, carry):
        for r in range(RAND):
            b = table[t, r]
            span = pl.ds(pl.multiple_of(b * 64, 64), 64)
            acc[span] = acc[span] + z[t, r * 64 : r * 64 + 64].astype(F32)
        return carry

    lax.fori_loop(0, NB, step, 0)
    home = jnp.where(pos[0] == 0, 1.0, 0.0)
    pushes = []

    def send(src, dst, n):
        push = pltpu.make_async_copy(src, dst, sem.at[n])
        push.start()
        pushes.append(push)

    for n, b in enumerate(EDGES):
        rk, rv = edge[n * 128 : n * 128 + 64], edge[n * 128 + 64 : n * 128 + 128]
        if b < GLOB:
            rk = rk + home * gtot[1, b * 64 : b * 64 + 64]
            rv = rv + home * gtot[2, b * 64 : b * 64 + 64]
        else:
            rk = rk + hback[64:128].astype(F32)
            rv = rv + hback[128:192].astype(F32)
        out_edge[n, 0:64] = rk.astype(BF16)
        out_edge[n, 64:128] = rv.astype(BF16)
        send(out_edge.at[n], w.at[b, pl.ds(64, 128)], NB + n)
    for b in range(NB):
        span = slice(b * 64, b * 64 + 64)
        rq = acc[span]
        if b < GLOB:
            rq = rq + home * gtot[0, span]
        if b == NB - 1:
            rq = rq + hback[0:64].astype(F32)
        out[b] = rq.astype(BF16)
        send(out.at[b], w.at[b, pl.ds(0, 64)], b)
    for push in pushes:
        push.wait()


def unpack_body(w, q, k, v):
    for h in range(HEADS):
        cols = pl.ds(h * HD, HD)
        q[:, cols] = w[h, 0:64]
        k[:, cols] = w[h, 64:128]
        v[:, cols] = w[h, 128:192]


def struct(shape, dtype=BF16):
    return jax.ShapeDtypeStruct(shape, dtype)


def far(shape, dtype=BF16):
    return pltpu.HBM(shape, dtype)


def near(shape, dtype=BF16):
    return pltpu.VMEM(shape, dtype)


def hold(x):
    return pltpu.with_memory_space_constraint(x, pltpu.VMEM)


def keep_far(x):
    return pltpu.with_memory_space_constraint(x, pltpu.HBM)


def exchange(x, axis):
    return lax.all_to_all(x, axis, split_axis=0, concat_axis=0, tiled=True)


def per_device(query, key, value, output, grad_out, logsumexp, rand_blocks):
    position = lax.axis_index("seq")
    pos = position.astype(jnp.int32).reshape(1)
    rows = NB * BLK
    groups = NB
    dma = pltpu.SemaphoreType.DMA
    whole = pltpu.VMEM((BLK, HEADS * HD), BF16)
    packed = call(
        pack_body,
        far((HEADS, SLAB, HD)),
        [HB] * 5,
        HB,
        nbytes=5 << 18,
        scratch=[whole] * 5 + [pltpu.VMEM((HEADS, SLAB, HD), BF16), dma((5,)), dma((HEADS,))],
    )(*map(keep_far, (query, key, value, output, grad_out)))
    x = exchange(packed, "head")
    table = call(table_body, struct((2 * NB, HD), jnp.int32), [SM, VM], VM, nbytes=1 << 14)(
        pos, rand_blocks.reshape(NB, NB * RAND)
    )
    y, halo, glob = call(
        select_body,
        (far((NB, PAIR, HD)), struct((SLAB, HD)), struct((GLOB, SLAB, HD))),
        [SM, SM, VM, VM],
        (HB, VM, VM),
        nbytes=3 << 20,
        scratch=[
            pltpu.VMEM((NB, 16, BLK), F32),
            pltpu.VMEM((NB, PAIR, HD), BF16),
            dma((NB,)),
        ],
    )(pos, table, x, logsumexp)
    y = exchange(y, "seq")
    halo = lax.ppermute(halo, "seq", [(s, s + 1) for s in range(groups - 1)])

    def spread(glob, reach):
        starts = range(0, groups, 4 * reach)
        source = glob
        for n in (1, 2, 3):
            glob = glob + lax.ppermute(source, "seq", [(s, s + n * reach) for s in starts])
        return glob

    glob = spread(glob, 4)
    grid = pltpu.VMEM((rows, HD), F32)
    far_acc = far((rows, HD), F32)
    acc = near((rows, HD), F32)
    dq_w, dk_w, dv_w = call(
        window_body,
        (far_acc,) * 3,
        [SM, VM, VM],
        (HB,) * 3,
        flops=1 << 29,
        nbytes=2 << 20,
        scratch=[grid] * 3 + [dma((3,))],
    )(pos, x, logsumexp)
    glob, halo, y, dq_w = lax.optimization_barrier((glob, halo, y, dq_w))
    glob = spread(glob, 1)
    dk_r, dv_r, z = call(
        rand_body,
        (far_acc, far_acc, far((NB, RAND * BLK, HD))),
        [SM, VM, VM],
        (HB,) * 3,
        flops=1 << 29,
        nbytes=4 << 20,
        scratch=[
            grid,
            grid,
            pltpu.VMEM((NB, RAND * BLK, HD), BF16),
            dma((NB,)),
            dma((8,)),
            pltpu.VMEM((3, HD, HD), F32),
            pltpu.VMEM((3, HD, HD), F32),
            pltpu.VMEM((3, 2, HD, HD), BF16),
        ],
    )(table, x, y)
    glob, z = lax.optimization_barrier((glob, z))
    z = exchange(z, "seq")
    dq_g, dk_g, dv_g, gpart, glow, hback = call(
        global_body,
        (acc,) * 3 + (struct((3, HD, HD), F32), struct((3, HD, HD)), struct((3 * BLK, HD))),
        [SM] + [VM] * 4,
        (VM,) * 6,
        flops=1 << 29,
        nbytes=4 << 20,
        scratch=[
            pltpu.VMEM((3, HD, HD), F32),
            pltpu.VMEM((3, 256, 256), F32),
            pltpu.VMEM((3, 256, 256), F32),
            pltpu.VMEM((3, 2, 256, 256), BF16),
        ],
    )(pos, x, logsumexp, glob, halo)
    hback = lax.ppermute(hback, "seq", [(s, s - 1) for s in range(1, groups)])

    def collect(gpart, glow, reach):
        span = range(0, groups, 4 * reach)
        for n in (1, 2, 3):
            moved = lax.ppermute(glow, "seq", [(s + n * reach, s) for s in span])
            gpart = gpart + moved.astype(F32)
        return gpart

    gpart = collect(gpart, glow, 1)
    w, dq, edge = call(
        gather_body,
        (far((NB, 3 * BLK, HD)), acc, struct((len(EDGES) * 2 * BLK, HD), F32)),
        [VM] * 3 + [HB] * 5,
        (HB, VM, VM),
        flops=1 << 24,
        nbytes=4 << 20,
        scratch=[grid] * 5 + [pltpu.VMEM((NB, 2 * BLK, HD), BF16), dma((5,)), dma((NB,))],
    )(*map(hold, (dq_g, dk_g, dv_g)), *map(keep_far, (dq_w, dk_w, dv_w, dk_r, dv_r)))
    gpart, w, dq, edge, hback = lax.optimization_barrier((gpart, w, dq, edge, hback))
    gpart = collect(gpart, gpart.astype(BF16), 4)
    w = call(
        merge_body,
        far((NB, 3 * BLK, HD)),
        [SM, SM] + [VM] * 5 + [HB],
        HB,
        nbytes=4 << 20,
        scratch=[
            grid,
            pltpu.VMEM((NB, BLK, HD), BF16),
            pltpu.VMEM((len(EDGES), 2 * BLK, HD), BF16),
            dma((NB + len(EDGES),)),
        ],
        aliases={7: 0},
    )(pos, table, hold(dq), edge, z, hback, gpart, w)
    w = exchange(w, "head")
    shape = struct((BLK, HEADS * HD))
    return call(unpack_body, (shape, shape, shape), [VM], (VM,) * 3, nbytes=3 << 19)(w)


def solution(mesh):
    in_specs = (
        P(("seq", "head"), None),
        P(("seq", "head"), None),
        P(("seq", "head"), None),
        P(("seq", "head"), None),
        P(("seq", "head"), None),
        P("head", "seq"),
        P(),
    )
    out_specs = (P(("seq", "head"), None), P(("seq", "head"), None), P(("seq", "head"), None))
    return jax.shard_map(
        per_device, mesh=mesh, in_specs=in_specs, out_specs=out_specs, check_vma=False
    )
```

```python
import jax
import jax.numpy as jnp
from jax import lax
from jax.experimental import pallas as pl
from jax.experimental.pallas import tpu as pltpu
from jax.sharding import PartitionSpec as P

HEADS = 16
HD = 128
BLK = 64
GLOB = 2
RAND = 3
NB = 16
FACTOR = HD ** (-0.5)
OFF = 1e30
EDGES = (0, 1)
SLAB = 4 * BLK + 8
PAIR = RAND * 2 * BLK + 8
F32 = jnp.float32
BF16 = jnp.bfloat16

HB = pl.BlockSpec(memory_space=pltpu.HBM)
VM = pl.BlockSpec(memory_space=pltpu.VMEM)
SM = pl.BlockSpec(memory_space=pltpu.SMEM)


def call(body, outs, in_specs, out_specs, flops=0, nbytes=0, scratch=(), aliases={}, limit=8):
    return pl.pallas_call(
        body,
        out_shape=outs,
        in_specs=in_specs,
        out_specs=out_specs,
        scratch_shapes=list(scratch),
        input_output_aliases=aliases,
        compiler_params=pltpu.CompilerParams(vmem_limit_bytes=limit << 20),
        cost_estimate=pl.CostEstimate(flops=flops, bytes_accessed=nbytes, transcendentals=0),
    )


def nt(a, b):
    return lax.dot_general(a, b, (((1,), (1,)), ((), ())), preferred_element_type=F32)


def nn(a, b):
    return lax.dot_general(a, b, (((1,), (0,)), ((), ())), preferred_element_type=F32)


def tn(a, b):
    return lax.dot_general(a, b, (((0,), (0,)), ((), ())), preferred_element_type=F32)


def pieces(x):
    high = x.astype(BF16).astype(F32)
    return high, (x - high).astype(BF16).astype(F32)


def pack_body(q, k, v, o, g, out, qs, ks, vs, os, gs, ps, in_sem, out_sem):
    pulls = [
        pltpu.make_async_copy(src, dst, in_sem.at[i])
        for i, (src, dst) in enumerate(zip((o, g, q, k, v), (os, gs, qs, ks, vs)))
    ]
    for pull in pulls:
        pull.start()
    lane = lax.broadcasted_iota(jnp.int32, (BLK, HD), 1)
    row = lax.broadcasted_iota(jnp.int32, (8, HD), 0)
    deltas = jnp.zeros((BLK, HD), F32)
    pulls[0].wait()
    pulls[1].wait()
    for h in range(HEADS):
        cols = pl.ds(h * HD, HD)
        gh = gs[:, cols]
        ps[h, 192:256] = gh
        part = jnp.sum(gh.astype(F32) * os[:, cols].astype(F32), axis=1, keepdims=True)
        deltas = jnp.where(lane == h, part, deltas)
    turned = jnp.transpose(jnp.concatenate([deltas, jnp.zeros((BLK, HD), F32)], axis=0))
    high, low = pieces(turned)
    for pull in pulls[2:]:
        pull.wait()
    pushes = []
    for h in range(HEADS):
        cols = pl.ds(h * HD, HD)
        ps[h, 0:64] = qs[:, cols]
        ps[h, 64:128] = ks[:, cols]
        ps[h, 128:192] = vs[:, cols]
        tile = jnp.where(row == 0, high[h : h + 1], jnp.where(row == 1, low[h : h + 1], 0.0))
        ps[h, 256:264] = tile.astype(BF16)
        push = pltpu.make_async_copy(ps.at[h], out.at[h], out_sem.at[h])
        push.start()
        pushes.append(push)
    for push in pushes:
        push.wait()


def table_body(pos, entries, out):
    here = pos[0]
    e = entries[...]
    width = e.shape[1]
    lane = lax.broadcasted_iota(jnp.int32, (NB, width), 1)
    row = lax.broadcasted_iota(jnp.int32, (NB, width), 0)
    mine = jnp.sum(jnp.where(row == here, e, 0), axis=0, keepdims=True)
    to_group = jnp.broadcast_to(mine, (NB, width)) >> 4
    hit = jnp.concatenate(
        [jnp.where(to_group == row, 1.0, 0.0), jnp.where((e >> 4) == here, 1.0, 0.0)], axis=0
    )
    value = jnp.concatenate([(lane * 171) >> 9, e & 15], axis=0)
    ii = lax.broadcasted_iota(jnp.int32, (width, width), 0)
    jj = lax.broadcasted_iota(jnp.int32, (width, width), 1)
    before = jnp.where(ii < jj, 1.0, 0.0).astype(BF16)
    rank = nn(hit.astype(BF16), before)
    out_lane = lax.broadcasted_iota(jnp.int32, (2 * NB, HD), 1)
    result = jnp.zeros((2 * NB, HD), jnp.int32)
    for r in range(RAND):
        chosen = jnp.where((hit > 0.5) & (jnp.abs(rank - r) < 0.5), value, 0)
        total = jnp.sum(chosen, axis=1, keepdims=True)
        result = jnp.where(out_lane == r, total, result)
    out[...] = result


def left_half():
    return lax.broadcasted_iota(jnp.int32, (1, HD), 1) < BLK


def low_pair(one, other):
    return jnp.where(left_half(), one, pltpu.roll(other, BLK, 1))


def high_pair(one, other):
    return jnp.where(left_half(), pltpu.roll(one, BLK, 1), other)


def norm_rows(lse, b):
    pair = lse[:, (b // 2) * HD : (b // 2 + 1) * HD]
    return pair if b % 2 else pltpu.roll(pair, BLK, 1)


def select_body(pos, table, x, lse, dest, last, first, glob, ext, out, sem):
    row = lax.broadcasted_iota(jnp.int32, (8, HD), 0)
    lse_all = lse[...]

    def ext_of(b, norm):
        high, low = pieces(norm)
        tile = jnp.where(row == 0, high, jnp.where(row == 1, low, 0.0))
        return jnp.where(left_half(), x[b, 256:264].astype(F32), tile)

    for b in range(NB):
        norm = norm_rows(lse_all, b)
        if b < GLOB:
            plain = ext_of(b, norm)
            full = plain.astype(BF16)
            if b == 0:
                first[0:256] = x[b, 0:256]
                first[256:264] = full
            keep = pos[0] == 0
            glob[b, 0:256] = jnp.where(keep, x[b, 0:256], jnp.zeros((256, HD), BF16))
            glob[b, 256:264] = jnp.where(keep, full, jnp.zeros((8, HD), BF16))
            norm = jnp.where(pos[0] == 0, OFF, norm)
        ext[b] = ext_of(b, norm)
        if b == NB - 1:
            last[0:256] = x[b, 0:256]
            last[256:264] = ext[b].astype(BF16)


    def step(i, carry):
        for c in range(2):
            t = i * 2 + c
            tile = jnp.zeros((8, HD), F32)
            for r in range(RAND):
                b = table[t, r]
                out[t, r * 64 : r * 64 + 64] = x[b, 0:64]
                out[t, 192 + r * 64 : 256 + r * 64] = x[b, 192:256]
                part = ext[b]
                if r:
                    part = pltpu.roll(part, 2 * r, 0)
                tile = tile + part
            out[t, 384:392] = tile.astype(BF16)
            pltpu.make_async_copy(out.at[t], dest.at[t], sem.at[t]).start()
        return carry

    lax.fori_loop(0, NB // 2, step, 0)

    def finish(t, carry):
        pltpu.make_async_copy(out.at[t], dest.at[t], sem.at[t]).wait()
        return carry

    lax.fori_loop(0, NB, finish, 0)


def grads(q, g, norm, delta, k, v, keep=None):
    st = nt(k, q) * FACTOR
    pt = jnp.exp(st - norm)
    if keep is not None:
        pt = jnp.where(keep, pt, 0.0)
    dst = (pt * (nt(v, g) - delta)).astype(BF16)
    return tn(dst, k), nn(dst, q), nn(pt.astype(BF16), g)


def staged(tiles, scores, probs, lows):
    depth = 3
    held = {}
    for step in range(len(tiles) + 2):
        if step < len(tiles):
            tile = tiles[step]()
            held[step] = tile
            shape = (tile["k"].shape[0], tile["q"].shape[0])
            slot = step % depth
            view = (slot, slice(0, shape[0]), slice(0, shape[1]))
            scores[view] = nt(tile["k"], tile["q"])
            probs[view] = nt(tile["v"], tile["g"])
        n = step - 1
        if 0 <= n < len(tiles):
            tile = held[n]
            shape = (tile["k"].shape[0], tile["q"].shape[0])
            view = (n % depth, slice(0, shape[0]), slice(0, shape[1]))
            pt = jnp.exp(scores[view] * FACTOR - tile["norm"])
            if tile.get("keep") is not None:
                pt = jnp.where(tile["keep"], pt, 0.0)
            low_view = (n % depth, 0) + view[1:]
            lows[low_view] = pt.astype(BF16)
            low_view = (n % depth, 1) + view[1:]
            lows[low_view] = (pt * (probs[view] - tile["delta"])).astype(BF16)
        n = step - 2
        if 0 <= n < len(tiles):
            tile = held.pop(n)
            shape = (tile["k"].shape[0], tile["q"].shape[0])
            cut = (slice(0, shape[0]), slice(0, shape[1]))
            pt = lows[(n % depth, 0) + cut]
            dst = lows[(n % depth, 1) + cut]
            tile["use"](tn(dst, tile["k"]), nn(dst, tile["q"]), nn(pt, tile["g"]))


def two(ext, a):
    return ext[a : a + 1].astype(F32) + ext[a + 1 : a + 2].astype(F32)


def joined(ref, a, first, last):
    return jnp.concatenate([ref[n, a * 64 : (a + 1) * 64] for n in range(first, last)], axis=0)


def pair_delta(x, b):
    e0 = x[b, 256:264].astype(F32)
    e1 = x[b + 1, 256:264].astype(F32)
    return low_pair(two(e0, 0), two(e1, 0))


def masked_norms(pos, lse):
    lse_all = lse[...]
    lanes = lax.broadcasted_iota(jnp.int32, lse_all.shape, 1)
    return jnp.where((pos[0] == 0) & (lanes < GLOB * BLK), OFF, lse_all)


def window_body(pos, x, lse, dq_out, dk_out, dv_out, dq, dk, dv, sem):
    lse_all = masked_norms(pos, lse)
    for i in range(NB // 2):
        b = 2 * i
        norm = lse_all[:, i * HD : (i + 1) * HD]
        low, high = max(b - 1, 0), min(b + 3, NB)
        shape = ((high - low) * BLK, HD)
        kb = (lax.broadcasted_iota(jnp.int32, shape, 0) >> 6) + low
        qb = (lax.broadcasted_iota(jnp.int32, shape, 1) >> 6) + b
        keep = jnp.abs(kb - qb) <= 1
        if low < GLOB:
            keep = keep & ((pos[0] > 0) | (kb >= GLOB))
        wq, wk, wv = grads(
            joined(x, 0, b, b + 2),
            joined(x, 3, b, b + 2),
            norm,
            pair_delta(x, b),
            joined(x, 1, low, high),
            joined(x, 2, low, high),
            keep,
        )
        dq[b * 64 : b * 64 + 128] = wq
        for acc, part in ((dk, wk), (dv, wv)):
            old = min(b + 1, NB) * 64 if b else 0
            seen = slice(low * 64, old)
            if b:
                acc[seen] = acc[seen] + part[0 : old - low * 64]
            acc[old : high * 64] = part[old - low * 64 :]
    pushes = [
        pltpu.make_async_copy(src, dst, sem.at[n])
        for n, (src, dst) in enumerate(((dq, dq_out), (dk, dk_out), (dv, dv_out)))
    ]
    for push in pushes:
        push.start()
    for push in pushes:
        push.wait()


def rand_body(table, x, y, dk_out, dv_out, z, dk, dv, buf, sem, acc_sem, scores, probs, lows):
    dk[...] = jnp.zeros_like(dk)
    dv[...] = jnp.zeros_like(dv)
    sub = lax.broadcasted_iota(jnp.int32, (HD, HD), 0)
    lane = lax.broadcasted_iota(jnp.int32, (HD, HD), 1)
    keep = (sub >> 6) == (lane >> 6)
    entries = [(t, r) for t in range(NB) for r in range(RAND)]

    def tile_of(n):
        pair = entries[2 * n : 2 * n + 2]

        def make():
            def both(base):
                return jnp.concatenate(
                    [y[t, base + r * 64 : base + r * 64 + 64] for t, r in pair], axis=0
                )

            sides = [two(y[t, 384:392].astype(F32), 2 * r) for t, r in pair]
            js = [table[NB + t, r] for t, r in pair]

            def use(pq, pk, pv):
                low = (pq * FACTOR).astype(BF16)
                for m, (t, r) in enumerate(pair):
                    rows = slice(m * 64, m * 64 + 64)
                    buf[t, r * 64 : r * 64 + 64] = low[rows]
                    span = pl.ds(pl.multiple_of(js[m] * 64, 64), 64)
                    dk[span] = dk[span] + pk[rows]
                    dv[span] = dv[span] + pv[rows]
                    if r == RAND - 1:
                        pltpu.make_async_copy(buf.at[t], z.at[t], sem.at[t]).start()

            return dict(
                q=both(0),
                g=both(192),
                k=jnp.concatenate([x[j, 64:128] for j in js], axis=0),
                v=jnp.concatenate([x[j, 128:192] for j in js], axis=0),
                norm=high_pair(*sides),
                delta=low_pair(*sides),
                keep=keep,
                use=use,
            )

        return make

    staged([tile_of(n) for n in range(len(entries) // 2)], scores, probs, lows)
    drains = []
    for n in range(4):
        span = pl.ds(n * 256, 256)
        for m, (src, dst) in enumerate(((dk, dk_out), (dv, dv_out))):
            drain = pltpu.make_async_copy(src.at[span], dst.at[span], acc_sem.at[2 * n + m])
            drain.start()
            drains.append(drain)
    for drain in drains:
        drain.wait()

    def finish(t, carry):
        pltpu.make_async_copy(buf.at[t], z.at[t], sem.at[t]).wait()
        return carry

    lax.fori_loop(0, NB, finish, 0)


def global_body(
    pos, x, lse, glob, dq_out, dk_out, dv_out, gpart, glow,
    dq, dk, dv, sem, sums, scores, probs, lows,
):
    here = pos[0]
    lse_all = masked_norms(pos, lse)
    gq, gk, gv, gg = (joined(glob, a, 0, GLOB) for a in range(4))
    sides = [two(glob[n, 256:264].astype(F32), 0) for n in range(GLOB)]
    gdelta = low_pair(*sides)
    gnorm = high_pair(*sides)
    sums[...] = jnp.zeros_like(sums)
    tiles = []
    for i in range(4):
        b = 4 * i
        span = slice(b * 64, b * 64 + 256)

        def down(b=b, span=span):
            def use(fq, fk, fv):
                sums[0] = sums[0] + fq
                dk[span] = fk
                dv[span] = fv

            return dict(
                q=gq,
                g=gg,
                k=joined(x, 1, b, b + 4),
                v=joined(x, 2, b, b + 4),
                norm=gnorm,
                delta=gdelta,
                use=use,
            )

        def across(b=b, span=span):
            def use(wq, wk, wv):
                dq[span] = wq
                sums[1] = sums[1] + wk
                sums[2] = sums[2] + wv

            return dict(
                q=joined(x, 0, b, b + 4),
                g=joined(x, 3, b, b + 4),
                k=gk,
                v=gv,
                norm=lse_all[:, span],
                delta=jnp.concatenate([pair_delta(x, b), pair_delta(x, b + 2)], axis=1),
                use=use,
            )

        tiles += [down, across]
    staged(tiles, scores, probs, lows)
    gq_sum, gk_sum, gv_sum = sums[0], sums[1], sums[2]
    pushes = [
        pltpu.make_async_copy(src, dst, sem.at[n])
        for n, (src, dst) in enumerate(((dq, dq_out), (dk, dk_out), (dv, dv_out)))
    ]
    for push in pushes:
        push.start()
    for n, total in enumerate((gq_sum * FACTOR, gk_sum * FACTOR, gv_sum)):
        gpart[n] = total
        glow[n] = total.astype(BF16)
    for push in pushes:
        push.wait()


def gather_body(
    pos, x, lse, before, after, dq_w, dk_w, dv_w, dq_g, dk_g, dv_g, dk_r, dv_r, w, dq, edge,
    s0, s1, s2, dq_s, dk_s, dv_s, s3, s4, buf, in_sem, out_sem,
):
    here = pos[0]
    held = (s0, s1, s2, dq_s, dk_s, dv_s, s3, s4)
    sources = (dq_w, dk_w, dv_w, dq_g, dk_g, dv_g, dk_r, dv_r)
    pulls = [
        pltpu.make_async_copy(src, dst, in_sem.at[n])
        for n, (src, dst) in enumerate(zip(sources, held))
    ]
    for pull in pulls:
        pull.start()
    lse_all = masked_norms(pos, lse)
    extra = []
    for slab, b in ((before, 0), (after, NB - 1)):
        span = slice(b * 64, b * 64 + 64)
        far_ext = two(slab[256:264].astype(F32), 0)
        own_ext = two(x[b, 256:264].astype(F32), 0)
        far_norm = far_ext[:, 64:128]
        if b == 0:
            far_norm = jnp.where(here == 0, OFF, far_norm)
        own_q, _, _ = grads(
            x[b, 0:64],
            x[b, 192:256],
            lse_all[:, span],
            own_ext[:, 0:64],
            slab[64:128],
            slab[128:192],
        )
        _, own_k, own_v = grads(
            slab[0:64],
            slab[192:256],
            far_norm,
            far_ext[:, 0:64],
            x[b, 64:128],
            x[b, 128:192],
        )
        extra.append((span, own_q, own_k, own_v))
    for pull in pulls:
        pull.wait()
    for span, own_q, own_k, own_v in extra:
        dq_s[span] = dq_s[span] + own_q
        dk_s[span] = dk_s[span] + own_k
        dv_s[span] = dv_s[span] + own_v
    dq[...] = dq_s[...] + s0[...]
    pushes = []
    for b in range(NB):
        span = slice(b * 64, b * 64 + 64)
        rk = (dk_s[span] + s1[span] + s3[span]) * FACTOR
        rv = dv_s[span] + s2[span] + s4[span]
        if b in EDGES:
            at = EDGES.index(b) * 128
            edge[at : at + 64] = rk
            edge[at + 64 : at + 128] = rv
            continue
        buf[b, 0:64] = rk.astype(BF16)
        buf[b, 64:128] = rv.astype(BF16)
        push = pltpu.make_async_copy(buf.at[b], w.at[b, pl.ds(64, 128)], out_sem.at[b])
        push.start()
        pushes.append(push)
    for push in pushes:
        push.wait()


def merge_body(pos, table, dq, edge, z, gtot, w_in, w, acc, out, out_edge, sem):
    acc[...] = dq[...] * FACTOR

    def step(t, carry):
        for r in range(RAND):
            b = table[t, r]
            span = pl.ds(pl.multiple_of(b * 64, 64), 64)
            acc[span] = acc[span] + z[t, r * 64 : r * 64 + 64].astype(F32)
        return carry

    lax.fori_loop(0, NB, step, 0)
    home = jnp.where(pos[0] == 0, 1.0, 0.0)
    pushes = []

    def send(src, dst, n):
        push = pltpu.make_async_copy(src, dst, sem.at[n])
        push.start()
        pushes.append(push)

    for n, b in enumerate(EDGES):
        rk, rv = edge[n * 128 : n * 128 + 64], edge[n * 128 + 64 : n * 128 + 128]
        rk = rk + home * gtot[1, b * 64 : b * 64 + 64]
        rv = rv + home * gtot[2, b * 64 : b * 64 + 64]
        out_edge[n, 0:64] = rk.astype(BF16)
        out_edge[n, 64:128] = rv.astype(BF16)
        send(out_edge.at[n], w.at[b, pl.ds(64, 128)], NB + n)
    for b in range(NB):
        span = slice(b * 64, b * 64 + 64)
        rq = acc[span]
        if b < GLOB:
            rq = rq + home * gtot[0, span]
        out[b] = rq.astype(BF16)
        send(out.at[b], w.at[b, pl.ds(0, 64)], b)
    for push in pushes:
        push.wait()


def unpack_body(w, q, k, v):
    for h in range(HEADS):
        cols = pl.ds(h * HD, HD)
        q[:, cols] = w[h, 0:64]
        k[:, cols] = w[h, 64:128]
        v[:, cols] = w[h, 128:192]


def struct(shape, dtype=BF16):
    return jax.ShapeDtypeStruct(shape, dtype)


def far(shape, dtype=BF16):
    return pltpu.HBM(shape, dtype)


def near(shape, dtype=BF16):
    return pltpu.VMEM(shape, dtype)


def hold(x):
    return pltpu.with_memory_space_constraint(x, pltpu.VMEM)


def keep_far(x):
    return pltpu.with_memory_space_constraint(x, pltpu.HBM)


def exchange(x, axis):
    return lax.all_to_all(x, axis, split_axis=0, concat_axis=0, tiled=True)


def per_device(query, key, value, output, grad_out, logsumexp, rand_blocks):
    position = lax.axis_index("seq")
    pos = position.astype(jnp.int32).reshape(1)
    rows = NB * BLK
    groups = NB
    dma = pltpu.SemaphoreType.DMA
    whole = pltpu.VMEM((BLK, HEADS * HD), BF16)
    packed = call(
        pack_body,
        far((HEADS, SLAB, HD)),
        [HB] * 5,
        HB,
        nbytes=5 << 18,
        scratch=[whole] * 5 + [pltpu.VMEM((HEADS, SLAB, HD), BF16), dma((5,)), dma((HEADS,))],
    )(*map(keep_far, (query, key, value, output, grad_out)))
    x = exchange(packed, "head")
    table = call(table_body, struct((2 * NB, HD), jnp.int32), [SM, VM], VM, nbytes=1 << 14)(
        pos, rand_blocks.reshape(NB, NB * RAND)
    )
    y, last, first, glob = call(
        select_body,
        (far((NB, PAIR, HD)), struct((SLAB, HD)), struct((SLAB, HD)), struct((GLOB, SLAB, HD))),
        [SM, SM, VM, VM],
        (HB, VM, VM, VM),
        nbytes=3 << 20,
        scratch=[
            pltpu.VMEM((NB, 8, HD), F32),
            pltpu.VMEM((NB, PAIR, HD), BF16),
            dma((NB,)),
        ],
    )(pos, table, x, logsumexp)
    def spread(glob, reach, starts):
        source = glob
        for n in (1, 2, 3):
            glob = glob + lax.ppermute(source, "seq", [(s, s + n * reach) for s in starts])
        return glob

    def collect(gpart, glow, reach, starts):
        for n in (1, 2, 3):
            moved = lax.ppermute(glow, "seq", [(s + n * reach, s) for s in starts])
            gpart = gpart + moved.astype(F32)
        return gpart

    corners = range(0, groups, 4)
    glob = spread(glob, 4, (0,))
    glob, y = lax.optimization_barrier((glob, y))
    y = exchange(y, "seq")
    glob = spread(glob, 1, corners)
    grid = pltpu.VMEM((rows, HD), F32)
    far_acc = far((rows, HD), F32)
    acc = near((rows, HD), F32)
    dq_w, dk_w, dv_w = call(
        window_body,
        (far_acc,) * 3,
        [SM, VM, VM],
        (HB,) * 3,
        flops=1 << 29,
        nbytes=2 << 20,
        scratch=[grid] * 3 + [dma((3,))],
    )(pos, x, logsumexp)
    glob, dq_w = lax.optimization_barrier((glob, dq_w))
    dq_g, dk_g, dv_g, gpart, glow = call(
        global_body,
        (far_acc,) * 3 + (struct((3, HD, HD), F32), struct((3, HD, HD))),
        [SM] + [VM] * 3,
        (HB,) * 3 + (VM,) * 2,
        flops=1 << 29,
        nbytes=4 << 20,
        scratch=[grid] * 3
        + [
            dma((3,)),
            pltpu.VMEM((3, HD, HD), F32),
            pltpu.VMEM((3, 256, 256), F32),
            pltpu.VMEM((3, 256, 256), F32),
            pltpu.VMEM((3, 2, 256, 256), BF16),
        ],
    )(pos, x, logsumexp, glob)
    glow, last, first = lax.optimization_barrier((glow, last, first))
    gpart = collect(gpart, glow, 1, corners)
    before = lax.ppermute(last, "seq", [(s, s + 1) for s in range(groups - 1)])
    after = lax.ppermute(first, "seq", [(s + 1, s) for s in range(groups - 1)])
    y, gpart, before, after = lax.optimization_barrier((y, gpart, before, after))
    dk_r, dv_r, z = call(
        rand_body,
        (far_acc, far_acc, far((NB, RAND * BLK, HD))),
        [SM, VM, VM],
        (HB,) * 3,
        flops=1 << 29,
        nbytes=4 << 20,
        scratch=[
            grid,
            grid,
            pltpu.VMEM((NB, RAND * BLK, HD), BF16),
            dma((NB,)),
            dma((8,)),
            pltpu.VMEM((3, HD, HD), F32),
            pltpu.VMEM((3, HD, HD), F32),
            pltpu.VMEM((3, 2, HD, HD), BF16),
        ],
    )(table, x, y)
    z, gpart = lax.optimization_barrier((z, gpart))
    z = exchange(z, "seq")
    gpart = collect(gpart, gpart.astype(BF16), 4, (0,))
    w, dq, edge = call(
        gather_body,
        (far((NB, 3 * BLK, HD)), acc, struct((len(EDGES) * 2 * BLK, HD), F32)),
        [SM] + [VM] * 4 + [HB] * 8,
        (HB, VM, VM),
        flops=1 << 24,
        nbytes=4 << 20,
        scratch=[grid] * 8 + [pltpu.VMEM((NB, 2 * BLK, HD), BF16), dma((8,)), dma((NB,))],
    )(
        pos,
        x,
        logsumexp,
        before,
        after,
        *map(keep_far, (dq_w, dk_w, dv_w, dq_g, dk_g, dv_g, dk_r, dv_r)),
    )
    w = call(
        merge_body,
        far((NB, 3 * BLK, HD)),
        [SM, SM] + [VM] * 4 + [HB],
        HB,
        nbytes=4 << 20,
        scratch=[
            grid,
            pltpu.VMEM((NB, BLK, HD), BF16),
            pltpu.VMEM((len(EDGES), 2 * BLK, HD), BF16),
            dma((NB + len(EDGES),)),
        ],
        aliases={6: 0},
    )(pos, table, hold(dq), edge, z, gpart, w)
    w = exchange(w, "head")
    shape = struct((BLK, HEADS * HD))
    return call(unpack_body, (shape, shape, shape), [VM], (VM,) * 3, nbytes=3 << 19)(w)


def solution(mesh):
    in_specs = (
        P(("seq", "head"), None),
        P(("seq", "head"), None),
        P(("seq", "head"), None),
        P(("seq", "head"), None),
        P(("seq", "head"), None),
        P("head", "seq"),
        P(),
    )
    out_specs = (P(("seq", "head"), None), P(("seq", "head"), None), P(("seq", "head"), None))
    return jax.shard_map(
        per_device, mesh=mesh, in_specs=in_specs, out_specs=out_specs, check_vma=False
    )
```

```python
import jax
import jax.numpy as jnp
from jax import lax
from jax.experimental import pallas as pl
from jax.experimental.pallas import tpu as pltpu
from jax.sharding import PartitionSpec as P

HEADS = 16
HD = 128
BLK = 64
GLOB = 2
RAND = 3
NB = 16
FACTOR = HD ** (-0.5)
OFF = 1e30
EDGES = (0, 1)
SLAB = 4 * BLK + 8
PAIR = RAND * 2 * BLK + 8
F32 = jnp.float32
BF16 = jnp.bfloat16

HB = pl.BlockSpec(memory_space=pltpu.HBM)
VM = pl.BlockSpec(memory_space=pltpu.VMEM)
SM = pl.BlockSpec(memory_space=pltpu.SMEM)


def call(body, outs, in_specs, out_specs, flops=0, nbytes=0, scratch=(), aliases={}, limit=8):
    return pl.pallas_call(
        body,
        out_shape=outs,
        in_specs=in_specs,
        out_specs=out_specs,
        scratch_shapes=list(scratch),
        input_output_aliases=aliases,
        compiler_params=pltpu.CompilerParams(vmem_limit_bytes=limit << 20),
        cost_estimate=pl.CostEstimate(flops=flops, bytes_accessed=nbytes, transcendentals=0),
    )


def nt(a, b):
    return lax.dot_general(a, b, (((1,), (1,)), ((), ())), preferred_element_type=F32)


def nn(a, b):
    return lax.dot_general(a, b, (((1,), (0,)), ((), ())), preferred_element_type=F32)


def tn(a, b):
    return lax.dot_general(a, b, (((0,), (0,)), ((), ())), preferred_element_type=F32)


def pieces(x):
    high = x.astype(BF16).astype(F32)
    return high, (x - high).astype(BF16).astype(F32)


def pack_body(q, k, v, o, g, out, qs, ks, vs, os, gs, ps, in_sem, out_sem):
    pulls = [
        pltpu.make_async_copy(src, dst, in_sem.at[i])
        for i, (src, dst) in enumerate(zip((o, g, q, k, v), (os, gs, qs, ks, vs)))
    ]
    for pull in pulls:
        pull.start()
    lane = lax.broadcasted_iota(jnp.int32, (BLK, HD), 1)
    row = lax.broadcasted_iota(jnp.int32, (8, HD), 0)
    deltas = jnp.zeros((BLK, HD), F32)
    pulls[0].wait()
    pulls[1].wait()
    for h in range(HEADS):
        cols = pl.ds(h * HD, HD)
        gh = gs[:, cols]
        ps[h, 192:256] = gh
        part = jnp.sum(gh.astype(F32) * os[:, cols].astype(F32), axis=1, keepdims=True)
        deltas = jnp.where(lane == h, part, deltas)
    turned = jnp.transpose(jnp.concatenate([deltas, jnp.zeros((BLK, HD), F32)], axis=0))
    high, low = pieces(turned)
    for pull in pulls[2:]:
        pull.wait()
    pushes = []
    for h in range(HEADS):
        cols = pl.ds(h * HD, HD)
        ps[h, 0:64] = qs[:, cols]
        ps[h, 64:128] = ks[:, cols]
        ps[h, 128:192] = vs[:, cols]
        tile = jnp.where(row == 0, high[h : h + 1], jnp.where(row == 1, low[h : h + 1], 0.0))
        ps[h, 256:264] = tile.astype(BF16)
        push = pltpu.make_async_copy(ps.at[h], out.at[h], out_sem.at[h])
        push.start()
        pushes.append(push)
    for push in pushes:
        push.wait()


def table_body(pos, entries, out):
    here = pos[0]
    e = entries[...]
    width = e.shape[1]
    lane = lax.broadcasted_iota(jnp.int32, (NB, width), 1)
    row = lax.broadcasted_iota(jnp.int32, (NB, width), 0)
    mine = jnp.sum(jnp.where(row == here, e, 0), axis=0, keepdims=True)
    to_group = jnp.broadcast_to(mine, (NB, width)) >> 4
    hit = jnp.concatenate(
        [jnp.where(to_group == row, 1.0, 0.0), jnp.where((e >> 4) == here, 1.0, 0.0)], axis=0
    )
    value = jnp.concatenate([(lane * 171) >> 9, e & 15], axis=0)
    ii = lax.broadcasted_iota(jnp.int32, (width, width), 0)
    jj = lax.broadcasted_iota(jnp.int32, (width, width), 1)
    before = jnp.where(ii < jj, 1.0, 0.0).astype(BF16)
    rank = nn(hit.astype(BF16), before)
    out_lane = lax.broadcasted_iota(jnp.int32, (2 * NB, HD), 1)
    result = jnp.zeros((2 * NB, HD), jnp.int32)
    for r in range(RAND):
        chosen = jnp.where((hit > 0.5) & (jnp.abs(rank - r) < 0.5), value, 0)
        total = jnp.sum(chosen, axis=1, keepdims=True)
        result = jnp.where(out_lane == r, total, result)
    out[...] = result


def left_half():
    return lax.broadcasted_iota(jnp.int32, (1, HD), 1) < BLK


def low_pair(one, other):
    return jnp.where(left_half(), one, pltpu.roll(other, BLK, 1))


def high_pair(one, other):
    return jnp.where(left_half(), pltpu.roll(one, BLK, 1), other)


def norm_rows(lse, b):
    pair = lse[:, (b // 2) * HD : (b // 2 + 1) * HD]
    return pair if b % 2 else pltpu.roll(pair, BLK, 1)


def select_body(pos, table, x, lse, dest, last, first, glob, ext, out, sem):
    row = lax.broadcasted_iota(jnp.int32, (8, HD), 0)
    lse_all = lse[...]

    def ext_of(b, norm):
        high, low = pieces(norm)
        tile = jnp.where(row == 0, high, jnp.where(row == 1, low, 0.0))
        return jnp.where(left_half(), x[b, 256:264].astype(F32), tile)

    for b in range(NB):
        norm = norm_rows(lse_all, b)
        if b < GLOB:
            plain = ext_of(b, norm)
            full = plain.astype(BF16)
            if b == 0:
                first[0:256] = x[b, 0:256]
                first[256:264] = full
            keep = pos[0] == 0
            glob[b, 0:256] = jnp.where(keep, x[b, 0:256], jnp.zeros((256, HD), BF16))
            glob[b, 256:264] = jnp.where(keep, full, jnp.zeros((8, HD), BF16))
            norm = jnp.where(pos[0] == 0, OFF, norm)
        ext[b] = ext_of(b, norm)
        if b == NB - 1:
            last[0:256] = x[b, 0:256]
            last[256:264] = ext[b].astype(BF16)


    def step(i, carry):
        for c in range(4):
            t = i * 4 + c
            tile = jnp.zeros((8, HD), F32)
            for r in range(RAND):
                b = table[t, r]
                out[t, r * 64 : r * 64 + 64] = x[b, 0:64]
                out[t, 192 + r * 64 : 256 + r * 64] = x[b, 192:256]
                part = ext[b]
                if r:
                    part = pltpu.roll(part, 2 * r, 0)
                tile = tile + part
            out[t, 384:392] = tile.astype(BF16)
            pltpu.make_async_copy(out.at[t], dest.at[t], sem.at[t]).start()
        return carry

    lax.fori_loop(0, NB // 4, step, 0)

    def finish(t, carry):
        pltpu.make_async_copy(out.at[t], dest.at[t], sem.at[t]).wait()
        return carry

    lax.fori_loop(0, NB, finish, 0)


def grads(q, g, norm, delta, k, v, keep=None):
    st = nt(k, q) * FACTOR
    pt = jnp.exp(st - norm)
    if keep is not None:
        pt = jnp.where(keep, pt, 0.0)
    dst = (pt * (nt(v, g) - delta)).astype(BF16)
    return tn(dst, k), nn(dst, q), nn(pt.astype(BF16), g)


def staged(tiles, scores, probs, lows, want="qkv"):
    depth = 3
    held = {}
    for step in range(len(tiles) + 2):
        if step < len(tiles):
            tile = tiles[step]()
            held[step] = tile
            shape = (tile["k"].shape[0], tile["q"].shape[0])
            slot = step % depth
            view = (slot, slice(0, shape[0]), slice(0, shape[1]))
            scores[view] = nt(tile["k"], tile["q"])
            probs[view] = nt(tile["v"], tile["g"])
        n = step - 1
        if 0 <= n < len(tiles):
            tile = held[n]
            shape = (tile["k"].shape[0], tile["q"].shape[0])
            view = (n % depth, slice(0, shape[0]), slice(0, shape[1]))
            pt = jnp.exp(scores[view] * FACTOR - tile["norm"])
            if tile.get("keep") is not None:
                pt = jnp.where(tile["keep"], pt, 0.0)
            if "v" in want:
                low_view = (n % depth, 0) + view[1:]
                lows[low_view] = pt.astype(BF16)
            low_view = (n % depth, 1) + view[1:]
            lows[low_view] = (pt * (probs[view] - tile["delta"])).astype(BF16)
        n = step - 2
        if 0 <= n < len(tiles):
            tile = held.pop(n)
            shape = (tile["k"].shape[0], tile["q"].shape[0])
            cut = (slice(0, shape[0]), slice(0, shape[1]))
            dst = lows[(n % depth, 1) + cut]
            parts = []
            if "q" in want:
                parts.append(tn(dst, tile["k"]))
            if "k" in want:
                parts.append(nn(dst, tile["q"]))
            if "v" in want:
                parts.append(nn(lows[(n % depth, 0) + cut], tile["g"]))
            tile["use"](*parts)


def two(ext, a):
    return ext[a : a + 1].astype(F32) + ext[a + 1 : a + 2].astype(F32)


def joined(ref, a, first, last):
    return jnp.concatenate([ref[n, a * 64 : (a + 1) * 64] for n in range(first, last)], axis=0)


def pair_delta(x, b):
    e0 = x[b, 256:264].astype(F32)
    e1 = x[b + 1, 256:264].astype(F32)
    return low_pair(two(e0, 0), two(e1, 0))


def masked_norms(pos, lse):
    lse_all = lse[...]
    lanes = lax.broadcasted_iota(jnp.int32, lse_all.shape, 1)
    return jnp.where((pos[0] == 0) & (lanes < GLOB * BLK), OFF, lse_all)


def window_body(pos, x, lse, dq_out, dk_out, dv_out, dq, dk, dv, sem):
    lse_all = masked_norms(pos, lse)
    for i in range(NB // 2):
        b = 2 * i
        norm = lse_all[:, i * HD : (i + 1) * HD]
        low, high = max(b - 1, 0), min(b + 3, NB)
        shape = ((high - low) * BLK, HD)
        kb = (lax.broadcasted_iota(jnp.int32, shape, 0) >> 6) + low
        qb = (lax.broadcasted_iota(jnp.int32, shape, 1) >> 6) + b
        keep = jnp.abs(kb - qb) <= 1
        if low < GLOB:
            keep = keep & ((pos[0] > 0) | (kb >= GLOB))
        wq, wk, wv = grads(
            joined(x, 0, b, b + 2),
            joined(x, 3, b, b + 2),
            norm,
            pair_delta(x, b),
            joined(x, 1, low, high),
            joined(x, 2, low, high),
            keep,
        )
        dq[b * 64 : b * 64 + 128] = wq
        for acc, part in ((dk, wk), (dv, wv)):
            old = min(b + 1, NB) * 64 if b else 0
            seen = slice(low * 64, old)
            if b:
                acc[seen] = acc[seen] + part[0 : old - low * 64]
            acc[old : high * 64] = part[old - low * 64 :]
    pushes = [
        pltpu.make_async_copy(src, dst, sem.at[n])
        for n, (src, dst) in enumerate(((dq, dq_out), (dk, dk_out), (dv, dv_out)))
    ]
    for push in pushes:
        push.start()
    for push in pushes:
        push.wait()


def rand_tiles(table, x, y, use):
    sub = lax.broadcasted_iota(jnp.int32, (HD, HD), 0)
    lane = lax.broadcasted_iota(jnp.int32, (HD, HD), 1)
    keep = (sub >> 6) == (lane >> 6)
    entries = [(t, r) for t in range(NB) for r in range(RAND)]

    def tile_of(n):
        pair = entries[2 * n : 2 * n + 2]

        def make():
            def both(base):
                return jnp.concatenate(
                    [y[t, base + r * 64 : base + r * 64 + 64] for t, r in pair], axis=0
                )

            sides = [two(y[t, 384:392].astype(F32), 2 * r) for t, r in pair]
            js = [table[NB + t, r] for t, r in pair]
            return dict(
                q=both(0),
                g=both(192),
                k=jnp.concatenate([x[j, 64:128] for j in js], axis=0),
                v=jnp.concatenate([x[j, 128:192] for j in js], axis=0),
                norm=high_pair(*sides),
                delta=low_pair(*sides),
                keep=keep,
                use=lambda *parts: use(pair, js, *parts),
            )

        return make

    return [tile_of(n) for n in range(len(entries) // 2)]


def rand_query_body(table, x, y, z, y_out, buf, sem, y_sem, scores, probs, lows):
    saves = [
        pltpu.make_async_copy(y.at[pl.ds(2 * n, 2)], y_out.at[pl.ds(2 * n, 2)], y_sem.at[n])
        for n in range(NB // 2)
    ]
    for save in saves:
        save.start()

    def use(pair, js, pq):
        low = (pq * FACTOR).astype(BF16)
        for m, (t, r) in enumerate(pair):
            buf[t, r * 64 : r * 64 + 64] = low[m * 64 : m * 64 + 64]
            if r == RAND - 1:
                pltpu.make_async_copy(buf.at[t], z.at[t], sem.at[t]).start()

    staged(rand_tiles(table, x, y, use), scores, probs, lows, "q")
    for save in saves:
        save.wait()

    def finish(t, carry):
        pltpu.make_async_copy(buf.at[t], z.at[t], sem.at[t]).wait()
        return carry

    lax.fori_loop(0, NB, finish, 0)


def rand_key_body(table, x, y_far, dk_out, dv_out, y, dk, dv, y_sem, sem, scores, probs, lows):
    pulls = [
        pltpu.make_async_copy(y_far.at[pl.ds(2 * n, 2)], y.at[pl.ds(2 * n, 2)], y_sem.at[n])
        for n in range(NB // 2)
    ]
    for pull in pulls:
        pull.start()
    dk[...] = jnp.zeros_like(dk)
    dv[...] = jnp.zeros_like(dv)
    for pull in pulls:
        pull.wait()

    def use(pair, js, pk, pv):
        for m, j in enumerate(js):
            rows = slice(m * 64, m * 64 + 64)
            span = pl.ds(pl.multiple_of(j * 64, 64), 64)
            dk[span] = dk[span] + pk[rows]
            dv[span] = dv[span] + pv[rows]

    staged(rand_tiles(table, x, y, use), scores, probs, lows, "kv")
    pushes = [
        pltpu.make_async_copy(src, dst, sem.at[n])
        for n, (src, dst) in enumerate(((dk, dk_out), (dv, dv_out)))
    ]
    for push in pushes:
        push.start()
    for push in pushes:
        push.wait()


def global_body(
    pos, x, lse, glob, dq_out, dk_out, dv_out, gpart, glow,
    dq, dk, dv, sem, sums, scores, probs, lows,
):
    here = pos[0]
    lse_all = masked_norms(pos, lse)
    gq, gk, gv, gg = (joined(glob, a, 0, GLOB) for a in range(4))
    sides = [two(glob[n, 256:264].astype(F32), 0) for n in range(GLOB)]
    gdelta = low_pair(*sides)
    gnorm = high_pair(*sides)
    sums[...] = jnp.zeros_like(sums)
    tiles = []
    for i in range(4):
        b = 4 * i
        span = slice(b * 64, b * 64 + 256)

        def down(b=b, span=span):
            def use(fq, fk, fv):
                sums[0] = sums[0] + fq
                dk[span] = fk
                dv[span] = fv

            return dict(
                q=gq,
                g=gg,
                k=joined(x, 1, b, b + 4),
                v=joined(x, 2, b, b + 4),
                norm=gnorm,
                delta=gdelta,
                use=use,
            )

        def across(b=b, span=span):
            def use(wq, wk, wv):
                dq[span] = wq
                sums[1] = sums[1] + wk
                sums[2] = sums[2] + wv

            return dict(
                q=joined(x, 0, b, b + 4),
                g=joined(x, 3, b, b + 4),
                k=gk,
                v=gv,
                norm=lse_all[:, span],
                delta=jnp.concatenate([pair_delta(x, b), pair_delta(x, b + 2)], axis=1),
                use=use,
            )

        tiles += [down, across]
    staged(tiles, scores, probs, lows)
    gq_sum, gk_sum, gv_sum = sums[0], sums[1], sums[2]
    pushes = [
        pltpu.make_async_copy(src, dst, sem.at[n])
        for n, (src, dst) in enumerate(((dq, dq_out), (dk, dk_out), (dv, dv_out)))
    ]
    for push in pushes:
        push.start()
    for n, total in enumerate((gq_sum * FACTOR, gk_sum * FACTOR, gv_sum)):
        gpart[n] = total
        glow[n] = total.astype(BF16)
    for push in pushes:
        push.wait()


def gather_body(
    pos, x, lse, before, after, dq_w, dk_w, dv_w, dq_g, dk_g, dv_g, dk_r, dv_r, w, dq, edge,
    s0, s1, s2, dq_s, dk_s, dv_s, s3, s4, buf, in_sem, out_sem,
):
    here = pos[0]
    held = (s0, s1, s2, dq_s, dk_s, dv_s, s3, s4)
    sources = (dq_w, dk_w, dv_w, dq_g, dk_g, dv_g, dk_r, dv_r)
    pulls = [
        pltpu.make_async_copy(src, dst, in_sem.at[n])
        for n, (src, dst) in enumerate(zip(sources, held))
    ]
    for pull in pulls:
        pull.start()
    lse_all = masked_norms(pos, lse)
    extra = []
    for slab, b in ((before, 0), (after, NB - 1)):
        span = slice(b * 64, b * 64 + 64)
        far_ext = two(slab[256:264].astype(F32), 0)
        own_ext = two(x[b, 256:264].astype(F32), 0)
        far_norm = far_ext[:, 64:128]
        if b == 0:
            far_norm = jnp.where(here == 0, OFF, far_norm)
        own_q, _, _ = grads(
            x[b, 0:64],
            x[b, 192:256],
            lse_all[:, span],
            own_ext[:, 0:64],
            slab[64:128],
            slab[128:192],
        )
        _, own_k, own_v = grads(
            slab[0:64],
            slab[192:256],
            far_norm,
            far_ext[:, 0:64],
            x[b, 64:128],
            x[b, 128:192],
        )
        extra.append((span, own_q, own_k, own_v))
    for pull in pulls:
        pull.wait()
    for span, own_q, own_k, own_v in extra:
        dq_s[span] = dq_s[span] + own_q
        dk_s[span] = dk_s[span] + own_k
        dv_s[span] = dv_s[span] + own_v
    dq[...] = dq_s[...] + s0[...]
    pushes = []
    for b in range(NB):
        span = slice(b * 64, b * 64 + 64)
        rk = (dk_s[span] + s1[span] + s3[span]) * FACTOR
        rv = dv_s[span] + s2[span] + s4[span]
        if b in EDGES:
            at = EDGES.index(b) * 128
            edge[at : at + 64] = rk
            edge[at + 64 : at + 128] = rv
            continue
        buf[b, 0:64] = rk.astype(BF16)
        buf[b, 64:128] = rv.astype(BF16)
        push = pltpu.make_async_copy(buf.at[b], w.at[b, pl.ds(64, 128)], out_sem.at[b])
        push.start()
        pushes.append(push)
    for push in pushes:
        push.wait()


def merge_body(pos, table, dq, edge, z, gtot, w_in, w, acc, out, out_edge, sem):
    acc[...] = dq[...] * FACTOR
    for t in range(NB):
        for r in range(RAND):
            span = pl.ds(pl.multiple_of(table[t, r] * 64, 64), 64)
            acc[span] = acc[span] + z[t, r * 64 : r * 64 + 64].astype(F32)
    home = jnp.where(pos[0] == 0, 1.0, 0.0)
    pushes = []

    def send(src, dst, n):
        push = pltpu.make_async_copy(src, dst, sem.at[n])
        push.start()
        pushes.append(push)

    for n, b in enumerate(EDGES):
        rk, rv = edge[n * 128 : n * 128 + 64], edge[n * 128 + 64 : n * 128 + 128]
        rk = rk + home * gtot[1, b * 64 : b * 64 + 64]
        rv = rv + home * gtot[2, b * 64 : b * 64 + 64]
        out_edge[n, 0:64] = rk.astype(BF16)
        out_edge[n, 64:128] = rv.astype(BF16)
        send(out_edge.at[n], w.at[b, pl.ds(64, 128)], NB + n)
    for b in range(NB):
        span = slice(b * 64, b * 64 + 64)
        rq = acc[span]
        if b < GLOB:
            rq = rq + home * gtot[0, span]
        out[b] = rq.astype(BF16)
        send(out.at[b], w.at[b, pl.ds(0, 64)], b)
    for push in pushes:
        push.wait()


def unpack_body(w, q, k, v):
    for h in range(HEADS):
        cols = pl.ds(h * HD, HD)
        q[:, cols] = w[h, 0:64]
        k[:, cols] = w[h, 64:128]
        v[:, cols] = w[h, 128:192]


def struct(shape, dtype=BF16):
    return jax.ShapeDtypeStruct(shape, dtype)


def far(shape, dtype=BF16):
    return pltpu.HBM(shape, dtype)


def near(shape, dtype=BF16):
    return pltpu.VMEM(shape, dtype)


def hold(x):
    return pltpu.with_memory_space_constraint(x, pltpu.VMEM)


def keep_far(x):
    return pltpu.with_memory_space_constraint(x, pltpu.HBM)


def exchange(x, axis):
    return lax.all_to_all(x, axis, split_axis=0, concat_axis=0, tiled=True)


def per_device(query, key, value, output, grad_out, logsumexp, rand_blocks):
    position = lax.axis_index("seq")
    pos = position.astype(jnp.int32).reshape(1)
    rows = NB * BLK
    groups = NB
    dma = pltpu.SemaphoreType.DMA
    whole = pltpu.VMEM((BLK, HEADS * HD), BF16)
    packed = call(
        pack_body,
        far((HEADS, SLAB, HD)),
        [HB] * 5,
        HB,
        nbytes=5 << 18,
        scratch=[whole] * 5 + [pltpu.VMEM((HEADS, SLAB, HD), BF16), dma((5,)), dma((HEADS,))],
    )(*map(keep_far, (query, key, value, output, grad_out)))
    x = exchange(packed, "head")
    table = call(table_body, struct((2 * NB, HD), jnp.int32), [SM, VM], VM, nbytes=1 << 14)(
        pos, rand_blocks.reshape(NB, NB * RAND)
    )
    y, last, first, glob = call(
        select_body,
        (far((NB, PAIR, HD)), struct((SLAB, HD)), struct((SLAB, HD)), struct((GLOB, SLAB, HD))),
        [SM, SM, VM, VM],
        (HB, VM, VM, VM),
        nbytes=3 << 20,
        scratch=[
            pltpu.VMEM((NB, 8, HD), F32),
            pltpu.VMEM((NB, PAIR, HD), BF16),
            dma((NB,)),
        ],
    )(pos, table, x, logsumexp)
    def spread(glob, reach, starts):
        source = glob
        for n in (1, 2, 3):
            glob = glob + lax.ppermute(source, "seq", [(s, s + n * reach) for s in starts])
        return glob

    def collect(gpart, glow, reach, starts):
        for n in (1, 2, 3):
            moved = lax.ppermute(glow, "seq", [(s + n * reach, s) for s in starts])
            gpart = gpart + moved.astype(F32)
        return gpart

    corners = range(0, groups, 4)
    glob = spread(glob, 4, (0,))
    glob, y = lax.optimization_barrier((glob, y))
    y = exchange(y, "seq")
    glob = spread(glob, 1, corners)
    grid = pltpu.VMEM((rows, HD), F32)
    far_acc = far((rows, HD), F32)
    acc = near((rows, HD), F32)
    dq_w, dk_w, dv_w = call(
        window_body,
        (far_acc,) * 3,
        [SM, VM, VM],
        (HB,) * 3,
        flops=1 << 29,
        nbytes=2 << 20,
        scratch=[grid] * 3 + [dma((3,))],
    )(pos, x, logsumexp)
    glob, dq_w = lax.optimization_barrier((glob, dq_w))
    dq_g, dk_g, dv_g, gpart, glow = call(
        global_body,
        (far_acc,) * 3 + (struct((3, HD, HD), F32), struct((3, HD, HD))),
        [SM] + [VM] * 3,
        (HB,) * 3 + (VM,) * 2,
        flops=1 << 29,
        nbytes=4 << 20,
        scratch=[grid] * 3
        + [
            dma((3,)),
            pltpu.VMEM((3, HD, HD), F32),
            pltpu.VMEM((3, 256, 256), F32),
            pltpu.VMEM((3, 256, 256), F32),
            pltpu.VMEM((3, 2, 256, 256), BF16),
        ],
    )(pos, x, logsumexp, glob)
    glow, last, first = lax.optimization_barrier((glow, last, first))
    gpart = collect(gpart, glow, 1, corners)
    before = lax.ppermute(last, "seq", [(s, s + 1) for s in range(groups - 1)])
    after = lax.ppermute(first, "seq", [(s + 1, s) for s in range(groups - 1)])
    y, gpart, before, after = lax.optimization_barrier((y, gpart, before, after))
    stage_space = [
        pltpu.VMEM((3, HD, HD), F32),
        pltpu.VMEM((3, HD, HD), F32),
        pltpu.VMEM((3, 2, HD, HD), BF16),
    ]
    z, y = call(
        rand_query_body,
        (far((NB, RAND * BLK, HD)), far((NB, PAIR, HD))),
        [SM, VM, VM],
        (HB,) * 2,
        flops=1 << 29,
        nbytes=4 << 20,
        scratch=[pltpu.VMEM((NB, RAND * BLK, HD), BF16), dma((NB,)), dma((NB // 2,))]
        + stage_space,
    )(table, x, y)
    z, gpart, y = lax.optimization_barrier((z, gpart, y))
    z = exchange(z, "seq")
    moved = lax.ppermute(gpart.astype(BF16), "seq", [(4, 0), (12, 8)])
    gpart = gpart + moved.astype(F32)
    dk_r, dv_r = call(
        rand_key_body,
        (far_acc, far_acc),
        [SM, VM, HB],
        (HB,) * 2,
        flops=1 << 29,
        nbytes=4 << 20,
        scratch=[pltpu.VMEM((NB, PAIR, HD), BF16), grid, grid, dma((NB // 2,)), dma((2,))]
        + stage_space,
    )(table, x, keep_far(y))
    w, dq, edge = call(
        gather_body,
        (far((NB, 3 * BLK, HD)), acc, struct((len(EDGES) * 2 * BLK, HD), F32)),
        [SM] + [VM] * 4 + [HB] * 8,
        (HB, VM, VM),
        flops=1 << 24,
        nbytes=4 << 20,
        scratch=[grid] * 8 + [pltpu.VMEM((NB, 2 * BLK, HD), BF16), dma((8,)), dma((NB,))],
    )(
        pos,
        x,
        logsumexp,
        before,
        after,
        *map(keep_far, (dq_w, dk_w, dv_w, dq_g, dk_g, dv_g, dk_r, dv_r)),
    )
    gpart, w, dq, edge = lax.optimization_barrier((gpart, w, dq, edge))
    moved = lax.ppermute(gpart.astype(BF16), "seq", [(8, 0)])
    gpart = gpart + moved.astype(F32)
    w = call(
        merge_body,
        far((NB, 3 * BLK, HD)),
        [SM, SM] + [VM] * 4 + [HB],
        HB,
        nbytes=4 << 20,
        scratch=[
            grid,
            pltpu.VMEM((NB, BLK, HD), BF16),
            pltpu.VMEM((len(EDGES), 2 * BLK, HD), BF16),
            dma((NB + len(EDGES),)),
        ],
        aliases={6: 0},
    )(pos, table, hold(dq), edge, z, gpart, w)
    w = exchange(w, "head")
    shape = struct((BLK, HEADS * HD))
    return call(unpack_body, (shape, shape, shape), [VM], (VM,) * 3, nbytes=3 << 19)(w)


def solution(mesh):
    in_specs = (
        P(("seq", "head"), None),
        P(("seq", "head"), None),
        P(("seq", "head"), None),
        P(("seq", "head"), None),
        P(("seq", "head"), None),
        P("head", "seq"),
        P(),
    )
    out_specs = (P(("seq", "head"), None), P(("seq", "head"), None), P(("seq", "head"), None))
    return jax.shard_map(
        per_device, mesh=mesh, in_specs=in_specs, out_specs=out_specs, check_vma=False
    )
```

```python
import jax
import jax.numpy as jnp
from jax import lax
from jax.experimental import pallas as pl
from jax.experimental.pallas import tpu as pltpu
from jax.sharding import PartitionSpec as P

HEADS = 16
HD = 128
BLK = 64
GLOB = 2
RAND = 3
NB = 16
FACTOR = HD ** (-0.5)
OFF = 1e30
EDGES = (0, 1)
SLAB = 4 * BLK + 8
PAIR = RAND * 2 * BLK + 8
F32 = jnp.float32
BF16 = jnp.bfloat16

HB = pl.BlockSpec(memory_space=pltpu.HBM)
VM = pl.BlockSpec(memory_space=pltpu.VMEM)
SM = pl.BlockSpec(memory_space=pltpu.SMEM)


def call(body, outs, in_specs, out_specs, flops=0, nbytes=0, scratch=(), aliases={}, limit=8):
    return pl.pallas_call(
        body,
        out_shape=outs,
        in_specs=in_specs,
        out_specs=out_specs,
        scratch_shapes=list(scratch),
        input_output_aliases=aliases,
        compiler_params=pltpu.CompilerParams(vmem_limit_bytes=limit << 20),
        cost_estimate=pl.CostEstimate(flops=flops, bytes_accessed=nbytes, transcendentals=0),
    )


def nt(a, b):
    return lax.dot_general(a, b, (((1,), (1,)), ((), ())), preferred_element_type=F32)


def nn(a, b):
    return lax.dot_general(a, b, (((1,), (0,)), ((), ())), preferred_element_type=F32)


def tn(a, b):
    return lax.dot_general(a, b, (((0,), (0,)), ((), ())), preferred_element_type=F32)


def pieces(x):
    high = x.astype(BF16).astype(F32)
    return high, (x - high).astype(BF16).astype(F32)


def pack_body(q, k, v, o, g, out, qs, ks, vs, os, gs, ps, in_sem, out_sem):
    pulls = [
        pltpu.make_async_copy(src, dst, in_sem.at[i])
        for i, (src, dst) in enumerate(zip((o, g, q, k, v), (os, gs, qs, ks, vs)))
    ]
    for pull in pulls:
        pull.start()
    lane = lax.broadcasted_iota(jnp.int32, (BLK, HD), 1)
    row = lax.broadcasted_iota(jnp.int32, (8, HD), 0)
    deltas = jnp.zeros((BLK, HD), F32)
    pulls[0].wait()
    pulls[1].wait()
    for h in range(HEADS):
        cols = pl.ds(h * HD, HD)
        gh = gs[:, cols]
        ps[h, 192:256] = gh
        part = jnp.sum(gh.astype(F32) * os[:, cols].astype(F32), axis=1, keepdims=True)
        deltas = jnp.where(lane == h, part, deltas)
    turned = jnp.transpose(jnp.concatenate([deltas, jnp.zeros((BLK, HD), F32)], axis=0))
    high, low = pieces(turned)
    for pull in pulls[2:]:
        pull.wait()
    pushes = []
    for h in range(HEADS):
        cols = pl.ds(h * HD, HD)
        ps[h, 0:64] = qs[:, cols]
        ps[h, 64:128] = ks[:, cols]
        ps[h, 128:192] = vs[:, cols]
        tile = jnp.where(row == 0, high[h : h + 1], jnp.where(row == 1, low[h : h + 1], 0.0))
        ps[h, 256:264] = tile.astype(BF16)
        push = pltpu.make_async_copy(ps.at[h], out.at[h], out_sem.at[h])
        push.start()
        pushes.append(push)
    for push in pushes:
        push.wait()


def table_body(pos, entries, out):
    here = pos[0]
    e = entries[...]
    width = e.shape[1]
    lane = lax.broadcasted_iota(jnp.int32, (NB, width), 1)
    row = lax.broadcasted_iota(jnp.int32, (NB, width), 0)
    mine = jnp.sum(jnp.where(row == here, e, 0), axis=0, keepdims=True)
    to_group = jnp.broadcast_to(mine, (NB, width)) >> 4
    hit = jnp.concatenate(
        [jnp.where(to_group == row, 1.0, 0.0), jnp.where((e >> 4) == here, 1.0, 0.0)], axis=0
    )
    value = jnp.concatenate([(lane * 171) >> 9, e & 15], axis=0)
    ii = lax.broadcasted_iota(jnp.int32, (width, width), 0)
    jj = lax.broadcasted_iota(jnp.int32, (width, width), 1)
    before = jnp.where(ii < jj, 1.0, 0.0).astype(BF16)
    rank = nn(hit.astype(BF16), before)
    out_lane = lax.broadcasted_iota(jnp.int32, (2 * NB, HD), 1)
    result = jnp.zeros((2 * NB, HD), jnp.int32)
    for r in range(RAND):
        chosen = jnp.where((hit > 0.5) & (jnp.abs(rank - r) < 0.5), value, 0)
        total = jnp.sum(chosen, axis=1, keepdims=True)
        result = jnp.where(out_lane == r, total, result)
    out[...] = result


def left_half():
    return lax.broadcasted_iota(jnp.int32, (1, HD), 1) < BLK


def low_pair(one, other):
    return jnp.where(left_half(), one, pltpu.roll(other, BLK, 1))


def high_pair(one, other):
    return jnp.where(left_half(), pltpu.roll(one, BLK, 1), other)


def norm_rows(lse, b):
    pair = lse[:, (b // 2) * HD : (b // 2 + 1) * HD]
    return pair if b % 2 else pltpu.roll(pair, BLK, 1)


def block_ext(x, b, norm):
    row = lax.broadcasted_iota(jnp.int32, (8, HD), 0)
    high, low = pieces(norm)
    tile = jnp.where(row == 0, high, jnp.where(row == 1, low, 0.0))
    return jnp.where(left_half(), x[b, 256:264].astype(F32), tile)


def slab_body(pos, x, lse, last, first, glob):
    lse_all = lse[...]
    keep = pos[0] == 0
    for b in (0, 1, NB - 1):
        full = block_ext(x, b, norm_rows(lse_all, b)).astype(BF16)
        if b < GLOB:
            glob[b, 0:256] = jnp.where(keep, x[b, 0:256], jnp.zeros((256, HD), BF16))
            glob[b, 256:264] = jnp.where(keep, full, jnp.zeros((8, HD), BF16))
        for slab, owner in ((first, 0), (last, NB - 1)):
            if b == owner:
                slab[0:256] = x[b, 0:256]
                slab[256:264] = full


def select_body(pos, table, x, lse, dest, ext, out, sem):
    lse_all = lse[...]
    for b in range(NB):
        norm = norm_rows(lse_all, b)
        if b < GLOB:
            norm = jnp.where(pos[0] == 0, OFF, norm)
        ext[b] = block_ext(x, b, norm)

    def step(i, carry):
        for c in range(4):
            t = i * 4 + c
            tile = jnp.zeros((8, HD), F32)
            for r in range(RAND):
                b = table[t, r]
                out[t, r * 64 : r * 64 + 64] = x[b, 0:64]
                out[t, 192 + r * 64 : 256 + r * 64] = x[b, 192:256]
                part = ext[b]
                if r:
                    part = pltpu.roll(part, 2 * r, 0)
                tile = tile + part
            out[t, 384:392] = tile.astype(BF16)
            pltpu.make_async_copy(out.at[t], dest.at[t], sem.at[t]).start()
        return carry

    lax.fori_loop(0, NB // 4, step, 0)

    def finish(t, carry):
        pltpu.make_async_copy(out.at[t], dest.at[t], sem.at[t]).wait()
        return carry

    lax.fori_loop(0, NB, finish, 0)


def grads(q, g, norm, delta, k, v, keep=None):
    st = nt(k, q) * FACTOR
    pt = jnp.exp(st - norm)
    if keep is not None:
        pt = jnp.where(keep, pt, 0.0)
    dst = (pt * (nt(v, g) - delta)).astype(BF16)
    return tn(dst, k), nn(dst, q), nn(pt.astype(BF16), g)


def staged(tiles, scores, probs, lows, want="qkv"):
    depth = 3
    held = {}
    for step in range(len(tiles) + 2):
        if step < len(tiles):
            tile = tiles[step]()
            held[step] = tile
            shape = (tile["k"].shape[0], tile["q"].shape[0])
            slot = step % depth
            view = (slot, slice(0, shape[0]), slice(0, shape[1]))
            scores[view] = nt(tile["k"], tile["q"])
            probs[view] = nt(tile["v"], tile["g"])
        n = step - 1
        if 0 <= n < len(tiles):
            tile = held[n]
            shape = (tile["k"].shape[0], tile["q"].shape[0])
            view = (n % depth, slice(0, shape[0]), slice(0, shape[1]))
            pt = jnp.exp(scores[view] * FACTOR - tile["norm"])
            if tile.get("keep") is not None:
                pt = jnp.where(tile["keep"], pt, 0.0)
            if "v" in want:
                low_view = (n % depth, 0) + view[1:]
                lows[low_view] = pt.astype(BF16)
            low_view = (n % depth, 1) + view[1:]
            lows[low_view] = (pt * (probs[view] - tile["delta"])).astype(BF16)
        n = step - 2
        if 0 <= n < len(tiles):
            tile = held.pop(n)
            shape = (tile["k"].shape[0], tile["q"].shape[0])
            cut = (slice(0, shape[0]), slice(0, shape[1]))
            dst = lows[(n % depth, 1) + cut]
            parts = []
            if "q" in want:
                parts.append(tn(dst, tile["k"]))
            if "k" in want:
                parts.append(nn(dst, tile["q"]))
            if "v" in want:
                parts.append(nn(lows[(n % depth, 0) + cut], tile["g"]))
            tile["use"](*parts)


def two(ext, a):
    return ext[a : a + 1].astype(F32) + ext[a + 1 : a + 2].astype(F32)


def joined(ref, a, first, last):
    return jnp.concatenate([ref[n, a * 64 : (a + 1) * 64] for n in range(first, last)], axis=0)


def pair_delta(x, b):
    e0 = x[b, 256:264].astype(F32)
    e1 = x[b + 1, 256:264].astype(F32)
    return low_pair(two(e0, 0), two(e1, 0))


def masked_norms(pos, lse):
    lse_all = lse[...]
    lanes = lax.broadcasted_iota(jnp.int32, lse_all.shape, 1)
    return jnp.where((pos[0] == 0) & (lanes < GLOB * BLK), OFF, lse_all)


def window_body(pos, x, lse, dq_out, dk_out, dv_out, dq, dk, dv, sem):
    lse_all = masked_norms(pos, lse)
    for i in range(NB // 2):
        b = 2 * i
        norm = lse_all[:, i * HD : (i + 1) * HD]
        low, high = max(b - 1, 0), min(b + 3, NB)
        shape = ((high - low) * BLK, HD)
        kb = (lax.broadcasted_iota(jnp.int32, shape, 0) >> 6) + low
        qb = (lax.broadcasted_iota(jnp.int32, shape, 1) >> 6) + b
        keep = jnp.abs(kb - qb) <= 1
        if low < GLOB:
            keep = keep & ((pos[0] > 0) | (kb >= GLOB))
        wq, wk, wv = grads(
            joined(x, 0, b, b + 2),
            joined(x, 3, b, b + 2),
            norm,
            pair_delta(x, b),
            joined(x, 1, low, high),
            joined(x, 2, low, high),
            keep,
        )
        dq[b * 64 : b * 64 + 128] = wq
        for acc, part in ((dk, wk), (dv, wv)):
            old = min(b + 1, NB) * 64 if b else 0
            seen = slice(low * 64, old)
            if b:
                acc[seen] = acc[seen] + part[0 : old - low * 64]
            acc[old : high * 64] = part[old - low * 64 :]
    pushes = [
        pltpu.make_async_copy(src, dst, sem.at[n])
        for n, (src, dst) in enumerate(((dq, dq_out), (dk, dk_out), (dv, dv_out)))
    ]
    for push in pushes:
        push.start()
    for push in pushes:
        push.wait()


def rand_tiles(table, x, y, use):
    sub = lax.broadcasted_iota(jnp.int32, (HD, HD), 0)
    lane = lax.broadcasted_iota(jnp.int32, (HD, HD), 1)
    keep = (sub >> 6) == (lane >> 6)
    entries = [(t, r) for t in range(NB) for r in range(RAND)]

    def tile_of(n):
        pair = entries[2 * n : 2 * n + 2]

        def make():
            def both(base):
                return jnp.concatenate(
                    [y[t, base + r * 64 : base + r * 64 + 64] for t, r in pair], axis=0
                )

            sides = [two(y[t, 384:392].astype(F32), 2 * r) for t, r in pair]
            js = [table[NB + t, r] for t, r in pair]
            return dict(
                q=both(0),
                g=both(192),
                k=jnp.concatenate([x[j, 64:128] for j in js], axis=0),
                v=jnp.concatenate([x[j, 128:192] for j in js], axis=0),
                norm=high_pair(*sides),
                delta=low_pair(*sides),
                keep=keep,
                use=lambda *parts: use(pair, js, *parts),
            )

        return make

    return [tile_of(n) for n in range(len(entries) // 2)]


def rand_query_body(table, x, y, z, y_out, buf, sem, y_sem, scores, probs, lows):
    saves = [
        pltpu.make_async_copy(y.at[pl.ds(2 * n, 2)], y_out.at[pl.ds(2 * n, 2)], y_sem.at[n])
        for n in range(NB // 2)
    ]
    for save in saves:
        save.start()

    def use(pair, js, pq):
        low = (pq * FACTOR).astype(BF16)
        for m, (t, r) in enumerate(pair):
            buf[t, r * 64 : r * 64 + 64] = low[m * 64 : m * 64 + 64]
            if r == RAND - 1:
                pltpu.make_async_copy(buf.at[t], z.at[t], sem.at[t]).start()

    staged(rand_tiles(table, x, y, use), scores, probs, lows, "q")
    for save in saves:
        save.wait()

    def finish(t, carry):
        pltpu.make_async_copy(buf.at[t], z.at[t], sem.at[t]).wait()
        return carry

    lax.fori_loop(0, NB, finish, 0)


def rand_key_body(table, x, y_far, dk_out, dv_out, y, dk, dv, y_sem, sem, scores, probs, lows):
    pulls = [
        pltpu.make_async_copy(y_far.at[pl.ds(2 * n, 2)], y.at[pl.ds(2 * n, 2)], y_sem.at[n])
        for n in range(NB // 2)
    ]
    for pull in pulls:
        pull.start()
    dk[...] = jnp.zeros_like(dk)
    dv[...] = jnp.zeros_like(dv)
    for pull in pulls:
        pull.wait()

    def use(pair, js, pk, pv):
        for m, j in enumerate(js):
            rows = slice(m * 64, m * 64 + 64)
            span = pl.ds(pl.multiple_of(j * 64, 64), 64)
            dk[span] = dk[span] + pk[rows]
            dv[span] = dv[span] + pv[rows]

    staged(rand_tiles(table, x, y, use), scores, probs, lows, "kv")
    pushes = [
        pltpu.make_async_copy(src, dst, sem.at[n])
        for n, (src, dst) in enumerate(((dk, dk_out), (dv, dv_out)))
    ]
    for push in pushes:
        push.start()
    for push in pushes:
        push.wait()


def global_body(
    pos, x, lse, glob, dq_out, dk_out, dv_out, gpart, glow,
    dq, dk, dv, sem, sums, scores, probs, lows,
):
    here = pos[0]
    lse_all = masked_norms(pos, lse)
    gq, gk, gv, gg = (joined(glob, a, 0, GLOB) for a in range(4))
    sides = [two(glob[n, 256:264].astype(F32), 0) for n in range(GLOB)]
    gdelta = low_pair(*sides)
    gnorm = high_pair(*sides)
    sums[...] = jnp.zeros_like(sums)
    tiles = []
    for i in range(4):
        b = 4 * i
        span = slice(b * 64, b * 64 + 256)

        def down(b=b, span=span):
            def use(fq, fk, fv):
                sums[0] = sums[0] + fq
                dk[span] = fk
                dv[span] = fv

            return dict(
                q=gq,
                g=gg,
                k=joined(x, 1, b, b + 4),
                v=joined(x, 2, b, b + 4),
                norm=gnorm,
                delta=gdelta,
                use=use,
            )

        def across(b=b, span=span):
            def use(wq, wk, wv):
                dq[span] = wq
                sums[1] = sums[1] + wk
                sums[2] = sums[2] + wv

            return dict(
                q=joined(x, 0, b, b + 4),
                g=joined(x, 3, b, b + 4),
                k=gk,
                v=gv,
                norm=lse_all[:, span],
                delta=jnp.concatenate([pair_delta(x, b), pair_delta(x, b + 2)], axis=1),
                use=use,
            )

        tiles += [down, across]
    staged(tiles, scores, probs, lows)
    gq_sum, gk_sum, gv_sum = sums[0], sums[1], sums[2]
    pushes = [
        pltpu.make_async_copy(src, dst, sem.at[n])
        for n, (src, dst) in enumerate(((dq, dq_out), (dk, dk_out), (dv, dv_out)))
    ]
    for push in pushes:
        push.start()
    for n, total in enumerate((gq_sum * FACTOR, gk_sum * FACTOR, gv_sum)):
        gpart[n] = total
        glow[n] = total.astype(BF16)
    for push in pushes:
        push.wait()


def gather_body(
    pos, x, lse, before, after, dq_w, dk_w, dv_w, dq_g, dk_g, dv_g, dk_r, dv_r, w, dq, edge,
    s0, s1, s2, dq_s, dk_s, dv_s, s3, s4, buf, in_sem, out_sem,
):
    here = pos[0]
    held = (s0, s1, s2, dq_s, dk_s, dv_s, s3, s4)
    sources = (dq_w, dk_w, dv_w, dq_g, dk_g, dv_g, dk_r, dv_r)
    pulls = [
        pltpu.make_async_copy(src, dst, in_sem.at[n])
        for n, (src, dst) in enumerate(zip(sources, held))
    ]
    for pull in pulls:
        pull.start()
    lse_all = masked_norms(pos, lse)
    extra = []
    for slab, b in ((before, 0), (after, NB - 1)):
        span = slice(b * 64, b * 64 + 64)
        far_ext = two(slab[256:264].astype(F32), 0)
        own_ext = two(x[b, 256:264].astype(F32), 0)
        far_norm = far_ext[:, 64:128]
        if b == 0:
            far_norm = jnp.where(here == 0, OFF, far_norm)
        own_q, _, _ = grads(
            x[b, 0:64],
            x[b, 192:256],
            lse_all[:, span],
            own_ext[:, 0:64],
            slab[64:128],
            slab[128:192],
        )
        _, own_k, own_v = grads(
            slab[0:64],
            slab[192:256],
            far_norm,
            far_ext[:, 0:64],
            x[b, 64:128],
            x[b, 128:192],
        )
        extra.append((span, own_q, own_k, own_v))
    for pull in pulls:
        pull.wait()
    for span, own_q, own_k, own_v in extra:
        dq_s[span] = dq_s[span] + own_q
        dk_s[span] = dk_s[span] + own_k
        dv_s[span] = dv_s[span] + own_v
    dq[...] = dq_s[...] + s0[...]
    pushes = []
    for b in range(NB):
        span = slice(b * 64, b * 64 + 64)
        rk = (dk_s[span] + s1[span] + s3[span]) * FACTOR
        rv = dv_s[span] + s2[span] + s4[span]
        if b in EDGES:
            at = EDGES.index(b) * 128
            edge[at : at + 64] = rk
            edge[at + 64 : at + 128] = rv
            continue
        buf[b, 0:64] = rk.astype(BF16)
        buf[b, 64:128] = rv.astype(BF16)
        push = pltpu.make_async_copy(buf.at[b], w.at[b, pl.ds(64, 128)], out_sem.at[b])
        push.start()
        pushes.append(push)
    for push in pushes:
        push.wait()


def merge_body(pos, table, dq, edge, z, gtot, w_in, w, acc, out, out_edge, sem):
    acc[...] = dq[...] * FACTOR
    for t in range(NB):
        for r in range(RAND):
            span = pl.ds(pl.multiple_of(table[t, r] * 64, 64), 64)
            acc[span] = acc[span] + z[t, r * 64 : r * 64 + 64].astype(F32)
    home = jnp.where(pos[0] == 0, 1.0, 0.0)
    pushes = []

    def send(src, dst, n):
        push = pltpu.make_async_copy(src, dst, sem.at[n])
        push.start()
        pushes.append(push)

    for n, b in enumerate(EDGES):
        rk, rv = edge[n * 128 : n * 128 + 64], edge[n * 128 + 64 : n * 128 + 128]
        rk = rk + home * gtot[1, b * 64 : b * 64 + 64]
        rv = rv + home * gtot[2, b * 64 : b * 64 + 64]
        out_edge[n, 0:64] = rk.astype(BF16)
        out_edge[n, 64:128] = rv.astype(BF16)
        send(out_edge.at[n], w.at[b, pl.ds(64, 128)], NB + n)
    for b in range(NB):
        span = slice(b * 64, b * 64 + 64)
        rq = acc[span]
        if b < GLOB:
            rq = rq + home * gtot[0, span]
        out[b] = rq.astype(BF16)
        send(out.at[b], w.at[b, pl.ds(0, 64)], b)
    for push in pushes:
        push.wait()


def unpack_body(w, q, k, v):
    for h in range(HEADS):
        cols = pl.ds(h * HD, HD)
        q[:, cols] = w[h, 0:64]
        k[:, cols] = w[h, 64:128]
        v[:, cols] = w[h, 128:192]


def struct(shape, dtype=BF16):
    return jax.ShapeDtypeStruct(shape, dtype)


def far(shape, dtype=BF16):
    return pltpu.HBM(shape, dtype)


def near(shape, dtype=BF16):
    return pltpu.VMEM(shape, dtype)


def hold(x):
    return pltpu.with_memory_space_constraint(x, pltpu.VMEM)


def keep_far(x):
    return pltpu.with_memory_space_constraint(x, pltpu.HBM)


def exchange(x, axis):
    return lax.all_to_all(x, axis, split_axis=0, concat_axis=0, tiled=True)


def per_device(query, key, value, output, grad_out, logsumexp, rand_blocks):
    position = lax.axis_index("seq")
    pos = position.astype(jnp.int32).reshape(1)
    rows = NB * BLK
    groups = NB
    dma = pltpu.SemaphoreType.DMA
    whole = pltpu.VMEM((BLK, HEADS * HD), BF16)
    packed = call(
        pack_body,
        far((HEADS, SLAB, HD)),
        [HB] * 5,
        HB,
        nbytes=5 << 18,
        scratch=[whole] * 5 + [pltpu.VMEM((HEADS, SLAB, HD), BF16), dma((5,)), dma((HEADS,))],
    )(*map(keep_far, (query, key, value, output, grad_out)))
    x = exchange(packed, "head")
    table = call(table_body, struct((2 * NB, HD), jnp.int32), [SM, VM], VM, nbytes=1 << 14)(
        pos, rand_blocks.reshape(NB, NB * RAND)
    )
    last, first, glob = call(
        slab_body,
        (struct((SLAB, HD)), struct((SLAB, HD)), struct((GLOB, SLAB, HD))),
        [SM, VM, VM],
        (VM,) * 3,
        nbytes=1 << 18,
    )(pos, x, logsumexp)
    y = call(
        select_body,
        far((NB, PAIR, HD)),
        [SM, SM, VM, VM],
        HB,
        nbytes=3 << 20,
        scratch=[
            pltpu.VMEM((NB, 8, HD), F32),
            pltpu.VMEM((NB, PAIR, HD), BF16),
            dma((NB,)),
        ],
    )(pos, table, x, logsumexp)

    def spread(glob, reach, starts):
        source = glob
        for n in (1, 2, 3):
            glob = glob + lax.ppermute(source, "seq", [(s, s + n * reach) for s in starts])
        return glob

    def collect(gpart, glow, reach, starts):
        for n in (1, 2, 3):
            moved = lax.ppermute(glow, "seq", [(s + n * reach, s) for s in starts])
            gpart = gpart + moved.astype(F32)
        return gpart

    corners = range(0, groups, 4)
    glob = spread(glob, 4, (0,))
    glob, y = lax.optimization_barrier((glob, y))
    y = exchange(y, "seq")
    glob = spread(glob, 1, corners)
    grid = pltpu.VMEM((rows, HD), F32)
    far_acc = far((rows, HD), F32)
    acc = near((rows, HD), F32)
    dq_w, dk_w, dv_w = call(
        window_body,
        (far_acc,) * 3,
        [SM, VM, VM],
        (HB,) * 3,
        flops=1 << 29,
        nbytes=2 << 20,
        scratch=[grid] * 3 + [dma((3,))],
    )(pos, x, logsumexp)
    glob, dq_w = lax.optimization_barrier((glob, dq_w))
    dq_g, dk_g, dv_g, gpart, glow = call(
        global_body,
        (far_acc,) * 3 + (struct((3, HD, HD), F32), struct((3, HD, HD))),
        [SM] + [VM] * 3,
        (HB,) * 3 + (VM,) * 2,
        flops=1 << 29,
        nbytes=4 << 20,
        scratch=[grid] * 3
        + [
            dma((3,)),
            pltpu.VMEM((3, HD, HD), F32),
            pltpu.VMEM((3, 256, 256), F32),
            pltpu.VMEM((3, 256, 256), F32),
            pltpu.VMEM((3, 2, 256, 256), BF16),
        ],
    )(pos, x, logsumexp, glob)
    glow, last, first = lax.optimization_barrier((glow, last, first))
    gpart = collect(gpart, glow, 1, corners)
    before = lax.ppermute(last, "seq", [(s, s + 1) for s in range(groups - 1)])
    after = lax.ppermute(first, "seq", [(s + 1, s) for s in range(groups - 1)])
    y, gpart = lax.optimization_barrier((y, gpart))
    stage_space = [
        pltpu.VMEM((3, HD, HD), F32),
        pltpu.VMEM((3, HD, HD), F32),
        pltpu.VMEM((3, 2, HD, HD), BF16),
    ]
    z, y = call(
        rand_query_body,
        (far((NB, RAND * BLK, HD)), far((NB, PAIR, HD))),
        [SM, VM, VM],
        (HB,) * 2,
        flops=1 << 29,
        nbytes=4 << 20,
        scratch=[pltpu.VMEM((NB, RAND * BLK, HD), BF16), dma((NB,)), dma((NB // 2,))]
        + stage_space,
    )(table, x, y)
    z, gpart, y, before, after = lax.optimization_barrier((z, gpart, y, before, after))
    z = exchange(z, "seq")
    moved = lax.ppermute(gpart.astype(BF16), "seq", [(4, 0), (12, 8)])
    gpart = gpart + moved.astype(F32)
    dk_r, dv_r = call(
        rand_key_body,
        (far_acc, far_acc),
        [SM, VM, HB],
        (HB,) * 2,
        flops=1 << 29,
        nbytes=4 << 20,
        scratch=[pltpu.VMEM((NB, PAIR, HD), BF16), grid, grid, dma((NB // 2,)), dma((2,))]
        + stage_space,
    )(table, x, keep_far(y))
    w, dq, edge = call(
        gather_body,
        (far((NB, 3 * BLK, HD)), acc, struct((len(EDGES) * 2 * BLK, HD), F32)),
        [SM] + [VM] * 4 + [HB] * 8,
        (HB, VM, VM),
        flops=1 << 24,
        nbytes=4 << 20,
        scratch=[grid] * 8 + [pltpu.VMEM((NB, 2 * BLK, HD), BF16), dma((8,)), dma((NB,))],
    )(
        pos,
        x,
        logsumexp,
        before,
        after,
        *map(keep_far, (dq_w, dk_w, dv_w, dq_g, dk_g, dv_g, dk_r, dv_r)),
    )
    gpart, w, dq, edge = lax.optimization_barrier((gpart, w, dq, edge))
    moved = lax.ppermute(gpart.astype(BF16), "seq", [(8, 0)])
    gpart = gpart + moved.astype(F32)
    w = call(
        merge_body,
        far((NB, 3 * BLK, HD)),
        [SM, SM] + [VM] * 4 + [HB],
        HB,
        nbytes=4 << 20,
        scratch=[
            grid,
            pltpu.VMEM((NB, BLK, HD), BF16),
            pltpu.VMEM((len(EDGES), 2 * BLK, HD), BF16),
            dma((NB + len(EDGES),)),
        ],
        aliases={6: 0},
    )(pos, table, hold(dq), edge, z, gpart, w)
    w = exchange(w, "head")
    shape = struct((BLK, HEADS * HD))
    return call(unpack_body, (shape, shape, shape), [VM], (VM,) * 3, nbytes=3 << 19)(w)


def solution(mesh):
    in_specs = (
        P(("seq", "head"), None),
        P(("seq", "head"), None),
        P(("seq", "head"), None),
        P(("seq", "head"), None),
        P(("seq", "head"), None),
        P("head", "seq"),
        P(),
    )
    out_specs = (P(("seq", "head"), None), P(("seq", "head"), None), P(("seq", "head"), None))
    return jax.shard_map(
        per_device, mesh=mesh, in_specs=in_specs, out_specs=out_specs, check_vma=False
    )
```

```python
import jax
import jax.numpy as jnp
from jax import lax
from jax.experimental import pallas as pl
from jax.experimental.pallas import tpu as pltpu
from jax.sharding import PartitionSpec as P

HEADS = 16
HD = 128
BLK = 64
GLOB = 2
RAND = 3
NB = 16
FACTOR = HD ** (-0.5)
OFF = 1e30
EDGES = (0, 1)
SLAB = 4 * BLK + 8
PAIR = RAND * 2 * BLK + 8
F32 = jnp.float32
BF16 = jnp.bfloat16

HB = pl.BlockSpec(memory_space=pltpu.HBM)
VM = pl.BlockSpec(memory_space=pltpu.VMEM)
SM = pl.BlockSpec(memory_space=pltpu.SMEM)


def call(body, outs, in_specs, out_specs, flops=0, nbytes=0, scratch=(), aliases={}, limit=8):
    return pl.pallas_call(
        body,
        out_shape=outs,
        in_specs=in_specs,
        out_specs=out_specs,
        scratch_shapes=list(scratch),
        input_output_aliases=aliases,
        compiler_params=pltpu.CompilerParams(vmem_limit_bytes=limit << 20),
        cost_estimate=pl.CostEstimate(flops=flops, bytes_accessed=nbytes, transcendentals=0),
    )


def nt(a, b):
    return lax.dot_general(a, b, (((1,), (1,)), ((), ())), preferred_element_type=F32)


def nn(a, b):
    return lax.dot_general(a, b, (((1,), (0,)), ((), ())), preferred_element_type=F32)


def tn(a, b):
    return lax.dot_general(a, b, (((0,), (0,)), ((), ())), preferred_element_type=F32)


def pieces(x):
    high = x.astype(BF16).astype(F32)
    return high, (x - high).astype(BF16).astype(F32)


def pack_body(q, k, v, o, g, out, qs, ks, vs, os, gs, ps, in_sem, out_sem):
    pulls = [
        pltpu.make_async_copy(src, dst, in_sem.at[i])
        for i, (src, dst) in enumerate(zip((o, g, q, k, v), (os, gs, qs, ks, vs)))
    ]
    for pull in pulls:
        pull.start()
    lane = lax.broadcasted_iota(jnp.int32, (BLK, HD), 1)
    row = lax.broadcasted_iota(jnp.int32, (8, HD), 0)
    deltas = jnp.zeros((BLK, HD), F32)
    pulls[0].wait()
    pulls[1].wait()
    for h in range(HEADS):
        cols = pl.ds(h * HD, HD)
        gh = gs[:, cols]
        ps[h, 192:256] = gh
        part = jnp.sum(gh.astype(F32) * os[:, cols].astype(F32), axis=1, keepdims=True)
        deltas = jnp.where(lane == h, part, deltas)
    turned = jnp.transpose(jnp.concatenate([deltas, jnp.zeros((BLK, HD), F32)], axis=0))
    high, low = pieces(turned)
    for pull in pulls[2:]:
        pull.wait()
    pushes = []
    for h in range(HEADS):
        cols = pl.ds(h * HD, HD)
        ps[h, 0:64] = qs[:, cols]
        ps[h, 64:128] = ks[:, cols]
        ps[h, 128:192] = vs[:, cols]
        tile = jnp.where(row == 0, high[h : h + 1], jnp.where(row == 1, low[h : h + 1], 0.0))
        ps[h, 256:264] = tile.astype(BF16)
        push = pltpu.make_async_copy(ps.at[h], out.at[h], out_sem.at[h])
        push.start()
        pushes.append(push)
    for push in pushes:
        push.wait()


def table_body(pos, entries, out):
    here = pos[0]
    e = entries[...]
    width = e.shape[1]
    lane = lax.broadcasted_iota(jnp.int32, (NB, width), 1)
    row = lax.broadcasted_iota(jnp.int32, (NB, width), 0)
    mine = jnp.sum(jnp.where(row == here, e, 0), axis=0, keepdims=True)
    to_group = jnp.broadcast_to(mine, (NB, width)) >> 4
    hit = jnp.concatenate(
        [jnp.where(to_group == row, 1.0, 0.0), jnp.where((e >> 4) == here, 1.0, 0.0)], axis=0
    )
    value = jnp.concatenate([(lane * 171) >> 9, e & 15], axis=0)
    ii = lax.broadcasted_iota(jnp.int32, (width, width), 0)
    jj = lax.broadcasted_iota(jnp.int32, (width, width), 1)
    before = jnp.where(ii < jj, 1.0, 0.0).astype(BF16)
    rank = nn(hit.astype(BF16), before)
    out_lane = lax.broadcasted_iota(jnp.int32, (2 * NB, HD), 1)
    result = jnp.zeros((2 * NB, HD), jnp.int32)
    for r in range(RAND):
        chosen = jnp.where((hit > 0.5) & (jnp.abs(rank - r) < 0.5), value, 0)
        total = jnp.sum(chosen, axis=1, keepdims=True)
        result = jnp.where(out_lane == r, total, result)
    out[...] = result


def left_half():
    return lax.broadcasted_iota(jnp.int32, (1, HD), 1) < BLK


def low_pair(one, other):
    return jnp.where(left_half(), one, pltpu.roll(other, BLK, 1))


def high_pair(one, other):
    return jnp.where(left_half(), pltpu.roll(one, BLK, 1), other)


def norm_rows(lse, b):
    pair = lse[:, (b // 2) * HD : (b // 2 + 1) * HD]
    return pair if b % 2 else pltpu.roll(pair, BLK, 1)


def block_ext(x, b, norm):
    row = lax.broadcasted_iota(jnp.int32, (8, HD), 0)
    high, low = pieces(norm)
    tile = jnp.where(row == 0, high, jnp.where(row == 1, low, 0.0))
    return jnp.where(left_half(), x[b, 256:264].astype(F32), tile)


def slab_body(pos, x, lse, last, first, glob):
    lse_all = lse[...]
    keep = pos[0] == 0
    for b in (0, 1, NB - 1):
        full = block_ext(x, b, norm_rows(lse_all, b)).astype(BF16)
        if b < GLOB:
            glob[b, 0:256] = jnp.where(keep, x[b, 0:256], jnp.zeros((256, HD), BF16))
            glob[b, 256:264] = jnp.where(keep, full, jnp.zeros((8, HD), BF16))
        for slab, owner in ((first, 0), (last, NB - 1)):
            if b == owner:
                slab[0:256] = x[b, 0:256]
                slab[256:264] = full


def select_body(pos, table, x, lse, dest, ext, out, sem):
    lse_all = lse[...]
    for b in range(NB):
        norm = norm_rows(lse_all, b)
        if b < GLOB:
            norm = jnp.where(pos[0] == 0, OFF, norm)
        ext[b] = block_ext(x, b, norm)

    def step(i, carry):
        for c in range(4):
            t = i * 4 + c
            tile = jnp.zeros((8, HD), F32)
            for r in range(RAND):
                b = table[t, r]
                out[t, r * 64 : r * 64 + 64] = x[b, 0:64]
                out[t, 192 + r * 64 : 256 + r * 64] = x[b, 192:256]
                part = ext[b]
                if r:
                    part = pltpu.roll(part, 2 * r, 0)
                tile = tile + part
            out[t, 384:392] = tile.astype(BF16)
            pltpu.make_async_copy(out.at[t], dest.at[t], sem.at[t]).start()
        return carry

    lax.fori_loop(0, NB // 4, step, 0)

    def finish(t, carry):
        pltpu.make_async_copy(out.at[t], dest.at[t], sem.at[t]).wait()
        return carry

    lax.fori_loop(0, NB, finish, 0)


def grads(q, g, norm, delta, k, v, keep=None):
    st = nt(k, q) * FACTOR
    pt = jnp.exp(st - norm)
    if keep is not None:
        pt = jnp.where(keep, pt, 0.0)
    dst = (pt * (nt(v, g) - delta)).astype(BF16)
    return tn(dst, k), nn(dst, q), nn(pt.astype(BF16), g)


def staged(tiles, scores, probs, lows, want="qkv"):
    depth = 4
    held = {}
    for step in range(len(tiles) + 3):
        if step < len(tiles):
            tile = tiles[step]()
            held[step] = tile
            shape = (tile["k"].shape[0], tile["q"].shape[0])
            slot = step % depth
            view = (slot, slice(0, shape[0]), slice(0, shape[1]))
            scores[view] = nt(tile["k"], tile["q"])
            probs[view] = nt(tile["v"], tile["g"])
        n = step - 1
        if 0 <= n < len(tiles):
            tile = held[n]
            shape = (tile["k"].shape[0], tile["q"].shape[0])
            view = (n % depth, slice(0, shape[0]), slice(0, shape[1]))
            pt = jnp.exp(scores[view] * FACTOR - tile["norm"])
            if tile.get("keep") is not None:
                pt = jnp.where(tile["keep"], pt, 0.0)
            if "v" in want:
                low_view = (n % depth, 0) + view[1:]
                lows[low_view] = pt.astype(BF16)
            low_view = (n % depth, 1) + view[1:]
            lows[low_view] = (pt * (probs[view] - tile["delta"])).astype(BF16)
        n = step - 3
        if 0 <= n < len(tiles):
            tile = held.pop(n)
            shape = (tile["k"].shape[0], tile["q"].shape[0])
            cut = (slice(0, shape[0]), slice(0, shape[1]))
            dst = lows[(n % depth, 1) + cut]
            parts = []
            if "q" in want:
                parts.append(tn(dst, tile["k"]))
            if "k" in want:
                parts.append(nn(dst, tile["q"]))
            if "v" in want:
                parts.append(nn(lows[(n % depth, 0) + cut], tile["g"]))
            tile["use"](*parts)


def two(ext, a):
    return ext[a : a + 1].astype(F32) + ext[a + 1 : a + 2].astype(F32)


def joined(ref, a, first, last):
    return jnp.concatenate([ref[n, a * 64 : (a + 1) * 64] for n in range(first, last)], axis=0)


def pair_delta(x, b):
    e0 = x[b, 256:264].astype(F32)
    e1 = x[b + 1, 256:264].astype(F32)
    return low_pair(two(e0, 0), two(e1, 0))


def masked_norms(pos, lse):
    lse_all = lse[...]
    lanes = lax.broadcasted_iota(jnp.int32, lse_all.shape, 1)
    return jnp.where((pos[0] == 0) & (lanes < GLOB * BLK), OFF, lse_all)


def window_body(pos, x, lse, dq_out, dk_out, dv_out, dq, dk, dv, sem):
    lse_all = masked_norms(pos, lse)
    for i in range(NB // 2):
        b = 2 * i
        norm = lse_all[:, i * HD : (i + 1) * HD]
        low, high = max(b - 1, 0), min(b + 3, NB)
        shape = ((high - low) * BLK, HD)
        kb = (lax.broadcasted_iota(jnp.int32, shape, 0) >> 6) + low
        qb = (lax.broadcasted_iota(jnp.int32, shape, 1) >> 6) + b
        keep = jnp.abs(kb - qb) <= 1
        if low < GLOB:
            keep = keep & ((pos[0] > 0) | (kb >= GLOB))
        wq, wk, wv = grads(
            joined(x, 0, b, b + 2),
            joined(x, 3, b, b + 2),
            norm,
            pair_delta(x, b),
            joined(x, 1, low, high),
            joined(x, 2, low, high),
            keep,
        )
        dq[b * 64 : b * 64 + 128] = wq
        for acc, part in ((dk, wk), (dv, wv)):
            old = min(b + 1, NB) * 64 if b else 0
            seen = slice(low * 64, old)
            if b:
                acc[seen] = acc[seen] + part[0 : old - low * 64]
            acc[old : high * 64] = part[old - low * 64 :]
    pushes = [
        pltpu.make_async_copy(src, dst, sem.at[n])
        for n, (src, dst) in enumerate(((dq, dq_out), (dk, dk_out), (dv, dv_out)))
    ]
    for push in pushes:
        push.start()
    for push in pushes:
        push.wait()


def rand_tiles(table, x, y, use):
    sub = lax.broadcasted_iota(jnp.int32, (HD, HD), 0)
    lane = lax.broadcasted_iota(jnp.int32, (HD, HD), 1)
    keep = (sub >> 6) == (lane >> 6)
    entries = [(t, r) for t in range(NB) for r in range(RAND)]

    def tile_of(n):
        pair = entries[2 * n : 2 * n + 2]

        def make():
            def both(base):
                return jnp.concatenate(
                    [y[t, base + r * 64 : base + r * 64 + 64] for t, r in pair], axis=0
                )

            sides = [two(y[t, 384:392].astype(F32), 2 * r) for t, r in pair]
            js = [table[NB + t, r] for t, r in pair]
            return dict(
                q=both(0),
                g=both(192),
                k=jnp.concatenate([x[j, 64:128] for j in js], axis=0),
                v=jnp.concatenate([x[j, 128:192] for j in js], axis=0),
                norm=high_pair(*sides),
                delta=low_pair(*sides),
                keep=keep,
                use=lambda *parts: use(pair, js, *parts),
            )

        return make

    return [tile_of(n) for n in range(len(entries) // 2)]


def rand_query_body(table, x, y, z, y_out, buf, sem, y_sem, scores, probs, lows):
    saves = [
        pltpu.make_async_copy(y.at[pl.ds(2 * n, 2)], y_out.at[pl.ds(2 * n, 2)], y_sem.at[n])
        for n in range(NB // 2)
    ]
    for save in saves:
        save.start()

    def use(pair, js, pq):
        low = (pq * FACTOR).astype(BF16)
        for m, (t, r) in enumerate(pair):
            buf[t, r * 64 : r * 64 + 64] = low[m * 64 : m * 64 + 64]
            if r == RAND - 1:
                pltpu.make_async_copy(buf.at[t], z.at[t], sem.at[t]).start()

    staged(rand_tiles(table, x, y, use), scores, probs, lows, "q")
    for save in saves:
        save.wait()

    def finish(t, carry):
        pltpu.make_async_copy(buf.at[t], z.at[t], sem.at[t]).wait()
        return carry

    lax.fori_loop(0, NB, finish, 0)


def rand_key_body(table, x, y_far, dk_out, dv_out, y, dk, dv, y_sem, sem, scores, probs, lows):
    pulls = [
        pltpu.make_async_copy(y_far.at[pl.ds(2 * n, 2)], y.at[pl.ds(2 * n, 2)], y_sem.at[n])
        for n in range(NB // 2)
    ]
    for pull in pulls:
        pull.start()
    dk[...] = jnp.zeros_like(dk)
    dv[...] = jnp.zeros_like(dv)
    for pull in pulls:
        pull.wait()

    def use(pair, js, pk, pv):
        for m, j in enumerate(js):
            rows = slice(m * 64, m * 64 + 64)
            span = pl.ds(pl.multiple_of(j * 64, 64), 64)
            dk[span] = dk[span] + pk[rows]
            dv[span] = dv[span] + pv[rows]

    staged(rand_tiles(table, x, y, use), scores, probs, lows, "kv")
    pushes = [
        pltpu.make_async_copy(src, dst, sem.at[n])
        for n, (src, dst) in enumerate(((dk, dk_out), (dv, dv_out)))
    ]
    for push in pushes:
        push.start()
    for push in pushes:
        push.wait()


def global_body(
    pos, x, lse, glob, dq_out, dk_out, dv_out, gpart, glow,
    dq, dk, dv, sem, sums, scores, probs, lows,
):
    here = pos[0]
    lse_all = masked_norms(pos, lse)
    gq, gk, gv, gg = (joined(glob, a, 0, GLOB) for a in range(4))
    sides = [two(glob[n, 256:264].astype(F32), 0) for n in range(GLOB)]
    gdelta = low_pair(*sides)
    gnorm = high_pair(*sides)
    sums[...] = jnp.zeros_like(sums)
    tiles = []
    for i in range(4):
        b = 4 * i
        span = slice(b * 64, b * 64 + 256)

        def down(b=b, span=span):
            def use(fq, fk, fv):
                sums[0] = sums[0] + fq
                dk[span] = fk
                dv[span] = fv

            return dict(
                q=gq,
                g=gg,
                k=joined(x, 1, b, b + 4),
                v=joined(x, 2, b, b + 4),
                norm=gnorm,
                delta=gdelta,
                use=use,
            )

        def across(b=b, span=span):
            def use(wq, wk, wv):
                dq[span] = wq
                sums[1] = sums[1] + wk
                sums[2] = sums[2] + wv

            return dict(
                q=joined(x, 0, b, b + 4),
                g=joined(x, 3, b, b + 4),
                k=gk,
                v=gv,
                norm=lse_all[:, span],
                delta=jnp.concatenate([pair_delta(x, b), pair_delta(x, b + 2)], axis=1),
                use=use,
            )

        tiles += [down, across]
    staged(tiles, scores, probs, lows)
    gq_sum, gk_sum, gv_sum = sums[0], sums[1], sums[2]
    pushes = [
        pltpu.make_async_copy(src, dst, sem.at[n])
        for n, (src, dst) in enumerate(((dq, dq_out), (dk, dk_out), (dv, dv_out)))
    ]
    for push in pushes:
        push.start()
    for n, total in enumerate((gq_sum * FACTOR, gk_sum * FACTOR, gv_sum)):
        gpart[n] = total
        glow[n] = total.astype(BF16)
    for push in pushes:
        push.wait()


def gather_body(
    pos, x, lse, before, after, dq_w, dk_w, dv_w, dq_g, dk_g, dv_g, dk_r, dv_r, w, dq, edge,
    s0, s1, s2, dq_s, dk_s, dv_s, s3, s4, buf, in_sem, out_sem,
):
    here = pos[0]
    held = (s0, s1, s2, dq_s, dk_s, dv_s, s3, s4)
    sources = (dq_w, dk_w, dv_w, dq_g, dk_g, dv_g, dk_r, dv_r)
    pulls = [
        pltpu.make_async_copy(src, dst, in_sem.at[n])
        for n, (src, dst) in enumerate(zip(sources, held))
    ]
    for pull in pulls:
        pull.start()
    lse_all = masked_norms(pos, lse)
    extra = []
    for slab, b in ((before, 0), (after, NB - 1)):
        span = slice(b * 64, b * 64 + 64)
        far_ext = two(slab[256:264].astype(F32), 0)
        own_ext = two(x[b, 256:264].astype(F32), 0)
        far_norm = far_ext[:, 64:128]
        if b == 0:
            far_norm = jnp.where(here == 0, OFF, far_norm)
        own_q, _, _ = grads(
            x[b, 0:64],
            x[b, 192:256],
            lse_all[:, span],
            own_ext[:, 0:64],
            slab[64:128],
            slab[128:192],
        )
        _, own_k, own_v = grads(
            slab[0:64],
            slab[192:256],
            far_norm,
            far_ext[:, 0:64],
            x[b, 64:128],
            x[b, 128:192],
        )
        extra.append((span, own_q, own_k, own_v))
    for pull in pulls:
        pull.wait()
    for span, own_q, own_k, own_v in extra:
        dq_s[span] = dq_s[span] + own_q
        dk_s[span] = dk_s[span] + own_k
        dv_s[span] = dv_s[span] + own_v
    dq[...] = dq_s[...] + s0[...]
    pushes = []
    for b in range(NB):
        span = slice(b * 64, b * 64 + 64)
        rk = (dk_s[span] + s1[span] + s3[span]) * FACTOR
        rv = dv_s[span] + s2[span] + s4[span]
        if b in EDGES:
            at = EDGES.index(b) * 128
            edge[at : at + 64] = rk
            edge[at + 64 : at + 128] = rv
            continue
        buf[b, 0:64] = rk.astype(BF16)
        buf[b, 64:128] = rv.astype(BF16)
        push = pltpu.make_async_copy(buf.at[b], w.at[b, pl.ds(64, 128)], out_sem.at[b])
        push.start()
        pushes.append(push)
    for push in pushes:
        push.wait()


def merge_body(pos, table, dq, edge, z, gtot, w_in, w, acc, out, out_edge, sem):
    acc[...] = dq[...] * FACTOR
    for t in range(NB):
        for r in range(RAND):
            span = pl.ds(pl.multiple_of(table[t, r] * 64, 64), 64)
            acc[span] = acc[span] + z[t, r * 64 : r * 64 + 64].astype(F32)
    home = jnp.where(pos[0] == 0, 1.0, 0.0)
    pushes = []

    def send(src, dst, n):
        push = pltpu.make_async_copy(src, dst, sem.at[n])
        push.start()
        pushes.append(push)

    for n, b in enumerate(EDGES):
        rk, rv = edge[n * 128 : n * 128 + 64], edge[n * 128 + 64 : n * 128 + 128]
        rk = rk + home * gtot[1, b * 64 : b * 64 + 64]
        rv = rv + home * gtot[2, b * 64 : b * 64 + 64]
        out_edge[n, 0:64] = rk.astype(BF16)
        out_edge[n, 64:128] = rv.astype(BF16)
        send(out_edge.at[n], w.at[b, pl.ds(64, 128)], NB + n)
    for b in range(NB):
        span = slice(b * 64, b * 64 + 64)
        rq = acc[span]
        if b < GLOB:
            rq = rq + home * gtot[0, span]
        out[b] = rq.astype(BF16)
        send(out.at[b], w.at[b, pl.ds(0, 64)], b)
    for push in pushes:
        push.wait()


def unpack_body(w, q, k, v):
    for h in range(HEADS):
        cols = pl.ds(h * HD, HD)
        q[:, cols] = w[h, 0:64]
        k[:, cols] = w[h, 64:128]
        v[:, cols] = w[h, 128:192]


def struct(shape, dtype=BF16):
    return jax.ShapeDtypeStruct(shape, dtype)


def far(shape, dtype=BF16):
    return pltpu.HBM(shape, dtype)


def near(shape, dtype=BF16):
    return pltpu.VMEM(shape, dtype)


def hold(x):
    return pltpu.with_memory_space_constraint(x, pltpu.VMEM)


def keep_far(x):
    return pltpu.with_memory_space_constraint(x, pltpu.HBM)


def exchange(x, axis):
    return lax.all_to_all(x, axis, split_axis=0, concat_axis=0, tiled=True)


def per_device(query, key, value, output, grad_out, logsumexp, rand_blocks):
    position = lax.axis_index("seq")
    pos = position.astype(jnp.int32).reshape(1)
    rows = NB * BLK
    groups = NB
    dma = pltpu.SemaphoreType.DMA
    whole = pltpu.VMEM((BLK, HEADS * HD), BF16)
    packed = call(
        pack_body,
        far((HEADS, SLAB, HD)),
        [HB] * 5,
        HB,
        nbytes=5 << 18,
        scratch=[whole] * 5 + [pltpu.VMEM((HEADS, SLAB, HD), BF16), dma((5,)), dma((HEADS,))],
    )(*map(keep_far, (query, key, value, output, grad_out)))
    x = exchange(packed, "head")
    table = call(table_body, struct((2 * NB, HD), jnp.int32), [SM, VM], VM, nbytes=1 << 14)(
        pos, rand_blocks.reshape(NB, NB * RAND)
    )
    last, first, glob = call(
        slab_body,
        (struct((SLAB, HD)), struct((SLAB, HD)), struct((GLOB, SLAB, HD))),
        [SM, VM, VM],
        (VM,) * 3,
        nbytes=1 << 18,
    )(pos, x, logsumexp)
    y = call(
        select_body,
        far((NB, PAIR, HD)),
        [SM, SM, VM, VM],
        HB,
        nbytes=3 << 20,
        scratch=[
            pltpu.VMEM((NB, 8, HD), F32),
            pltpu.VMEM((NB, PAIR, HD), BF16),
            dma((NB,)),
        ],
    )(pos, table, x, logsumexp)

    def spread(glob, reach, starts):
        source = glob
        for n in (1, 2, 3):
            glob = glob + lax.ppermute(source, "seq", [(s, s + n * reach) for s in starts])
        return glob

    def collect(gpart, glow, reach, starts):
        for n in (1, 2, 3):
            moved = lax.ppermute(glow, "seq", [(s + n * reach, s) for s in starts])
            gpart = gpart + moved.astype(F32)
        return gpart

    corners = range(0, groups, 4)
    glob = spread(glob, 4, (0,))
    glob, y = lax.optimization_barrier((glob, y))
    y = exchange(y, "seq")
    glob = spread(glob, 1, corners)
    grid = pltpu.VMEM((rows, HD), F32)
    far_acc = far((rows, HD), F32)
    acc = near((rows, HD), F32)
    dq_w, dk_w, dv_w = call(
        window_body,
        (far_acc,) * 3,
        [SM, VM, VM],
        (HB,) * 3,
        flops=1 << 29,
        nbytes=2 << 20,
        scratch=[grid] * 3 + [dma((3,))],
    )(pos, x, logsumexp)
    glob, dq_w = lax.optimization_barrier((glob, dq_w))
    dq_g, dk_g, dv_g, gpart, glow = call(
        global_body,
        (far_acc,) * 3 + (struct((3, HD, HD), F32), struct((3, HD, HD))),
        [SM] + [VM] * 3,
        (HB,) * 3 + (VM,) * 2,
        flops=1 << 29,
        nbytes=4 << 20,
        scratch=[grid] * 3
        + [
            dma((3,)),
            pltpu.VMEM((3, HD, HD), F32),
            pltpu.VMEM((4, 256, 256), F32),
            pltpu.VMEM((4, 256, 256), F32),
            pltpu.VMEM((4, 2, 256, 256), BF16),
        ],
    )(pos, x, logsumexp, glob)
    glow, last, first = lax.optimization_barrier((glow, last, first))
    gpart = collect(gpart, glow, 1, corners)
    before = lax.ppermute(last, "seq", [(s, s + 1) for s in range(groups - 1)])
    after = lax.ppermute(first, "seq", [(s + 1, s) for s in range(groups - 1)])
    y, gpart = lax.optimization_barrier((y, gpart))
    stage_space = [
        pltpu.VMEM((4, HD, HD), F32),
        pltpu.VMEM((4, HD, HD), F32),
        pltpu.VMEM((4, 2, HD, HD), BF16),
    ]
    z, y = call(
        rand_query_body,
        (far((NB, RAND * BLK, HD)), far((NB, PAIR, HD))),
        [SM, VM, VM],
        (HB,) * 2,
        flops=1 << 29,
        nbytes=4 << 20,
        scratch=[pltpu.VMEM((NB, RAND * BLK, HD), BF16), dma((NB,)), dma((NB // 2,))]
        + stage_space,
    )(table, x, y)
    z, gpart, y, before, after = lax.optimization_barrier((z, gpart, y, before, after))
    z = exchange(z, "seq")
    moved = lax.ppermute(gpart.astype(BF16), "seq", [(4, 0), (12, 8)])
    gpart = gpart + moved.astype(F32)
    dk_r, dv_r = call(
        rand_key_body,
        (far_acc, far_acc),
        [SM, VM, HB],
        (HB,) * 2,
        flops=1 << 29,
        nbytes=4 << 20,
        scratch=[pltpu.VMEM((NB, PAIR, HD), BF16), grid, grid, dma((NB // 2,)), dma((2,))]
        + stage_space,
    )(table, x, keep_far(y))
    w, dq, edge = call(
        gather_body,
        (far((NB, 3 * BLK, HD)), acc, struct((len(EDGES) * 2 * BLK, HD), F32)),
        [SM] + [VM] * 4 + [HB] * 8,
        (HB, VM, VM),
        flops=1 << 24,
        nbytes=4 << 20,
        scratch=[grid] * 8 + [pltpu.VMEM((NB, 2 * BLK, HD), BF16), dma((8,)), dma((NB,))],
    )(
        pos,
        x,
        logsumexp,
        before,
        after,
        *map(keep_far, (dq_w, dk_w, dv_w, dq_g, dk_g, dv_g, dk_r, dv_r)),
    )
    gpart, w, dq, edge = lax.optimization_barrier((gpart, w, dq, edge))
    moved = lax.ppermute(gpart.astype(BF16), "seq", [(8, 0)])
    gpart = gpart + moved.astype(F32)
    w = call(
        merge_body,
        far((NB, 3 * BLK, HD)),
        [SM, SM] + [VM] * 4 + [HB],
        HB,
        nbytes=4 << 20,
        scratch=[
            grid,
            pltpu.VMEM((NB, BLK, HD), BF16),
            pltpu.VMEM((len(EDGES), 2 * BLK, HD), BF16),
            dma((NB + len(EDGES),)),
        ],
        aliases={6: 0},
    )(pos, table, hold(dq), edge, z, gpart, w)
    w = exchange(w, "head")
    shape = struct((BLK, HEADS * HD))
    return call(unpack_body, (shape, shape, shape), [VM], (VM,) * 3, nbytes=3 << 19)(w)


def solution(mesh):
    in_specs = (
        P(("seq", "head"), None),
        P(("seq", "head"), None),
        P(("seq", "head"), None),
        P(("seq", "head"), None),
        P(("seq", "head"), None),
        P("head", "seq"),
        P(),
    )
    out_specs = (P(("seq", "head"), None), P(("seq", "head"), None), P(("seq", "head"), None))
    return jax.shard_map(
        per_device, mesh=mesh, in_specs=in_specs, out_specs=out_specs, check_vma=False
    )
```
